128 devices in a mesh: wide: 32 (over x, z_hi, y), narrow: 4 (over z_lo, core).
Axes of the slice: x: 4, y: 4, z: 4 (z_hi: 2, z_lo: 2; z = z_hi * 2 + z_lo), core: 2. Of those that a mesh axis runs over, the one named last changes fastest.
Arguments:
- tokens: bfloat16 [49152, 512], P(('wide', 'narrow')), may hold values from -6 to 6
- cotangent: bfloat16 [49152, 512], P(('wide', 'narrow')), may hold values from -6 to 6
- lengths: int32 [32, 3], P('wide'), may hold values from 1 to 768, 1536 in all within a row
- master: float32 [3277824], P('narrow'), may hold values from -2 to 2
- first_moment: float32 [3277824], P('narrow'), may hold values from -0.6 to 0.6
- second_moment: float32 [3277824], P('narrow'), may hold values from 0.001 to 0.03
Outputs:
- output: bfloat16 [49152, 512], P(('wide', 'narrow'))
- d_tokens: bfloat16 [49152, 512], P(('wide', 'narrow'))
- gradient: float32 [3277824], P('narrow')
- new_master: float32 [3277824], P('narrow')
- new_first: float32 [3277824], P('narrow')
- new_second: float32 [3277824], P('narrow')
The draws below stay inside these ranges and needn't reach their ends.
Inputs may be any that keep to these rules, and one draw needn't show every extreme that they name: Row g holds in order the lengths of the 3 sequences that fill group g's 1536 tokens.
All inputs are finite; a program needn't handle non-finite values.
Results may differ from the reference program's by a relative error of at most 0.015.
The reference program's roundings to bfloat16 on the way count: a program that leaves them out, or rounds other values in their place, can miss the bound.
Values may be sent and summed in bfloat16 or wider, within the bound.
A program may use at most 192 MiB of HBM per device.

```python
import math
import jax
import jax.numpy as jnp
import numpy as np
from jax import lax

MODEL_WIDTH = 512
QUERY_HEADS = 15
KEYVAL_HEADS = 5
HEAD_SIZE = 64
FEEDFWD_UNITS = 1280
NSEQ = 3
STEP = 4
GROUP_TOKENS = 1536
GROUPS = 32
TOKENS = 49152
SEQ_MOST = 768
NPARAM = 3277824
N_WIDE = 32


def draw_master(key, part):
    count_entries = [MODEL_WIDTH * QUERY_HEADS * HEAD_SIZE, MODEL_WIDTH * KEYVAL_HEADS * HEAD_SIZE, MODEL_WIDTH * KEYVAL_HEADS * HEAD_SIZE, QUERY_HEADS * HEAD_SIZE * MODEL_WIDTH, MODEL_WIDTH * FEEDFWD_UNITS, MODEL_WIDTH * FEEDFWD_UNITS, FEEDFWD_UNITS * MODEL_WIDTH]
    scales = [MODEL_WIDTH ** (-0.5), MODEL_WIDTH ** (-0.5), MODEL_WIDTH ** (-0.5), 0.25, MODEL_WIDTH ** (-0.5), MODEL_WIDTH ** (-0.5), FEEDFWD_UNITS ** (-0.5)]
    streams = jax.random.split(key, 8)
    pieces = []
    for number in range(7):
        sample = jax.random.truncated_normal(streams[number], -4.0, 4.0, (count_entries[number],), jnp.float32)
        pieces.append(sample * scales[number])
    gain_values = 1.0 + 0.15 * jax.random.uniform(streams[7], (2 * MODEL_WIDTH,), jnp.float32, -1.0, 1.0)
    pieces.append(gain_values)
    return jnp.concatenate(pieces)


def level_of(own_key, extent, shards, smallest, high):
    def one(axis_at, parts):
        steps = jax.random.uniform(jax.random.fold_in(jax.random.fold_in(own_key, 6), axis_at), (parts,), jnp.float32, smallest / len(shards), high / len(shards))
        return jnp.repeat(jnp.exp(steps), extent[axis_at] // parts).reshape((-1,) + (1,) * (len(extent) - axis_at - 1))

    level = one(*shards[0])
    for cut in shards[1:]:
        level = level * one(*cut)
    return level


def split_up(count, total, most, skew):
    portions = [(1 << 20) // math.isqrt(rank ** skew) + 1 for rank in range(2, count + 1)]
    surplus, counts = total - most - (count - 1), [1] * (count - 1)
    while surplus > 0:
        candidates = [i for i in range(count - 1) if counts[i] < most]
        mass, left = sum([portions[i] for i in candidates]), surplus
        for i in candidates:
            addition = min(most - counts[i], max(1, left * portions[i] // mass), surplus)
            counts[i] = counts[i] + addition
            surplus = surplus - addition
    return np.array([most] + counts)


def uneven(rng, count, total, limit, skew):
    if count == 2:
        one = jax.random.randint(rng, (), max(1, total - limit), min(limit, total - 1) + 1)
        return jnp.stack([one, total - one])
    sizes = jnp.asarray(split_up(count, total, limit, skew), jnp.int32)
    pairs = (count - 1) // 2
    giver, taker = sizes[1:1 + 2 * pairs:2], sizes[2:2 + 2 * pairs:2]
    margin = jnp.minimum(giver - 1, limit - taker)
    passed = jax.random.randint(jax.random.fold_in(rng, 1), (pairs,), 0, 1 << 20) % (margin + 1)
    sizes = sizes.at[1:1 + 2 * pairs:2].set(giver - passed).at[2:2 + 2 * pairs:2].set(taker + passed)
    return sizes[jax.random.permutation(jax.random.fold_in(rng, 2), count)]


def scatter_about(key, extent, deviation, limit, cuts=(), kind=jnp.bfloat16):
    result = jax.random.normal(key, extent, jnp.float32) * deviation
    if len(cuts) > 0:
        result = level_of(key, extent, cuts, -0.22, 0.18) * result
    return jnp.clip(result, min=-limit, max=limit).astype(kind)


def setup_inputs(seed: int = 0) -> dict:
    streams_of = jax.random.split(jax.random.key(seed), 7)
    return {
        "tokens": scatter_about(streams_of[0], (TOKENS, MODEL_WIDTH), 1.0, 6.0, ((0, 128),)),
        "cotangent": scatter_about(streams_of[1], (TOKENS, MODEL_WIDTH), 1.0, 6.0, ((0, 128),)),
        "lengths": jax.vmap(lambda own: uneven(own, NSEQ, GROUP_TOKENS, SEQ_MOST, 2))(jax.random.split(streams_of[2], GROUPS)).reshape((GROUPS, NSEQ)).astype(jnp.int32),
        "master": draw_master(jax.random.fold_in(streams_of[6], 71), 0),
        "first_moment": scatter_about(streams_of[4], (NPARAM,), 0.1, 0.6, ((0, 4),), jnp.float32),
        "second_moment": jnp.clip(jnp.exp(math.log(0.03) - 3.4011973 * jax.random.uniform(streams_of[5], (NPARAM,), jnp.float32) ** level_of(streams_of[5], (NPARAM,), ((0, 4),), -0.2, 0.2)), 0.001, 0.03),
    }


eps_norm = 1e-05
rope_base = 100000.0
beta_one = 0.9
beta_two = 0.95
learn_rate = 0.03
decay_rate = 0.1
adam_eps = 1e-08
masked_logits = -1e+30

def unpack(flat):
    arrangement_list = [(MODEL_WIDTH, QUERY_HEADS * HEAD_SIZE), (MODEL_WIDTH, KEYVAL_HEADS * HEAD_SIZE), (MODEL_WIDTH, KEYVAL_HEADS * HEAD_SIZE), (QUERY_HEADS * HEAD_SIZE, MODEL_WIDTH), (MODEL_WIDTH, FEEDFWD_UNITS), (MODEL_WIDTH, FEEDFWD_UNITS), (FEEDFWD_UNITS, MODEL_WIDTH), (MODEL_WIDTH,), (MODEL_WIDTH,)]
    pieces = []
    offset = 0
    for layout in arrangement_list:
        length = math.prod(layout)
        pieces.append(flat[offset:offset + length].reshape(layout))
        offset = offset + length
    return pieces

def place_tokens(indices, lengths_row):
    seq_ends = jnp.cumsum(lengths_row).astype(jnp.int32)
    seq_starts = (seq_ends - lengths_row).astype(jnp.int32)
    member = (indices[:, None] >= seq_starts[None, :]) & (indices[:, None] < seq_ends[None, :])
    numbers = jnp.arange(lengths_row.shape[0], dtype=jnp.int32)
    segment = lax.optimization_barrier(jnp.sum(jnp.where(member, numbers[None, :], 0), axis=1)).astype(jnp.int32)
    token_position = (indices - lax.optimization_barrier(jnp.sum(jnp.where(member, seq_starts[None, :], 0), axis=1))).astype(jnp.int32)
    return (segment, token_position)

def normalize(values):
    inverse_rms = lax.rsqrt(lax.optimization_barrier(jnp.mean(values * values, axis=-1, keepdims=True)) + eps_norm)
    return (values * inverse_rms, inverse_rms)

def apply_rotary(values, token_position, head_count, turn_sign):
    half_dim = HEAD_SIZE // 2
    inverse = rope_base ** (-2.0 * jnp.arange(half_dim, dtype=jnp.float32) / HEAD_SIZE)
    angles = token_position.astype(jnp.float32)[:, None] * inverse[None, :]
    cosine = jnp.cos(angles)[:, None, :]
    sine = turn_sign * jnp.sin(angles)[:, None, :]
    shaped = values.reshape(values.shape[0], head_count, HEAD_SIZE)
    first_half = shaped[:, :, :half_dim]
    second_half = shaped[:, :, half_dim:]
    turned = jnp.concatenate([first_half * cosine - second_half * sine, second_half * cosine + first_half * sine], axis=-1)
    return turned.reshape(values.shape)

def layer_group(tok_group, cot_group, lengths_row, weights):
    w_query, w_key, w_value, w_out, w_gate, w_up, w_down, gain_one, gain_two = weights
    group_width = QUERY_HEADS // KEYVAL_HEADS
    score_scale = HEAD_SIZE ** (-0.5)
    indices = jnp.arange(GROUP_TOKENS, dtype=jnp.int32)
    segment, token_position = place_tokens(indices, lengths_row)
    allowed = (segment[:, None] == segment[None, :]) & (indices[None, :] <= indices[:, None])
    allowed = allowed[None, None]
    resid = tok_group.astype(jnp.float32)
    normed_one, inverse_one = normalize(resid)
    hidden_one = (normed_one * gain_one.astype(jnp.float32)).astype(jnp.bfloat16)
    query = jnp.dot(hidden_one, w_query, preferred_element_type=jnp.float32)
    key_projection = jnp.dot(hidden_one, w_key, preferred_element_type=jnp.float32)
    value_proj = jnp.dot(hidden_one, w_value, preferred_element_type=jnp.float32)
    query_batch = apply_rotary(query, token_position, QUERY_HEADS, 1.0).astype(jnp.bfloat16)
    key_batch = apply_rotary(key_projection, token_position, KEYVAL_HEADS, 1.0).astype(jnp.bfloat16)
    value_batch = value_proj.astype(jnp.bfloat16)
    query_tensor_split = query_batch.astype(jnp.float32).reshape(GROUP_TOKENS, KEYVAL_HEADS, group_width, HEAD_SIZE)
    key_tensor_split = key_batch.astype(jnp.float32).reshape(GROUP_TOKENS, KEYVAL_HEADS, HEAD_SIZE)
    value_tensor_split = value_batch.astype(jnp.float32).reshape(GROUP_TOKENS, KEYVAL_HEADS, HEAD_SIZE)
    scores = jnp.einsum('qgrd,kgd->grqk', query_tensor_split, key_tensor_split) * score_scale
    row_top = lax.optimization_barrier(jnp.max(jnp.where(allowed, scores, masked_logits), axis=-1, keepdims=True))
    row_total = lax.optimization_barrier(jnp.sum(jnp.where(allowed, jnp.exp(scores - row_top), 0.0), axis=-1, keepdims=True))
    lse = row_top + jnp.log(row_total)
    probs = jnp.where(allowed, jnp.exp(scores - lse), 0.0)
    probs_b = probs.astype(jnp.bfloat16).astype(jnp.float32)
    attention_output_split = jnp.einsum('grqk,kgd->qgrd', probs_b, value_tensor_split)
    attention_output = attention_output_split.reshape(GROUP_TOKENS, QUERY_HEADS * HEAD_SIZE).astype(jnp.bfloat16)
    mixed = resid + jnp.dot(attention_output, w_out, preferred_element_type=jnp.float32)
    normed_two, inverse_two = normalize(mixed)
    hidden_two = (normed_two * gain_two.astype(jnp.float32)).astype(jnp.bfloat16)
    gate = jnp.dot(hidden_two, w_gate, preferred_element_type=jnp.float32)
    upward = jnp.dot(hidden_two, w_up, preferred_element_type=jnp.float32)
    sigma = jax.nn.sigmoid(gate)
    activated = (gate * sigma * upward).astype(jnp.bfloat16)
    output = (mixed + jnp.dot(activated, w_down, preferred_element_type=jnp.float32)).astype(jnp.bfloat16)
    d_act = jnp.dot(cot_group, w_down.T, preferred_element_type=jnp.float32)
    g_down = jnp.dot(activated.T, cot_group, preferred_element_type=jnp.float32)
    d_gate = (d_act * upward * sigma * (1.0 + gate * (1.0 - sigma))).astype(jnp.bfloat16)
    d_up = (d_act * gate * sigma).astype(jnp.bfloat16)
    g_gate = jnp.dot(hidden_two.T, d_gate, preferred_element_type=jnp.float32)
    g_up = jnp.dot(hidden_two.T, d_up, preferred_element_type=jnp.float32)
    d_hidden_two = jnp.dot(d_gate, w_gate.T, preferred_element_type=jnp.float32) + jnp.dot(d_up, w_up.T, preferred_element_type=jnp.float32)
    g_gain_two = lax.optimization_barrier(jnp.sum(d_hidden_two * normed_two, axis=0))
    dn_two = d_hidden_two * gain_two.astype(jnp.float32)
    d_mixed = cot_group.astype(jnp.float32) + inverse_two * (dn_two - normed_two * lax.optimization_barrier(jnp.mean(dn_two * normed_two, axis=-1, keepdims=True)))
    d_mixed_b = d_mixed.astype(jnp.bfloat16)
    g_out = jnp.dot(attention_output.T, d_mixed_b, preferred_element_type=jnp.float32)
    attention_output_gradient = jnp.dot(d_mixed_b, w_out.T, preferred_element_type=jnp.float32).astype(jnp.bfloat16)
    split_gradient = attention_output_gradient.astype(jnp.float32).reshape(GROUP_TOKENS, KEYVAL_HEADS, group_width, HEAD_SIZE)
    softmax_correction = lax.optimization_barrier(jnp.sum(split_gradient * attention_output.astype(jnp.float32).reshape(GROUP_TOKENS, KEYVAL_HEADS, group_width, HEAD_SIZE), axis=-1)).transpose(1, 2, 0)
    value_gradient = jnp.einsum('pozf,zpom->fpm', probs_b, split_gradient)
    d_probs = jnp.einsum('qgrd,kgd->grqk', split_gradient, value_tensor_split)
    score_gradient = (probs * (d_probs - softmax_correction[..., None]) * score_scale).astype(jnp.bfloat16).astype(jnp.float32)
    d_query = jnp.einsum('grqk,kgd->qgrd', score_gradient, key_tensor_split).reshape(GROUP_TOKENS, QUERY_HEADS * HEAD_SIZE)
    key_gradient = jnp.einsum('pozf,zpom->fpm', score_gradient, query_tensor_split).reshape(GROUP_TOKENS, KEYVAL_HEADS * HEAD_SIZE)
    d_query_b = apply_rotary(d_query, token_position, QUERY_HEADS, -1.0).astype(jnp.bfloat16)
    key_gradient_batch = apply_rotary(key_gradient, token_position, KEYVAL_HEADS, -1.0).astype(jnp.bfloat16)
    value_gradient_batch = value_gradient.reshape(GROUP_TOKENS, KEYVAL_HEADS * HEAD_SIZE).astype(jnp.bfloat16)
    g_query = jnp.dot(hidden_one.T, d_query_b, preferred_element_type=jnp.float32)
    g_key = jnp.dot(hidden_one.T, key_gradient_batch, preferred_element_type=jnp.float32)
    g_value = jnp.dot(hidden_one.T, value_gradient_batch, preferred_element_type=jnp.float32)
    d_hidden_one = jnp.dot(d_query_b, w_query.T, preferred_element_type=jnp.float32) + jnp.dot(key_gradient_batch, w_key.T, preferred_element_type=jnp.float32) + jnp.dot(value_gradient_batch, w_value.T, preferred_element_type=jnp.float32)
    g_gain_one = lax.optimization_barrier(jnp.sum(d_hidden_one * normed_one, axis=0))
    dn_one = d_hidden_one * gain_one.astype(jnp.float32)
    d_tokens = (d_mixed + inverse_one * (dn_one - normed_one * lax.optimization_barrier(jnp.mean(dn_one * normed_one, axis=-1, keepdims=True)))).astype(jnp.bfloat16)
    grads = jnp.concatenate([g_query.reshape(-1), g_key.reshape(-1), g_value.reshape(-1), g_out.reshape(-1), g_gate.reshape(-1), g_up.reshape(-1), g_down.reshape(-1), g_gain_one, g_gain_two])
    return (output, d_tokens, grads)

def reference(tokens, cotangent, lengths, master, first_moment, second_moment):
    weights = unpack(master.astype(jnp.bfloat16))
    tok_groups = tokens.reshape(N_WIDE, GROUP_TOKENS, MODEL_WIDTH)
    cot_groups = cotangent.reshape(N_WIDE, GROUP_TOKENS, MODEL_WIDTH)

    def visit_group(running_denominator, inputs):
        tok_group, cot_group, lengths_row = inputs
        output, d_tokens, grads = layer_group(tok_group, cot_group, lengths_row, weights)
        return (running_denominator + grads, (output, d_tokens))
    start_total = jnp.zeros((NPARAM,), jnp.float32)
    running_denominator, (outputs, d_all) = lax.scan(visit_group, start_total, (tok_groups, cot_groups, lengths))
    gradient = running_denominator * (1.0 / math.sqrt(TOKENS))
    new_first = beta_one * first_moment + (1.0 - beta_one) * gradient
    new_second = beta_two * second_moment + (1.0 - beta_two) * gradient * gradient
    first_hat = new_first / (1.0 - beta_one ** STEP)
    second_hat = new_second / (1.0 - beta_two ** STEP)
    indices = jnp.arange(NPARAM, dtype=jnp.int32)
    decay = jnp.where(indices < NPARAM - 2 * MODEL_WIDTH, decay_rate, 0.0)
    new_master = master - learn_rate * (first_hat / (jnp.sqrt(second_hat) + adam_eps) + decay * master)
    return (outputs.reshape(TOKENS, MODEL_WIDTH), d_all.reshape(TOKENS, MODEL_WIDTH), gradient, new_master, new_first, new_second)
```

```python
import math

import jax
import jax.numpy as jnp
from jax import lax
from jax.sharding import PartitionSpec as P

MODEL_WIDTH = 512
QUERY_HEADS = 15
KEYVAL_HEADS = 5
HEAD_SIZE = 64
FEEDFWD_UNITS = 1280
STEP = 4
NPARAM = 3277824


eps_norm = 1e-05
rope_base = 100000.0
beta_one = 0.9
beta_two = 0.95
learn_rate = 0.03
decay_rate = 0.1
adam_eps = 1e-08
masked_logits = -1e30


def unpack(flat):
    arrangement_list = [
        (MODEL_WIDTH, QUERY_HEADS * HEAD_SIZE),
        (MODEL_WIDTH, KEYVAL_HEADS * HEAD_SIZE),
        (MODEL_WIDTH, KEYVAL_HEADS * HEAD_SIZE),
        (QUERY_HEADS * HEAD_SIZE, MODEL_WIDTH),
        (MODEL_WIDTH, FEEDFWD_UNITS),
        (MODEL_WIDTH, FEEDFWD_UNITS),
        (FEEDFWD_UNITS, MODEL_WIDTH),
        (MODEL_WIDTH,),
        (MODEL_WIDTH,),
    ]
    pieces = []
    offset = 0
    for layout in arrangement_list:
        length = math.prod(layout)
        pieces.append(flat[offset : offset + length].reshape(layout))
        offset = offset + length
    return pieces


def place_tokens(indices, lengths_row):
    seq_ends = jnp.cumsum(lengths_row)
    seq_starts = seq_ends - lengths_row
    member = (indices[:, None] >= seq_starts[None, :]) & (indices[:, None] < seq_ends[None, :])
    numbers = jnp.arange(lengths_row.shape[0], dtype=jnp.int32)
    segment = jnp.sum(jnp.where(member, numbers[None, :], 0), axis=1)
    token_position = indices - jnp.sum(jnp.where(member, seq_starts[None, :], 0), axis=1)
    return (segment, token_position)


def normalize(values):
    inverse_rms = lax.rsqrt(jnp.mean(values * values, axis=-1, keepdims=True) + eps_norm)
    return (values * inverse_rms, inverse_rms)


def apply_rotary(values, token_position, head_count, turn_sign):
    half_dim = HEAD_SIZE // 2
    inverse = rope_base ** (-2.0 * jnp.arange(half_dim, dtype=jnp.float32) / HEAD_SIZE)
    angles = token_position.astype(jnp.float32)[:, None] * inverse[None, :]
    cosine = jnp.cos(angles)[:, None, :]
    sine = turn_sign * jnp.sin(angles)[:, None, :]
    shaped = values.reshape(values.shape[0], head_count, HEAD_SIZE)
    first_half = shaped[:, :, :half_dim]
    second_half = shaped[:, :, half_dim:]
    turned = jnp.concatenate(
        [first_half * cosine - second_half * sine, second_half * cosine + first_half * sine],
        axis=-1,
    )
    return turned.reshape(values.shape)


def keep_carry(carry):
    return carry


def body(tokens, cotangent, lengths, master, first_moment, second_moment):
    token_rows = tokens.shape[0]
    narrow_size = lax.axis_size("narrow")
    group_rows = token_rows * narrow_size
    narrow_rank = lax.axis_index("narrow")
    group_width = QUERY_HEADS // KEYVAL_HEADS
    score_scale = HEAD_SIZE ** (-0.5)
    shard_len = master.shape[0]
    replica = lax.all_gather(
        master.astype(jnp.bfloat16).reshape(shard_len // 128, 128), "narrow", axis=0, tiled=False
    ).reshape(-1)
    w_query, w_key, w_value, w_out, w_gate, w_up, w_down, gain_one, gain_two = unpack(replica)
    lengths_row = lengths[0]
    local_index = narrow_rank * token_rows + jnp.arange(token_rows, dtype=jnp.int32)
    segment, token_position = place_tokens(local_index, lengths_row)
    group_index = jnp.arange(group_rows, dtype=jnp.int32)
    key_segment = place_tokens(group_index, lengths_row)[0]
    first_start = local_index[0] - token_position[0]
    last_index = local_index[token_rows - 1]
    range_rows = min(512, group_rows)
    span_starts = list(range(0, group_rows, range_rows))
    resid = tokens.astype(jnp.float32)
    normed_one, inverse_one = normalize(resid)
    hidden_one = (normed_one * gain_one.astype(jnp.float32)).astype(jnp.bfloat16)
    query = jnp.dot(hidden_one, w_query, preferred_element_type=jnp.float32)
    key_projection = jnp.dot(hidden_one, w_key, preferred_element_type=jnp.float32)
    value_proj = jnp.dot(hidden_one, w_value, preferred_element_type=jnp.float32)
    query_batch = apply_rotary(query, token_position, QUERY_HEADS, 1.0).astype(jnp.bfloat16)
    key_batch = apply_rotary(key_projection, token_position, KEYVAL_HEADS, 1.0).astype(jnp.bfloat16)
    value_batch = value_proj.astype(jnp.bfloat16)
    kv_width = KEYVAL_HEADS * HEAD_SIZE
    kv_all = lax.all_gather(
        jnp.concatenate([key_batch, value_batch], axis=1), "narrow", axis=0, tiled=True
    )
    key_all, value_all = kv_all[:, :kv_width], kv_all[:, kv_width:]
    query_tensor_split = query_batch.reshape(token_rows, KEYVAL_HEADS, group_width, HEAD_SIZE)

    def span_setup(span_start, key_source, value_source):
        key_tensor_split = lax.slice_in_dim(
            key_source, span_start, span_start + range_rows
        ).reshape(range_rows, KEYVAL_HEADS, HEAD_SIZE)
        value_tensor_split = lax.slice_in_dim(
            value_source, span_start, span_start + range_rows
        ).reshape(range_rows, KEYVAL_HEADS, HEAD_SIZE)
        span_segment = lax.slice_in_dim(key_segment, span_start, span_start + range_rows)
        span_index = lax.slice_in_dim(group_index, span_start, span_start + range_rows)
        allowed = (segment[:, None] == span_segment[None, :]) & (
            span_index[None, :] <= local_index[:, None]
        )
        needed = (span_start <= last_index) & (span_start + range_rows - 1 >= first_start)
        return (key_tensor_split, value_tensor_split, allowed[None, None], needed)

    running_maximum = jnp.full((KEYVAL_HEADS, group_width, token_rows), masked_logits, jnp.float32)
    running_denominator = jnp.zeros((KEYVAL_HEADS, group_width, token_rows), jnp.float32)
    for span_start in span_starts:
        key_tensor_split, value_tensor_split, allowed, needed = span_setup(
            span_start, key_all, value_all
        )

        def extend(carry):
            old_top, old_total = carry
            scores = (
                jnp.einsum(
                    "qgrd,kgd->grqk",
                    query_tensor_split,
                    key_tensor_split,
                    preferred_element_type=jnp.float32,
                )
                * score_scale
            )
            new_top = jnp.maximum(
                old_top, jnp.max(jnp.where(allowed, scores, masked_logits), axis=-1)
            )
            span_sum = jnp.sum(
                jnp.where(allowed, jnp.exp(scores - new_top[..., None]), 0.0), axis=-1
            )
            return (new_top, old_total * jnp.exp(old_top - new_top) + span_sum)

        running_maximum, running_denominator = lax.cond(
            needed, extend, keep_carry, (running_maximum, running_denominator)
        )
    lse = running_maximum + jnp.log(running_denominator)
    running_total = jnp.zeros((token_rows, KEYVAL_HEADS, group_width, HEAD_SIZE), jnp.float32)
    for span_start in span_starts:
        key_tensor_split, value_tensor_split, allowed, needed = span_setup(
            span_start, key_all, value_all
        )

        def weigh_values(carry):
            scores = (
                jnp.einsum(
                    "qgrd,kgd->grqk",
                    query_tensor_split,
                    key_tensor_split,
                    preferred_element_type=jnp.float32,
                )
                * score_scale
            )
            probs_b = jnp.where(allowed, jnp.exp(scores - lse[..., None]), 0.0).astype(jnp.bfloat16)
            return carry + jnp.einsum(
                "grqk,kgd->qgrd", probs_b, value_tensor_split, preferred_element_type=jnp.float32
            )

        running_total = lax.cond(needed, weigh_values, keep_carry, running_total)
    attention_output = running_total.reshape(token_rows, QUERY_HEADS * HEAD_SIZE).astype(
        jnp.bfloat16
    )
    mixed = resid + jnp.dot(attention_output, w_out, preferred_element_type=jnp.float32)
    normed_two, inverse_two = normalize(mixed)
    hidden_two = (normed_two * gain_two.astype(jnp.float32)).astype(jnp.bfloat16)
    gate = jnp.dot(hidden_two, w_gate, preferred_element_type=jnp.float32)
    upward = jnp.dot(hidden_two, w_up, preferred_element_type=jnp.float32)
    sigma = jax.nn.sigmoid(gate)
    activated = (gate * sigma * upward).astype(jnp.bfloat16)
    output = (mixed + jnp.dot(activated, w_down, preferred_element_type=jnp.float32)).astype(
        jnp.bfloat16
    )
    d_act = jnp.dot(cotangent, w_down.T, preferred_element_type=jnp.float32)
    g_down = jnp.dot(activated.T, cotangent, preferred_element_type=jnp.float32)
    d_gate = (d_act * upward * sigma * (1.0 + gate * (1.0 - sigma))).astype(jnp.bfloat16)
    d_up = (d_act * gate * sigma).astype(jnp.bfloat16)
    g_gate = jnp.dot(hidden_two.T, d_gate, preferred_element_type=jnp.float32)
    g_up = jnp.dot(hidden_two.T, d_up, preferred_element_type=jnp.float32)
    d_hidden_two = jnp.dot(d_gate, w_gate.T, preferred_element_type=jnp.float32) + jnp.dot(
        d_up, w_up.T, preferred_element_type=jnp.float32
    )
    g_gain_two = jnp.sum(d_hidden_two * normed_two, axis=0)
    dn_two = d_hidden_two * gain_two.astype(jnp.float32)
    d_mixed = cotangent.astype(jnp.float32) + inverse_two * (
        dn_two - normed_two * jnp.mean(dn_two * normed_two, axis=-1, keepdims=True)
    )
    d_mixed_b = d_mixed.astype(jnp.bfloat16)
    g_out = jnp.dot(attention_output.T, d_mixed_b, preferred_element_type=jnp.float32)
    attention_output_gradient = jnp.dot(
        d_mixed_b, w_out.T, preferred_element_type=jnp.float32
    ).astype(jnp.bfloat16)
    split_gradient = attention_output_gradient.reshape(
        token_rows, KEYVAL_HEADS, group_width, HEAD_SIZE
    )
    attention_output_split = attention_output.reshape(
        token_rows, KEYVAL_HEADS, group_width, HEAD_SIZE
    )
    softmax_correction = jnp.sum(
        split_gradient.astype(jnp.float32) * attention_output_split.astype(jnp.float32), axis=-1
    ).transpose(1, 2, 0)
    key_back, value_back = (key_all, value_all)
    query_gradient_running = jnp.zeros(
        (token_rows, KEYVAL_HEADS, group_width, HEAD_SIZE), jnp.float32
    )
    key_contributions = []
    value_contributions = []
    for span_start in span_starts:
        key_tensor_split, value_tensor_split, allowed, needed = span_setup(
            span_start, key_back, value_back
        )

        def back_span(carry):
            scores = (
                jnp.einsum(
                    "qgrd,kgd->grqk",
                    query_tensor_split,
                    key_tensor_split,
                    preferred_element_type=jnp.float32,
                )
                * score_scale
            )
            probs = jnp.where(allowed, jnp.exp(scores - lse[..., None]), 0.0)
            probs_b = probs.astype(jnp.bfloat16)
            value_gradient_range = jnp.einsum(
                "pozf,zpom->fpm", probs_b, split_gradient, preferred_element_type=jnp.float32
            )
            d_probs = jnp.einsum(
                "qgrd,kgd->grqk",
                split_gradient,
                value_tensor_split,
                preferred_element_type=jnp.float32,
            )
            score_gradient = (
                probs * (d_probs - softmax_correction[..., None]) * score_scale
            ).astype(jnp.bfloat16)
            new_acc = carry + jnp.einsum(
                "grqk,kgd->qgrd",
                score_gradient,
                key_tensor_split,
                preferred_element_type=jnp.float32,
            )
            key_gradient_range = jnp.einsum(
                "pozf,zpom->fpm",
                score_gradient,
                query_tensor_split,
                preferred_element_type=jnp.float32,
            )
            return (new_acc, key_gradient_range, value_gradient_range)

        def skip_span(carry):
            blank_range = jnp.zeros((range_rows, KEYVAL_HEADS, HEAD_SIZE), jnp.float32)
            return (carry, blank_range, blank_range)

        query_gradient_running, key_gradient_range, value_gradient_range = lax.cond(
            needed, back_span, skip_span, query_gradient_running
        )
        key_contributions.append(key_gradient_range.reshape(range_rows, KEYVAL_HEADS * HEAD_SIZE))
        value_contributions.append(
            value_gradient_range.reshape(range_rows, KEYVAL_HEADS * HEAD_SIZE)
        )
    key_sum_in = jnp.concatenate(key_contributions, axis=0)
    value_sum_in = jnp.concatenate(value_contributions, axis=0)
    kv_grad = lax.psum_scatter(
        jnp.concatenate([key_sum_in, value_sum_in], axis=1), "narrow", scatter_dimension=0, tiled=True
    )
    key_gradient, value_gradient = kv_grad[:, :kv_width], kv_grad[:, kv_width:]
    d_query = query_gradient_running.reshape(token_rows, QUERY_HEADS * HEAD_SIZE)
    d_query_b = apply_rotary(d_query, token_position, QUERY_HEADS, -1.0).astype(jnp.bfloat16)
    key_gradient_batch = apply_rotary(key_gradient, token_position, KEYVAL_HEADS, -1.0).astype(
        jnp.bfloat16
    )
    value_gradient_batch = value_gradient.astype(jnp.bfloat16)
    g_query = jnp.dot(hidden_one.T, d_query_b, preferred_element_type=jnp.float32)
    g_key = jnp.dot(hidden_one.T, key_gradient_batch, preferred_element_type=jnp.float32)
    g_value = jnp.dot(hidden_one.T, value_gradient_batch, preferred_element_type=jnp.float32)
    d_hidden_one = (
        jnp.dot(d_query_b, w_query.T, preferred_element_type=jnp.float32)
        + jnp.dot(key_gradient_batch, w_key.T, preferred_element_type=jnp.float32)
        + jnp.dot(value_gradient_batch, w_value.T, preferred_element_type=jnp.float32)
    )
    g_gain_one = jnp.sum(d_hidden_one * normed_one, axis=0)
    dn_one = d_hidden_one * gain_one.astype(jnp.float32)
    d_tokens = (
        d_mixed
        + inverse_one
        * (dn_one - normed_one * jnp.mean(dn_one * normed_one, axis=-1, keepdims=True))
    ).astype(jnp.bfloat16)
    local_grads = jnp.concatenate(
        [
            g_query.reshape(-1),
            g_key.reshape(-1),
            g_value.reshape(-1),
            g_out.reshape(-1),
            g_gate.reshape(-1),
            g_up.reshape(-1),
            g_down.reshape(-1),
            g_gain_one,
            g_gain_two,
        ]
    )
    narrow_sum = lax.psum_scatter(
        local_grads.reshape(narrow_size, -1, 128), "narrow", scatter_dimension=0, tiled=True
    )
    summed = lax.psum(narrow_sum, "wide").reshape(-1)
    token_total = token_rows * narrow_size * lax.axis_size("wide")
    gradient = summed * (1.0 / math.sqrt(token_total))
    new_first = beta_one * first_moment + (1.0 - beta_one) * gradient
    new_second = beta_two * second_moment + (1.0 - beta_two) * gradient * gradient
    first_hat = new_first / (1.0 - beta_one**STEP)
    second_hat = new_second / (1.0 - beta_two**STEP)
    entry_index = narrow_rank * shard_len + jnp.arange(shard_len, dtype=jnp.int32)
    decay = jnp.where(entry_index < NPARAM - 2 * MODEL_WIDTH, decay_rate, 0.0)
    new_master = master - learn_rate * (
        first_hat / (jnp.sqrt(second_hat) + adam_eps) + decay * master
    )
    return (output, d_tokens, gradient, new_master, new_first, new_second)


def solution(mesh):
    in_specs = (
        P(("wide", "narrow"), None),
        P(("wide", "narrow"), None),
        P("wide", None),
        P("narrow"),
        P("narrow"),
        P("narrow"),
    )
    out_specs = (
        P(("wide", "narrow"), None),
        P(("wide", "narrow"), None),
        P("narrow"),
        P("narrow"),
        P("narrow"),
        P("narrow"),
    )
    return jax.shard_map(body, mesh=mesh, in_specs=in_specs, out_specs=out_specs, check_vma=False)
```

```python
import math

import jax
import jax.numpy as jnp
from jax import lax
from jax.sharding import PartitionSpec as P

MODEL_WIDTH = 512
QUERY_HEADS = 15
KEYVAL_HEADS = 5
HEAD_SIZE = 64
FEEDFWD_UNITS = 1280
STEP = 4
NPARAM = 3277824


eps_norm = 1e-05
rope_base = 100000.0
beta_one = 0.9
beta_two = 0.95
learn_rate = 0.03
decay_rate = 0.1
adam_eps = 1e-08
masked_logits = -1e30


def unpack(flat):
    arrangement_list = [
        (MODEL_WIDTH, QUERY_HEADS * HEAD_SIZE),
        (MODEL_WIDTH, KEYVAL_HEADS * HEAD_SIZE),
        (MODEL_WIDTH, KEYVAL_HEADS * HEAD_SIZE),
        (QUERY_HEADS * HEAD_SIZE, MODEL_WIDTH),
        (MODEL_WIDTH, FEEDFWD_UNITS),
        (MODEL_WIDTH, FEEDFWD_UNITS),
        (FEEDFWD_UNITS, MODEL_WIDTH),
        (MODEL_WIDTH,),
        (MODEL_WIDTH,),
    ]
    pieces = []
    offset = 0
    for layout in arrangement_list:
        length = math.prod(layout)
        pieces.append(flat[offset : offset + length].reshape(layout))
        offset = offset + length
    return pieces


def place_tokens(indices, lengths_row):
    seq_ends = jnp.cumsum(lengths_row)
    seq_starts = seq_ends - lengths_row
    member = (indices[:, None] >= seq_starts[None, :]) & (indices[:, None] < seq_ends[None, :])
    numbers = jnp.arange(lengths_row.shape[0], dtype=jnp.int32)
    segment = jnp.sum(jnp.where(member, numbers[None, :], 0), axis=1)
    token_position = indices - jnp.sum(jnp.where(member, seq_starts[None, :], 0), axis=1)
    return (segment, token_position)


def normalize(values):
    inverse_rms = lax.rsqrt(jnp.mean(values * values, axis=-1, keepdims=True) + eps_norm)
    return (values * inverse_rms, inverse_rms)


def apply_rotary(values, token_position, head_count, turn_sign):
    half_dim = HEAD_SIZE // 2
    inverse = rope_base ** (-2.0 * jnp.arange(half_dim, dtype=jnp.float32) / HEAD_SIZE)
    angles = token_position.astype(jnp.float32)[:, None] * inverse[None, :]
    cosine = jnp.cos(angles)[:, None, :]
    sine = turn_sign * jnp.sin(angles)[:, None, :]
    shaped = values.reshape(values.shape[0], head_count, HEAD_SIZE)
    first_half = shaped[:, :, :half_dim]
    second_half = shaped[:, :, half_dim:]
    turned = jnp.concatenate(
        [first_half * cosine - second_half * sine, second_half * cosine + first_half * sine],
        axis=-1,
    )
    return turned.reshape(values.shape)


def keep_carry(carry):
    return carry


def body(tokens, cotangent, lengths, master, first_moment, second_moment):
    token_rows = tokens.shape[0]
    narrow_size = lax.axis_size("narrow")
    group_rows = token_rows * narrow_size
    narrow_rank = lax.axis_index("narrow")
    group_width = QUERY_HEADS // KEYVAL_HEADS
    score_scale = HEAD_SIZE ** (-0.5)
    shard_len = master.shape[0]
    replica = lax.all_gather(
        master.astype(jnp.bfloat16).reshape(shard_len // 128, 128), "narrow", axis=0, tiled=False
    ).reshape(-1)
    w_query, w_key, w_value, w_out, w_gate, w_up, w_down, gain_one, gain_two = unpack(replica)
    lengths_row = lengths[0]
    local_index = narrow_rank * token_rows + jnp.arange(token_rows, dtype=jnp.int32)
    segment, token_position = place_tokens(local_index, lengths_row)
    group_index = jnp.arange(group_rows, dtype=jnp.int32)
    key_segment = place_tokens(group_index, lengths_row)[0]
    first_start = local_index[0] - token_position[0]
    last_index = local_index[token_rows - 1]
    range_rows = min(512, group_rows)
    span_starts = list(range(0, group_rows, range_rows))
    resid = tokens.astype(jnp.float32)
    normed_one, inverse_one = normalize(resid)
    hidden_one = (normed_one * gain_one.astype(jnp.float32)).astype(jnp.bfloat16)
    query = jnp.dot(hidden_one, w_query, preferred_element_type=jnp.float32)
    key_projection = jnp.dot(hidden_one, w_key, preferred_element_type=jnp.float32)
    value_proj = jnp.dot(hidden_one, w_value, preferred_element_type=jnp.float32)
    query_batch = apply_rotary(query, token_position, QUERY_HEADS, 1.0).astype(jnp.bfloat16)
    key_batch = apply_rotary(key_projection, token_position, KEYVAL_HEADS, 1.0).astype(jnp.bfloat16)
    value_batch = value_proj.astype(jnp.bfloat16)
    kv_width = KEYVAL_HEADS * HEAD_SIZE
    kv_all = lax.all_gather(
        jnp.concatenate([key_batch, value_batch], axis=1), "narrow", axis=0, tiled=True
    )
    key_all, value_all = kv_all[:, :kv_width], kv_all[:, kv_width:]
    query_tensor_split = query_batch.reshape(token_rows, KEYVAL_HEADS, group_width, HEAD_SIZE)

    def span_setup(span_start, key_source, value_source):
        key_tensor_split = lax.slice_in_dim(
            key_source, span_start, span_start + range_rows
        ).reshape(range_rows, KEYVAL_HEADS, HEAD_SIZE)
        value_tensor_split = lax.slice_in_dim(
            value_source, span_start, span_start + range_rows
        ).reshape(range_rows, KEYVAL_HEADS, HEAD_SIZE)
        span_segment = lax.slice_in_dim(key_segment, span_start, span_start + range_rows)
        span_index = lax.slice_in_dim(group_index, span_start, span_start + range_rows)
        allowed = (segment[:, None] == span_segment[None, :]) & (
            span_index[None, :] <= local_index[:, None]
        )
        needed = (span_start <= last_index) & (span_start + range_rows - 1 >= first_start)
        return (key_tensor_split, value_tensor_split, allowed[None, None], needed)

    running_maximum = jnp.full((KEYVAL_HEADS, group_width, token_rows), masked_logits, jnp.float32)
    running_denominator = jnp.zeros((KEYVAL_HEADS, group_width, token_rows), jnp.float32)
    for span_start in span_starts:
        key_tensor_split, value_tensor_split, allowed, needed = span_setup(
            span_start, key_all, value_all
        )

        def extend(carry):
            old_top, old_total = carry
            scores = (
                jnp.einsum(
                    "qgrd,kgd->grqk",
                    query_tensor_split,
                    key_tensor_split,
                    preferred_element_type=jnp.float32,
                )
                * score_scale
            )
            new_top = jnp.maximum(
                old_top, jnp.max(jnp.where(allowed, scores, masked_logits), axis=-1)
            )
            span_sum = jnp.sum(
                jnp.where(allowed, jnp.exp(scores - new_top[..., None]), 0.0), axis=-1
            )
            return (new_top, old_total * jnp.exp(old_top - new_top) + span_sum)

        running_maximum, running_denominator = lax.cond(
            needed, extend, keep_carry, (running_maximum, running_denominator)
        )
    lse = running_maximum + jnp.log(running_denominator)
    running_total = jnp.zeros((token_rows, KEYVAL_HEADS, group_width, HEAD_SIZE), jnp.float32)
    for span_start in span_starts:
        key_tensor_split, value_tensor_split, allowed, needed = span_setup(
            span_start, key_all, value_all
        )

        def weigh_values(carry):
            scores = (
                jnp.einsum(
                    "qgrd,kgd->grqk",
                    query_tensor_split,
                    key_tensor_split,
                    preferred_element_type=jnp.float32,
                )
                * score_scale
            )
            probs_b = jnp.where(allowed, jnp.exp(scores - lse[..., None]), 0.0).astype(jnp.bfloat16)
            return carry + jnp.einsum(
                "grqk,kgd->qgrd", probs_b, value_tensor_split, preferred_element_type=jnp.float32
            )

        running_total = lax.cond(needed, weigh_values, keep_carry, running_total)
    attention_output = running_total.reshape(token_rows, QUERY_HEADS * HEAD_SIZE).astype(
        jnp.bfloat16
    )
    mixed = resid + jnp.dot(attention_output, w_out, preferred_element_type=jnp.float32)
    normed_two, inverse_two = normalize(mixed)
    hidden_two = (normed_two * gain_two.astype(jnp.float32)).astype(jnp.bfloat16)
    gate = jnp.dot(hidden_two, w_gate, preferred_element_type=jnp.float32)
    upward = jnp.dot(hidden_two, w_up, preferred_element_type=jnp.float32)
    sigma = jax.nn.sigmoid(gate)
    activated = (gate * sigma * upward).astype(jnp.bfloat16)
    output = (mixed + jnp.dot(activated, w_down, preferred_element_type=jnp.float32)).astype(
        jnp.bfloat16
    )
    d_act = jnp.dot(cotangent, w_down.T, preferred_element_type=jnp.float32)
    g_down = jnp.dot(activated.T, cotangent, preferred_element_type=jnp.float32)
    d_gate = (d_act * upward * sigma * (1.0 + gate * (1.0 - sigma))).astype(jnp.bfloat16)
    d_up = (d_act * gate * sigma).astype(jnp.bfloat16)
    g_gate = jnp.dot(hidden_two.T, d_gate, preferred_element_type=jnp.float32)
    g_up = jnp.dot(hidden_two.T, d_up, preferred_element_type=jnp.float32)
    d_hidden_two = jnp.dot(d_gate, w_gate.T, preferred_element_type=jnp.float32) + jnp.dot(
        d_up, w_up.T, preferred_element_type=jnp.float32
    )
    g_gain_two = jnp.sum(d_hidden_two * normed_two, axis=0)
    dn_two = d_hidden_two * gain_two.astype(jnp.float32)
    d_mixed = cotangent.astype(jnp.float32) + inverse_two * (
        dn_two - normed_two * jnp.mean(dn_two * normed_two, axis=-1, keepdims=True)
    )
    d_mixed_b = d_mixed.astype(jnp.bfloat16)
    g_out = jnp.dot(attention_output.T, d_mixed_b, preferred_element_type=jnp.float32)
    attention_output_gradient = jnp.dot(
        d_mixed_b, w_out.T, preferred_element_type=jnp.float32
    ).astype(jnp.bfloat16)
    split_gradient = attention_output_gradient.reshape(
        token_rows, KEYVAL_HEADS, group_width, HEAD_SIZE
    )
    attention_output_split = attention_output.reshape(
        token_rows, KEYVAL_HEADS, group_width, HEAD_SIZE
    )
    softmax_correction = jnp.sum(
        split_gradient.astype(jnp.float32) * attention_output_split.astype(jnp.float32), axis=-1
    ).transpose(1, 2, 0)
    key_back, value_back = (key_all, value_all)
    query_gradient_running = jnp.zeros(
        (token_rows, KEYVAL_HEADS, group_width, HEAD_SIZE), jnp.float32
    )
    key_contributions = []
    value_contributions = []
    for span_start in span_starts:
        key_tensor_split, value_tensor_split, allowed, needed = span_setup(
            span_start, key_back, value_back
        )

        def back_span(carry):
            scores = (
                jnp.einsum(
                    "qgrd,kgd->grqk",
                    query_tensor_split,
                    key_tensor_split,
                    preferred_element_type=jnp.float32,
                )
                * score_scale
            )
            probs = jnp.where(allowed, jnp.exp(scores - lse[..., None]), 0.0)
            probs_b = probs.astype(jnp.bfloat16)
            value_gradient_range = jnp.einsum(
                "pozf,zpom->fpm", probs_b, split_gradient, preferred_element_type=jnp.float32
            )
            d_probs = jnp.einsum(
                "qgrd,kgd->grqk",
                split_gradient,
                value_tensor_split,
                preferred_element_type=jnp.float32,
            )
            score_gradient = (
                probs * (d_probs - softmax_correction[..., None]) * score_scale
            ).astype(jnp.bfloat16)
            new_acc = carry + jnp.einsum(
                "grqk,kgd->qgrd",
                score_gradient,
                key_tensor_split,
                preferred_element_type=jnp.float32,
            )
            key_gradient_range = jnp.einsum(
                "pozf,zpom->fpm",
                score_gradient,
                query_tensor_split,
                preferred_element_type=jnp.float32,
            )
            return (new_acc, key_gradient_range, value_gradient_range)

        def skip_span(carry):
            blank_range = jnp.zeros((range_rows, KEYVAL_HEADS, HEAD_SIZE), jnp.float32)
            return (carry, blank_range, blank_range)

        query_gradient_running, key_gradient_range, value_gradient_range = lax.cond(
            needed, back_span, skip_span, query_gradient_running
        )
        key_contributions.append(key_gradient_range.reshape(range_rows, KEYVAL_HEADS * HEAD_SIZE))
        value_contributions.append(
            value_gradient_range.reshape(range_rows, KEYVAL_HEADS * HEAD_SIZE)
        )
    key_sum_in = jnp.concatenate(key_contributions, axis=0)
    value_sum_in = jnp.concatenate(value_contributions, axis=0)
    kv_grad = lax.psum_scatter(
        jnp.concatenate([key_sum_in, value_sum_in], axis=1), "narrow", scatter_dimension=0, tiled=True
    )
    key_gradient, value_gradient = kv_grad[:, :kv_width], kv_grad[:, kv_width:]
    d_query = query_gradient_running.reshape(token_rows, QUERY_HEADS * HEAD_SIZE)
    d_query_b = apply_rotary(d_query, token_position, QUERY_HEADS, -1.0).astype(jnp.bfloat16)
    key_gradient_batch = apply_rotary(key_gradient, token_position, KEYVAL_HEADS, -1.0).astype(
        jnp.bfloat16
    )
    value_gradient_batch = value_gradient.astype(jnp.bfloat16)
    g_query = jnp.dot(hidden_one.T, d_query_b, preferred_element_type=jnp.float32)
    g_key = jnp.dot(hidden_one.T, key_gradient_batch, preferred_element_type=jnp.float32)
    g_value = jnp.dot(hidden_one.T, value_gradient_batch, preferred_element_type=jnp.float32)
    d_hidden_one = (
        jnp.dot(d_query_b, w_query.T, preferred_element_type=jnp.float32)
        + jnp.dot(key_gradient_batch, w_key.T, preferred_element_type=jnp.float32)
        + jnp.dot(value_gradient_batch, w_value.T, preferred_element_type=jnp.float32)
    )
    g_gain_one = jnp.sum(d_hidden_one * normed_one, axis=0)
    dn_one = d_hidden_one * gain_one.astype(jnp.float32)
    d_tokens = (
        d_mixed
        + inverse_one
        * (dn_one - normed_one * jnp.mean(dn_one * normed_one, axis=-1, keepdims=True))
    ).astype(jnp.bfloat16)
    local_grads = jnp.concatenate(
        [
            g_query.reshape(-1),
            g_key.reshape(-1),
            g_value.reshape(-1),
            g_out.reshape(-1),
            g_gate.reshape(-1),
            g_up.reshape(-1),
            g_down.reshape(-1),
            g_gain_one,
            g_gain_two,
        ]
    )
    whole_sum = lax.psum(local_grads, ("wide", "narrow"))
    summed = lax.dynamic_slice_in_dim(whole_sum, narrow_rank * shard_len, shard_len)
    token_total = token_rows * narrow_size * lax.axis_size("wide")
    gradient = summed * (1.0 / math.sqrt(token_total))
    new_first = beta_one * first_moment + (1.0 - beta_one) * gradient
    new_second = beta_two * second_moment + (1.0 - beta_two) * gradient * gradient
    first_hat = new_first / (1.0 - beta_one**STEP)
    second_hat = new_second / (1.0 - beta_two**STEP)
    entry_index = narrow_rank * shard_len + jnp.arange(shard_len, dtype=jnp.int32)
    decay = jnp.where(entry_index < NPARAM - 2 * MODEL_WIDTH, decay_rate, 0.0)
    new_master = master - learn_rate * (
        first_hat / (jnp.sqrt(second_hat) + adam_eps) + decay * master
    )
    return (output, d_tokens, gradient, new_master, new_first, new_second)


def solution(mesh):
    in_specs = (
        P(("wide", "narrow"), None),
        P(("wide", "narrow"), None),
        P("wide", None),
        P("narrow"),
        P("narrow"),
        P("narrow"),
    )
    out_specs = (
        P(("wide", "narrow"), None),
        P(("wide", "narrow"), None),
        P("narrow"),
        P("narrow"),
        P("narrow"),
        P("narrow"),
    )
    return jax.shard_map(body, mesh=mesh, in_specs=in_specs, out_specs=out_specs, check_vma=False)
```

```python
import math

import jax
import jax.numpy as jnp
from jax import lax
from jax.sharding import PartitionSpec as P

MODEL_WIDTH = 512
QUERY_HEADS = 15
KEYVAL_HEADS = 5
HEAD_SIZE = 64
FEEDFWD_UNITS = 1280
STEP = 4
NPARAM = 3277824


eps_norm = 1e-05
rope_base = 100000.0
beta_one = 0.9
beta_two = 0.95
learn_rate = 0.03
decay_rate = 0.1
adam_eps = 1e-08
masked_logits = -1e30


def unpack(flat):
    arrangement_list = [
        (MODEL_WIDTH, QUERY_HEADS * HEAD_SIZE),
        (MODEL_WIDTH, KEYVAL_HEADS * HEAD_SIZE),
        (MODEL_WIDTH, KEYVAL_HEADS * HEAD_SIZE),
        (QUERY_HEADS * HEAD_SIZE, MODEL_WIDTH),
        (MODEL_WIDTH, FEEDFWD_UNITS),
        (MODEL_WIDTH, FEEDFWD_UNITS),
        (FEEDFWD_UNITS, MODEL_WIDTH),
        (MODEL_WIDTH,),
        (MODEL_WIDTH,),
    ]
    pieces = []
    offset = 0
    for layout in arrangement_list:
        length = math.prod(layout)
        pieces.append(flat[offset : offset + length].reshape(layout))
        offset = offset + length
    return pieces


def place_tokens(indices, lengths_row):
    seq_ends = jnp.cumsum(lengths_row)
    seq_starts = seq_ends - lengths_row
    member = (indices[:, None] >= seq_starts[None, :]) & (indices[:, None] < seq_ends[None, :])
    numbers = jnp.arange(lengths_row.shape[0], dtype=jnp.int32)
    segment = jnp.sum(jnp.where(member, numbers[None, :], 0), axis=1)
    token_position = indices - jnp.sum(jnp.where(member, seq_starts[None, :], 0), axis=1)
    return (segment, token_position)


def normalize(values):
    inverse_rms = lax.rsqrt(jnp.mean(values * values, axis=-1, keepdims=True) + eps_norm)
    return (values * inverse_rms, inverse_rms)


def apply_rotary(values, token_position, head_count, turn_sign):
    half_dim = HEAD_SIZE // 2
    inverse = rope_base ** (-2.0 * jnp.arange(half_dim, dtype=jnp.float32) / HEAD_SIZE)
    angles = token_position.astype(jnp.float32)[:, None] * inverse[None, :]
    cosine = jnp.cos(angles)[:, None, :]
    sine = turn_sign * jnp.sin(angles)[:, None, :]
    shaped = values.reshape(values.shape[0], head_count, HEAD_SIZE)
    first_half = shaped[:, :, :half_dim]
    second_half = shaped[:, :, half_dim:]
    turned = jnp.concatenate(
        [first_half * cosine - second_half * sine, second_half * cosine + first_half * sine],
        axis=-1,
    )
    return turned.reshape(values.shape)


def keep_carry(carry):
    return carry


def body(tokens, cotangent, lengths, master, first_moment, second_moment):
    token_rows = tokens.shape[0]
    narrow_size = lax.axis_size("narrow")
    group_rows = token_rows * narrow_size
    narrow_rank = lax.axis_index("narrow")
    group_width = QUERY_HEADS // KEYVAL_HEADS
    score_scale = HEAD_SIZE ** (-0.5)
    shard_len = master.shape[0]
    replica = lax.all_gather(
        master.astype(jnp.bfloat16).reshape(shard_len // 128, 128), "narrow", axis=0, tiled=False
    ).reshape(-1)
    w_query, w_key, w_value, w_out, w_gate, w_up, w_down, gain_one, gain_two = unpack(replica)
    lengths_row = lengths[0]
    local_index = narrow_rank * token_rows + jnp.arange(token_rows, dtype=jnp.int32)
    segment, token_position = place_tokens(local_index, lengths_row)
    group_index = jnp.arange(group_rows, dtype=jnp.int32)
    key_segment = place_tokens(group_index, lengths_row)[0]
    first_start = local_index[0] - token_position[0]
    last_index = local_index[token_rows - 1]
    range_rows = min(512, group_rows)
    span_starts = list(range(0, group_rows, range_rows))
    resid = tokens.astype(jnp.float32)
    normed_one, inverse_one = normalize(resid)
    hidden_one = (normed_one * gain_one.astype(jnp.float32)).astype(jnp.bfloat16)
    query = jnp.dot(hidden_one, w_query, preferred_element_type=jnp.float32)
    key_projection = jnp.dot(hidden_one, w_key, preferred_element_type=jnp.float32)
    value_proj = jnp.dot(hidden_one, w_value, preferred_element_type=jnp.float32)
    query_batch = apply_rotary(query, token_position, QUERY_HEADS, 1.0).astype(jnp.bfloat16)
    key_batch = apply_rotary(key_projection, token_position, KEYVAL_HEADS, 1.0).astype(jnp.bfloat16)
    value_batch = value_proj.astype(jnp.bfloat16)
    kv_width = KEYVAL_HEADS * HEAD_SIZE
    kv_all = lax.all_gather(
        jnp.concatenate([key_batch, value_batch], axis=1), "narrow", axis=0, tiled=True
    )
    key_all, value_all = kv_all[:, :kv_width], kv_all[:, kv_width:]
    query_tensor_split = query_batch.reshape(token_rows, KEYVAL_HEADS, group_width, HEAD_SIZE)

    def span_setup(span_start, key_source, value_source):
        key_tensor_split = lax.slice_in_dim(
            key_source, span_start, span_start + range_rows
        ).reshape(range_rows, KEYVAL_HEADS, HEAD_SIZE)
        value_tensor_split = lax.slice_in_dim(
            value_source, span_start, span_start + range_rows
        ).reshape(range_rows, KEYVAL_HEADS, HEAD_SIZE)
        span_segment = lax.slice_in_dim(key_segment, span_start, span_start + range_rows)
        span_index = lax.slice_in_dim(group_index, span_start, span_start + range_rows)
        allowed = (segment[:, None] == span_segment[None, :]) & (
            span_index[None, :] <= local_index[:, None]
        )
        needed = (span_start <= last_index) & (span_start + range_rows - 1 >= first_start)
        return (key_tensor_split, value_tensor_split, allowed[None, None], needed)

    running_maximum = jnp.full((KEYVAL_HEADS, group_width, token_rows), masked_logits, jnp.float32)
    running_denominator = jnp.zeros((KEYVAL_HEADS, group_width, token_rows), jnp.float32)
    for span_start in span_starts:
        key_tensor_split, value_tensor_split, allowed, needed = span_setup(
            span_start, key_all, value_all
        )

        def extend(carry):
            old_top, old_total = carry
            scores = (
                jnp.einsum(
                    "qgrd,kgd->grqk",
                    query_tensor_split,
                    key_tensor_split,
                    preferred_element_type=jnp.float32,
                )
                * score_scale
            )
            new_top = jnp.maximum(
                old_top, jnp.max(jnp.where(allowed, scores, masked_logits), axis=-1)
            )
            span_sum = jnp.sum(
                jnp.where(allowed, jnp.exp(scores - new_top[..., None]), 0.0), axis=-1
            )
            return (new_top, old_total * jnp.exp(old_top - new_top) + span_sum)

        running_maximum, running_denominator = lax.cond(
            needed, extend, keep_carry, (running_maximum, running_denominator)
        )
    lse = running_maximum + jnp.log(running_denominator)
    running_total = jnp.zeros((token_rows, KEYVAL_HEADS, group_width, HEAD_SIZE), jnp.float32)
    for span_start in span_starts:
        key_tensor_split, value_tensor_split, allowed, needed = span_setup(
            span_start, key_all, value_all
        )

        def weigh_values(carry):
            scores = (
                jnp.einsum(
                    "qgrd,kgd->grqk",
                    query_tensor_split,
                    key_tensor_split,
                    preferred_element_type=jnp.float32,
                )
                * score_scale
            )
            probs_b = jnp.where(allowed, jnp.exp(scores - lse[..., None]), 0.0).astype(jnp.bfloat16)
            return carry + jnp.einsum(
                "grqk,kgd->qgrd", probs_b, value_tensor_split, preferred_element_type=jnp.float32
            )

        running_total = lax.cond(needed, weigh_values, keep_carry, running_total)
    attention_output = running_total.reshape(token_rows, QUERY_HEADS * HEAD_SIZE).astype(
        jnp.bfloat16
    )
    mixed = resid + jnp.dot(attention_output, w_out, preferred_element_type=jnp.float32)
    normed_two, inverse_two = normalize(mixed)
    hidden_two = (normed_two * gain_two.astype(jnp.float32)).astype(jnp.bfloat16)
    gate = jnp.dot(hidden_two, w_gate, preferred_element_type=jnp.float32)
    upward = jnp.dot(hidden_two, w_up, preferred_element_type=jnp.float32)
    sigma = jax.nn.sigmoid(gate)
    activated = (gate * sigma * upward).astype(jnp.bfloat16)
    output = (mixed + jnp.dot(activated, w_down, preferred_element_type=jnp.float32)).astype(
        jnp.bfloat16
    )
    d_act = jnp.dot(cotangent, w_down.T, preferred_element_type=jnp.float32)
    g_down = jnp.dot(activated.T, cotangent, preferred_element_type=jnp.float32)
    d_gate = (d_act * upward * sigma * (1.0 + gate * (1.0 - sigma))).astype(jnp.bfloat16)
    d_up = (d_act * gate * sigma).astype(jnp.bfloat16)
    g_gate = jnp.dot(hidden_two.T, d_gate, preferred_element_type=jnp.float32)
    g_up = jnp.dot(hidden_two.T, d_up, preferred_element_type=jnp.float32)
    d_hidden_two = jnp.dot(d_gate, w_gate.T, preferred_element_type=jnp.float32) + jnp.dot(
        d_up, w_up.T, preferred_element_type=jnp.float32
    )
    g_gain_two = jnp.sum(d_hidden_two * normed_two, axis=0)
    dn_two = d_hidden_two * gain_two.astype(jnp.float32)
    d_mixed = cotangent.astype(jnp.float32) + inverse_two * (
        dn_two - normed_two * jnp.mean(dn_two * normed_two, axis=-1, keepdims=True)
    )
    d_mixed_b = d_mixed.astype(jnp.bfloat16)
    g_out = jnp.dot(attention_output.T, d_mixed_b, preferred_element_type=jnp.float32)
    early_grads = jnp.concatenate(
        [g_out.reshape(-1), g_gate.reshape(-1), g_up.reshape(-1), g_down.reshape(-1), g_gain_two]
    )
    early_grads, d_mixed_b = lax.optimization_barrier((early_grads, d_mixed_b))
    early_sum = lax.psum(early_grads, ("wide", "narrow"))
    attention_output_gradient = jnp.dot(
        d_mixed_b, w_out.T, preferred_element_type=jnp.float32
    ).astype(jnp.bfloat16)
    split_gradient = attention_output_gradient.reshape(
        token_rows, KEYVAL_HEADS, group_width, HEAD_SIZE
    )
    attention_output_split = attention_output.reshape(
        token_rows, KEYVAL_HEADS, group_width, HEAD_SIZE
    )
    softmax_correction = jnp.sum(
        split_gradient.astype(jnp.float32) * attention_output_split.astype(jnp.float32), axis=-1
    ).transpose(1, 2, 0)
    key_back, value_back = (key_all, value_all)
    query_gradient_running = jnp.zeros(
        (token_rows, KEYVAL_HEADS, group_width, HEAD_SIZE), jnp.float32
    )
    key_contributions = []
    value_contributions = []
    for span_start in span_starts:
        key_tensor_split, value_tensor_split, allowed, needed = span_setup(
            span_start, key_back, value_back
        )

        def back_span(carry):
            scores = (
                jnp.einsum(
                    "qgrd,kgd->grqk",
                    query_tensor_split,
                    key_tensor_split,
                    preferred_element_type=jnp.float32,
                )
                * score_scale
            )
            probs = jnp.where(allowed, jnp.exp(scores - lse[..., None]), 0.0)
            probs_b = probs.astype(jnp.bfloat16)
            value_gradient_range = jnp.einsum(
                "pozf,zpom->fpm", probs_b, split_gradient, preferred_element_type=jnp.float32
            )
            d_probs = jnp.einsum(
                "qgrd,kgd->grqk",
                split_gradient,
                value_tensor_split,
                preferred_element_type=jnp.float32,
            )
            score_gradient = (
                probs * (d_probs - softmax_correction[..., None]) * score_scale
            ).astype(jnp.bfloat16)
            new_acc = carry + jnp.einsum(
                "grqk,kgd->qgrd",
                score_gradient,
                key_tensor_split,
                preferred_element_type=jnp.float32,
            )
            key_gradient_range = jnp.einsum(
                "pozf,zpom->fpm",
                score_gradient,
                query_tensor_split,
                preferred_element_type=jnp.float32,
            )
            return (new_acc, key_gradient_range, value_gradient_range)

        def skip_span(carry):
            blank_range = jnp.zeros((range_rows, KEYVAL_HEADS, HEAD_SIZE), jnp.float32)
            return (carry, blank_range, blank_range)

        query_gradient_running, key_gradient_range, value_gradient_range = lax.cond(
            needed, back_span, skip_span, query_gradient_running
        )
        key_contributions.append(key_gradient_range.reshape(range_rows, KEYVAL_HEADS * HEAD_SIZE))
        value_contributions.append(
            value_gradient_range.reshape(range_rows, KEYVAL_HEADS * HEAD_SIZE)
        )
    key_sum_in = jnp.concatenate(key_contributions, axis=0)
    value_sum_in = jnp.concatenate(value_contributions, axis=0)
    kv_sum_in = jnp.concatenate([key_sum_in, value_sum_in], axis=1).reshape(
        narrow_size, token_rows, 2 * kv_width
    )
    kv_grad = kv_sum_in[narrow_rank]
    for shift in range(1, narrow_size):
        sender_block = kv_sum_in[lax.rem(narrow_rank + narrow_size - shift, narrow_size)]
        kv_grad = kv_grad + lax.ppermute(
            sender_block,
            "narrow",
            [(source, source - shift) for source in range(shift, narrow_size)],
        )
    key_gradient, value_gradient = kv_grad[:, :kv_width], kv_grad[:, kv_width:]
    d_query = query_gradient_running.reshape(token_rows, QUERY_HEADS * HEAD_SIZE)
    d_query_b = apply_rotary(d_query, token_position, QUERY_HEADS, -1.0).astype(jnp.bfloat16)
    key_gradient_batch = apply_rotary(key_gradient, token_position, KEYVAL_HEADS, -1.0).astype(
        jnp.bfloat16
    )
    value_gradient_batch = value_gradient.astype(jnp.bfloat16)
    g_query = jnp.dot(hidden_one.T, d_query_b, preferred_element_type=jnp.float32)
    g_key = jnp.dot(hidden_one.T, key_gradient_batch, preferred_element_type=jnp.float32)
    g_value = jnp.dot(hidden_one.T, value_gradient_batch, preferred_element_type=jnp.float32)
    d_hidden_one = (
        jnp.dot(d_query_b, w_query.T, preferred_element_type=jnp.float32)
        + jnp.dot(key_gradient_batch, w_key.T, preferred_element_type=jnp.float32)
        + jnp.dot(value_gradient_batch, w_value.T, preferred_element_type=jnp.float32)
    )
    g_gain_one = jnp.sum(d_hidden_one * normed_one, axis=0)
    dn_one = d_hidden_one * gain_one.astype(jnp.float32)
    d_tokens = (
        d_mixed
        + inverse_one
        * (dn_one - normed_one * jnp.mean(dn_one * normed_one, axis=-1, keepdims=True))
    ).astype(jnp.bfloat16)
    late_grads = jnp.concatenate(
        [g_query.reshape(-1), g_key.reshape(-1), g_value.reshape(-1), g_gain_one]
    )
    late_grads, early_sum = lax.optimization_barrier((late_grads, early_sum))
    late_sum = lax.psum(late_grads, ("wide", "narrow"))
    late_split = late_grads.shape[0] - MODEL_WIDTH
    early_split = early_grads.shape[0] - MODEL_WIDTH
    whole_sum = jnp.concatenate(
        [
            late_sum[:late_split],
            early_sum[:early_split],
            late_sum[late_split:],
            early_sum[early_split:],
        ]
    )
    summed = lax.dynamic_slice_in_dim(whole_sum, narrow_rank * shard_len, shard_len)
    token_total = token_rows * narrow_size * lax.axis_size("wide")
    gradient = summed * (1.0 / math.sqrt(token_total))
    new_first = beta_one * first_moment + (1.0 - beta_one) * gradient
    new_second = beta_two * second_moment + (1.0 - beta_two) * gradient * gradient
    first_hat = new_first / (1.0 - beta_one**STEP)
    second_hat = new_second / (1.0 - beta_two**STEP)
    entry_index = narrow_rank * shard_len + jnp.arange(shard_len, dtype=jnp.int32)
    decay = jnp.where(entry_index < NPARAM - 2 * MODEL_WIDTH, decay_rate, 0.0)
    new_master = master - learn_rate * (
        first_hat / (jnp.sqrt(second_hat) + adam_eps) + decay * master
    )
    return (output, d_tokens, gradient, new_master, new_first, new_second)


def solution(mesh):
    in_specs = (
        P(("wide", "narrow"), None),
        P(("wide", "narrow"), None),
        P("wide", None),
        P("narrow"),
        P("narrow"),
        P("narrow"),
    )
    out_specs = (
        P(("wide", "narrow"), None),
        P(("wide", "narrow"), None),
        P("narrow"),
        P("narrow"),
        P("narrow"),
        P("narrow"),
    )
    return jax.shard_map(body, mesh=mesh, in_specs=in_specs, out_specs=out_specs, check_vma=False)
```

```python
import math

import jax
import jax.numpy as jnp
from jax import lax
from jax.sharding import PartitionSpec as P

MODEL_WIDTH = 512
QUERY_HEADS = 15
KEYVAL_HEADS = 5
HEAD_SIZE = 64
FEEDFWD_UNITS = 1280
STEP = 4
NPARAM = 3277824


eps_norm = 1e-05
rope_base = 100000.0
beta_one = 0.9
beta_two = 0.95
learn_rate = 0.03
decay_rate = 0.1
adam_eps = 1e-08
masked_logits = -1e30


def unpack(flat):
    arrangement_list = [
        (MODEL_WIDTH, QUERY_HEADS * HEAD_SIZE),
        (MODEL_WIDTH, KEYVAL_HEADS * HEAD_SIZE),
        (MODEL_WIDTH, KEYVAL_HEADS * HEAD_SIZE),
        (QUERY_HEADS * HEAD_SIZE, MODEL_WIDTH),
        (MODEL_WIDTH, FEEDFWD_UNITS),
        (MODEL_WIDTH, FEEDFWD_UNITS),
        (FEEDFWD_UNITS, MODEL_WIDTH),
        (MODEL_WIDTH,),
        (MODEL_WIDTH,),
    ]
    pieces = []
    offset = 0
    for layout in arrangement_list:
        length = math.prod(layout)
        pieces.append(flat[offset : offset + length].reshape(layout))
        offset = offset + length
    return pieces


def place_tokens(indices, lengths_row):
    seq_ends = jnp.cumsum(lengths_row)
    seq_starts = seq_ends - lengths_row
    member = (indices[:, None] >= seq_starts[None, :]) & (indices[:, None] < seq_ends[None, :])
    numbers = jnp.arange(lengths_row.shape[0], dtype=jnp.int32)
    segment = jnp.sum(jnp.where(member, numbers[None, :], 0), axis=1)
    token_position = indices - jnp.sum(jnp.where(member, seq_starts[None, :], 0), axis=1)
    return (segment, token_position)


def normalize(values):
    inverse_rms = lax.rsqrt(jnp.mean(values * values, axis=-1, keepdims=True) + eps_norm)
    return (values * inverse_rms, inverse_rms)


def apply_rotary(values, token_position, head_count, turn_sign):
    half_dim = HEAD_SIZE // 2
    inverse = rope_base ** (-2.0 * jnp.arange(half_dim, dtype=jnp.float32) / HEAD_SIZE)
    angles = token_position.astype(jnp.float32)[:, None] * inverse[None, :]
    cosine = jnp.cos(angles)[:, None, :]
    sine = turn_sign * jnp.sin(angles)[:, None, :]
    shaped = values.reshape(values.shape[0], head_count, HEAD_SIZE)
    first_half = shaped[:, :, :half_dim]
    second_half = shaped[:, :, half_dim:]
    turned = jnp.concatenate(
        [first_half * cosine - second_half * sine, second_half * cosine + first_half * sine],
        axis=-1,
    )
    return turned.reshape(values.shape)


def keep_carry(carry):
    return carry


def body(tokens, cotangent, lengths, master, first_moment, second_moment):
    token_rows = tokens.shape[0]
    narrow_size = lax.axis_size("narrow")
    group_rows = token_rows * narrow_size
    narrow_rank = lax.axis_index("narrow")
    group_width = QUERY_HEADS // KEYVAL_HEADS
    score_scale = HEAD_SIZE ** (-0.5)
    shard_len = master.shape[0]
    replica = lax.all_gather(
        master.astype(jnp.bfloat16).reshape(shard_len // 128, 128), "narrow", axis=0, tiled=False
    ).reshape(-1)
    w_query, w_key, w_value, w_out, w_gate, w_up, w_down, gain_one, gain_two = unpack(replica)
    lengths_row = lengths[0]
    local_index = narrow_rank * token_rows + jnp.arange(token_rows, dtype=jnp.int32)
    segment, token_position = place_tokens(local_index, lengths_row)
    group_index = jnp.arange(group_rows, dtype=jnp.int32)
    key_segment = place_tokens(group_index, lengths_row)[0]
    first_start = local_index[0] - token_position[0]
    last_index = local_index[token_rows - 1]
    range_rows = min(512, group_rows)
    span_starts = list(range(0, group_rows, range_rows))
    resid = tokens.astype(jnp.float32)
    normed_one, inverse_one = normalize(resid)
    hidden_one = (normed_one * gain_one.astype(jnp.float32)).astype(jnp.bfloat16)
    query = jnp.dot(hidden_one, w_query, preferred_element_type=jnp.float32)
    key_projection = jnp.dot(hidden_one, w_key, preferred_element_type=jnp.float32)
    value_proj = jnp.dot(hidden_one, w_value, preferred_element_type=jnp.float32)
    query_batch = apply_rotary(query, token_position, QUERY_HEADS, 1.0).astype(jnp.bfloat16)
    key_batch = apply_rotary(key_projection, token_position, KEYVAL_HEADS, 1.0).astype(jnp.bfloat16)
    value_batch = value_proj.astype(jnp.bfloat16)
    kv_width = KEYVAL_HEADS * HEAD_SIZE
    kv_all = lax.all_gather(
        jnp.concatenate([key_batch, value_batch], axis=1), "narrow", axis=0, tiled=True
    )
    key_all, value_all = kv_all[:, :kv_width], kv_all[:, kv_width:]
    query_tensor_split = query_batch.reshape(token_rows, KEYVAL_HEADS, group_width, HEAD_SIZE)

    def span_setup(span_start, key_source, value_source):
        key_tensor_split = lax.slice_in_dim(
            key_source, span_start, span_start + range_rows
        ).reshape(range_rows, KEYVAL_HEADS, HEAD_SIZE)
        value_tensor_split = lax.slice_in_dim(
            value_source, span_start, span_start + range_rows
        ).reshape(range_rows, KEYVAL_HEADS, HEAD_SIZE)
        span_segment = lax.slice_in_dim(key_segment, span_start, span_start + range_rows)
        span_index = lax.slice_in_dim(group_index, span_start, span_start + range_rows)
        allowed = (segment[:, None] == span_segment[None, :]) & (
            span_index[None, :] <= local_index[:, None]
        )
        needed = (span_start <= last_index) & (span_start + range_rows - 1 >= first_start)
        return (key_tensor_split, value_tensor_split, allowed[None, None], needed)

    running_maximum = jnp.full((KEYVAL_HEADS, group_width, token_rows), masked_logits, jnp.float32)
    running_denominator = jnp.zeros((KEYVAL_HEADS, group_width, token_rows), jnp.float32)
    for span_start in span_starts:
        key_tensor_split, value_tensor_split, allowed, needed = span_setup(
            span_start, key_all, value_all
        )

        def extend(carry):
            old_top, old_total = carry
            scores = (
                jnp.einsum(
                    "qgrd,kgd->grqk",
                    query_tensor_split,
                    key_tensor_split,
                    preferred_element_type=jnp.float32,
                )
                * score_scale
            )
            new_top = jnp.maximum(
                old_top, jnp.max(jnp.where(allowed, scores, masked_logits), axis=-1)
            )
            span_sum = jnp.sum(
                jnp.where(allowed, jnp.exp(scores - new_top[..., None]), 0.0), axis=-1
            )
            return (new_top, old_total * jnp.exp(old_top - new_top) + span_sum)

        running_maximum, running_denominator = lax.cond(
            needed, extend, keep_carry, (running_maximum, running_denominator)
        )
    lse = running_maximum + jnp.log(running_denominator)
    running_total = jnp.zeros((token_rows, KEYVAL_HEADS, group_width, HEAD_SIZE), jnp.float32)
    for span_start in span_starts:
        key_tensor_split, value_tensor_split, allowed, needed = span_setup(
            span_start, key_all, value_all
        )

        def weigh_values(carry):
            scores = (
                jnp.einsum(
                    "qgrd,kgd->grqk",
                    query_tensor_split,
                    key_tensor_split,
                    preferred_element_type=jnp.float32,
                )
                * score_scale
            )
            probs_b = jnp.where(allowed, jnp.exp(scores - lse[..., None]), 0.0).astype(jnp.bfloat16)
            return carry + jnp.einsum(
                "grqk,kgd->qgrd", probs_b, value_tensor_split, preferred_element_type=jnp.float32
            )

        running_total = lax.cond(needed, weigh_values, keep_carry, running_total)
    attention_output = running_total.reshape(token_rows, QUERY_HEADS * HEAD_SIZE).astype(
        jnp.bfloat16
    )
    mixed = resid + jnp.dot(attention_output, w_out, preferred_element_type=jnp.float32)
    normed_two, inverse_two = normalize(mixed)
    hidden_two = (normed_two * gain_two.astype(jnp.float32)).astype(jnp.bfloat16)
    gate = jnp.dot(hidden_two, w_gate, preferred_element_type=jnp.float32)
    upward = jnp.dot(hidden_two, w_up, preferred_element_type=jnp.float32)
    sigma = jax.nn.sigmoid(gate)
    activated = (gate * sigma * upward).astype(jnp.bfloat16)
    output = (mixed + jnp.dot(activated, w_down, preferred_element_type=jnp.float32)).astype(
        jnp.bfloat16
    )
    d_act = jnp.dot(cotangent, w_down.T, preferred_element_type=jnp.float32)
    g_down = jnp.dot(activated.T, cotangent, preferred_element_type=jnp.float32)
    d_gate = (d_act * upward * sigma * (1.0 + gate * (1.0 - sigma))).astype(jnp.bfloat16)
    d_up = (d_act * gate * sigma).astype(jnp.bfloat16)
    g_gate = jnp.dot(hidden_two.T, d_gate, preferred_element_type=jnp.float32)
    g_up = jnp.dot(hidden_two.T, d_up, preferred_element_type=jnp.float32)
    d_hidden_two = jnp.dot(d_gate, w_gate.T, preferred_element_type=jnp.float32) + jnp.dot(
        d_up, w_up.T, preferred_element_type=jnp.float32
    )
    g_gain_two = jnp.sum(d_hidden_two * normed_two, axis=0)
    dn_two = d_hidden_two * gain_two.astype(jnp.float32)
    d_mixed = cotangent.astype(jnp.float32) + inverse_two * (
        dn_two - normed_two * jnp.mean(dn_two * normed_two, axis=-1, keepdims=True)
    )
    d_mixed_b = d_mixed.astype(jnp.bfloat16)
    g_out = jnp.dot(attention_output.T, d_mixed_b, preferred_element_type=jnp.float32)
    attention_output_gradient = jnp.dot(
        d_mixed_b, w_out.T, preferred_element_type=jnp.float32
    ).astype(jnp.bfloat16)
    split_gradient = attention_output_gradient.reshape(
        token_rows, KEYVAL_HEADS, group_width, HEAD_SIZE
    )
    attention_output_split = attention_output.reshape(
        token_rows, KEYVAL_HEADS, group_width, HEAD_SIZE
    )
    softmax_correction = jnp.sum(
        split_gradient.astype(jnp.float32) * attention_output_split.astype(jnp.float32), axis=-1
    ).transpose(1, 2, 0)
    key_back, value_back = (key_all, value_all)
    query_gradient_running = jnp.zeros(
        (token_rows, KEYVAL_HEADS, group_width, HEAD_SIZE), jnp.float32
    )
    key_contributions = []
    value_contributions = []
    for span_start in span_starts:
        key_tensor_split, value_tensor_split, allowed, needed = span_setup(
            span_start, key_back, value_back
        )

        def back_span(carry):
            scores = (
                jnp.einsum(
                    "qgrd,kgd->grqk",
                    query_tensor_split,
                    key_tensor_split,
                    preferred_element_type=jnp.float32,
                )
                * score_scale
            )
            probs = jnp.where(allowed, jnp.exp(scores - lse[..., None]), 0.0)
            probs_b = probs.astype(jnp.bfloat16)
            value_gradient_range = jnp.einsum(
                "pozf,zpom->fpm", probs_b, split_gradient, preferred_element_type=jnp.float32
            )
            d_probs = jnp.einsum(
                "qgrd,kgd->grqk",
                split_gradient,
                value_tensor_split,
                preferred_element_type=jnp.float32,
            )
            score_gradient = (
                probs * (d_probs - softmax_correction[..., None]) * score_scale
            ).astype(jnp.bfloat16)
            new_acc = carry + jnp.einsum(
                "grqk,kgd->qgrd",
                score_gradient,
                key_tensor_split,
                preferred_element_type=jnp.float32,
            )
            key_gradient_range = jnp.einsum(
                "pozf,zpom->fpm",
                score_gradient,
                query_tensor_split,
                preferred_element_type=jnp.float32,
            )
            return (new_acc, key_gradient_range, value_gradient_range)

        def skip_span(carry):
            blank_range = jnp.zeros((range_rows, KEYVAL_HEADS, HEAD_SIZE), jnp.float32)
            return (carry, blank_range, blank_range)

        query_gradient_running, key_gradient_range, value_gradient_range = lax.cond(
            needed, back_span, skip_span, query_gradient_running
        )
        key_contributions.append(key_gradient_range.reshape(range_rows, KEYVAL_HEADS * HEAD_SIZE))
        value_contributions.append(
            value_gradient_range.reshape(range_rows, KEYVAL_HEADS * HEAD_SIZE)
        )
    key_sum_in = jnp.concatenate(key_contributions, axis=0)
    value_sum_in = jnp.concatenate(value_contributions, axis=0)
    kv_sum_in = jnp.concatenate([key_sum_in, value_sum_in], axis=1).reshape(
        narrow_size, token_rows, 2 * kv_width
    )
    kv_grad = kv_sum_in[narrow_rank]
    for shift in range(1, narrow_size):
        sender_block = kv_sum_in[lax.rem(narrow_rank + narrow_size - shift, narrow_size)]
        kv_grad = kv_grad + lax.ppermute(
            sender_block,
            "narrow",
            [(source, source - shift) for source in range(shift, narrow_size)],
        )
    key_gradient, value_gradient = kv_grad[:, :kv_width], kv_grad[:, kv_width:]
    d_query = query_gradient_running.reshape(token_rows, QUERY_HEADS * HEAD_SIZE)
    d_query_b = apply_rotary(d_query, token_position, QUERY_HEADS, -1.0).astype(jnp.bfloat16)
    key_gradient_batch = apply_rotary(key_gradient, token_position, KEYVAL_HEADS, -1.0).astype(
        jnp.bfloat16
    )
    value_gradient_batch = value_gradient.astype(jnp.bfloat16)
    g_query = jnp.dot(hidden_one.T, d_query_b, preferred_element_type=jnp.float32)
    g_key = jnp.dot(hidden_one.T, key_gradient_batch, preferred_element_type=jnp.float32)
    g_value = jnp.dot(hidden_one.T, value_gradient_batch, preferred_element_type=jnp.float32)
    d_hidden_one = (
        jnp.dot(d_query_b, w_query.T, preferred_element_type=jnp.float32)
        + jnp.dot(key_gradient_batch, w_key.T, preferred_element_type=jnp.float32)
        + jnp.dot(value_gradient_batch, w_value.T, preferred_element_type=jnp.float32)
    )
    g_gain_one = jnp.sum(d_hidden_one * normed_one, axis=0)
    dn_one = d_hidden_one * gain_one.astype(jnp.float32)
    d_tokens = (
        d_mixed
        + inverse_one
        * (dn_one - normed_one * jnp.mean(dn_one * normed_one, axis=-1, keepdims=True))
    ).astype(jnp.bfloat16)
    local_grads = jnp.concatenate(
        [
            g_query.reshape(-1),
            g_key.reshape(-1),
            g_value.reshape(-1),
            g_out.reshape(-1),
            g_gate.reshape(-1),
            g_up.reshape(-1),
            g_down.reshape(-1),
            g_gain_one,
            g_gain_two,
        ]
    )
    whole_sum = lax.psum(local_grads, ("wide", "narrow"))
    summed = lax.dynamic_slice_in_dim(whole_sum, narrow_rank * shard_len, shard_len)
    token_total = token_rows * narrow_size * lax.axis_size("wide")
    gradient = summed * (1.0 / math.sqrt(token_total))
    new_first = beta_one * first_moment + (1.0 - beta_one) * gradient
    new_second = beta_two * second_moment + (1.0 - beta_two) * gradient * gradient
    first_hat = new_first / (1.0 - beta_one**STEP)
    second_hat = new_second / (1.0 - beta_two**STEP)
    entry_index = narrow_rank * shard_len + jnp.arange(shard_len, dtype=jnp.int32)
    decay = jnp.where(entry_index < NPARAM - 2 * MODEL_WIDTH, decay_rate, 0.0)
    new_master = master - learn_rate * (
        first_hat / (jnp.sqrt(second_hat) + adam_eps) + decay * master
    )
    return (output, d_tokens, gradient, new_master, new_first, new_second)


def solution(mesh):
    in_specs = (
        P(("wide", "narrow"), None),
        P(("wide", "narrow"), None),
        P("wide", None),
        P("narrow"),
        P("narrow"),
        P("narrow"),
    )
    out_specs = (
        P(("wide", "narrow"), None),
        P(("wide", "narrow"), None),
        P("narrow"),
        P("narrow"),
        P("narrow"),
        P("narrow"),
    )
    return jax.shard_map(body, mesh=mesh, in_specs=in_specs, out_specs=out_specs, check_vma=False)
```

```python
import math

import jax
import jax.numpy as jnp
from jax import lax
from jax.experimental import pallas as pl
from jax.experimental.pallas import tpu as pltpu
from jax.sharding import PartitionSpec as P

MODEL_WIDTH = 512
QUERY_HEADS = 15
KEYVAL_HEADS = 5
HEAD_SIZE = 64
FEEDFWD_UNITS = 1280
STEP = 4
NPARAM = 3277824


eps_norm = 1e-05
rope_base = 100000.0
beta_one = 0.9
beta_two = 0.95
learn_rate = 0.03
decay_rate = 0.1
adam_eps = 1e-08
masked_logits = -1e30


def unpack(flat):
    arrangement_list = [
        (MODEL_WIDTH, QUERY_HEADS * HEAD_SIZE),
        (MODEL_WIDTH, KEYVAL_HEADS * HEAD_SIZE),
        (MODEL_WIDTH, KEYVAL_HEADS * HEAD_SIZE),
        (QUERY_HEADS * HEAD_SIZE, MODEL_WIDTH),
        (MODEL_WIDTH, FEEDFWD_UNITS),
        (MODEL_WIDTH, FEEDFWD_UNITS),
        (FEEDFWD_UNITS, MODEL_WIDTH),
        (MODEL_WIDTH,),
        (MODEL_WIDTH,),
    ]
    pieces = []
    offset = 0
    for layout in arrangement_list:
        length = math.prod(layout)
        pieces.append(flat[offset : offset + length].reshape(layout))
        offset = offset + length
    return pieces


def place_tokens(indices, lengths_row):
    seq_ends = jnp.cumsum(lengths_row)
    seq_starts = seq_ends - lengths_row
    member = (indices[:, None] >= seq_starts[None, :]) & (indices[:, None] < seq_ends[None, :])
    numbers = jnp.arange(lengths_row.shape[0], dtype=jnp.int32)
    segment = jnp.sum(jnp.where(member, numbers[None, :], 0), axis=1)
    token_position = indices - jnp.sum(jnp.where(member, seq_starts[None, :], 0), axis=1)
    return (segment, token_position)


def normalize(values):
    inverse_rms = lax.rsqrt(jnp.mean(values * values, axis=-1, keepdims=True) + eps_norm)
    return (values * inverse_rms, inverse_rms)


def apply_rotary(values, token_position, head_count, turn_sign):
    half_dim = HEAD_SIZE // 2
    inverse = rope_base ** (-2.0 * jnp.arange(half_dim, dtype=jnp.float32) / HEAD_SIZE)
    angles = token_position.astype(jnp.float32)[:, None] * inverse[None, :]
    cosine = jnp.cos(angles)[:, None, :]
    sine = turn_sign * jnp.sin(angles)[:, None, :]
    shaped = values.reshape(values.shape[0], head_count, HEAD_SIZE)
    first_half = shaped[:, :, :half_dim]
    second_half = shaped[:, :, half_dim:]
    turned = jnp.concatenate(
        [first_half * cosine - second_half * sine, second_half * cosine + first_half * sine],
        axis=-1,
    )
    return turned.reshape(values.shape)


def gather_kernel(src_ref, out_ref, send_sems, recv_sems):
    narrow = lax.axis_index("narrow")
    wide = lax.axis_index("wide")
    z_lo = narrow // 2
    core = narrow % 2
    z_hi = (wide // 4) % 2
    flipped = wide + 4 - 8 * z_hi
    half = src_ref.shape[0] // 2
    sibling = (wide, z_lo * 2 + 1 - core)
    across = [(wide, (1 - z_lo) * 2 + c) for c in (0, 1)]
    around = [(flipped, (1 - z_lo) * 2 + c) for c in (0, 1)]
    barrier = pltpu.get_barrier_semaphore()
    for peer in [sibling] + across + around:
        pl.semaphore_signal(barrier, 1, device_id=peer, device_id_type=pl.DeviceIdType.MESH)
    pl.semaphore_wait(barrier, 5)
    sends = [(sibling, 0), (sibling, 1)] + [(p, 0) for p in across] + [(p, 1) for p in around]
    copies = []
    for number, (peer, part) in enumerate(sends):
        rows = pl.ds(part * half, half)
        copy = pltpu.make_async_remote_copy(
            src_ref=src_ref.at[rows],
            dst_ref=out_ref.at[narrow, rows],
            send_sem=send_sems.at[number],
            recv_sem=recv_sems.at[narrow, part],
            device_id=peer,
            device_id_type=pl.DeviceIdType.MESH,
        )
        copy.start()
        copies.append(copy)
    out_ref[narrow] = src_ref[...]
    for copy in copies:
        copy.wait_send()
    for step in range(1, 4):
        owner = lax.rem(narrow + step, 4)
        for part in (0, 1):
            rows = pl.ds(part * half, half)
            pltpu.make_async_remote_copy(
                src_ref=src_ref.at[rows],
                dst_ref=out_ref.at[owner, rows],
                send_sem=send_sems.at[0],
                recv_sem=recv_sems.at[owner, part],
                device_id=sibling,
                device_id_type=pl.DeviceIdType.MESH,
            ).wait_recv()


def gather_replica(shard_rows):
    count, width = shard_rows.shape
    return pl.pallas_call(
        gather_kernel,
        out_shape=jax.ShapeDtypeStruct((4, count, width), shard_rows.dtype),
        in_specs=[pl.BlockSpec(memory_space=pltpu.VMEM)],
        out_specs=pl.BlockSpec(memory_space=pltpu.VMEM),
        scratch_shapes=[pltpu.SemaphoreType.DMA((6,)), pltpu.SemaphoreType.DMA((4, 2))],
        compiler_params=pltpu.CompilerParams(collective_id=0, has_side_effects=True),
    )(shard_rows)


def keep_carry(carry):
    return carry


def body(tokens, cotangent, lengths, master, first_moment, second_moment):
    token_rows = tokens.shape[0]
    narrow_size = lax.axis_size("narrow")
    group_rows = token_rows * narrow_size
    narrow_rank = lax.axis_index("narrow")
    group_width = QUERY_HEADS // KEYVAL_HEADS
    score_scale = HEAD_SIZE ** (-0.5)
    shard_len = master.shape[0]
    shard_rows = shard_len // 128
    padded_rows = -(-shard_rows // 32) * 32
    replica = gather_replica(
        jnp.pad(
            master.astype(jnp.bfloat16).reshape(shard_rows, 128),
            ((0, padded_rows - shard_rows), (0, 0)),
        )
    )[:, :shard_rows].reshape(-1)
    w_query, w_key, w_value, w_out, w_gate, w_up, w_down, gain_one, gain_two = unpack(replica)
    lengths_row = lengths[0]
    local_index = narrow_rank * token_rows + jnp.arange(token_rows, dtype=jnp.int32)
    segment, token_position = place_tokens(local_index, lengths_row)
    group_index = jnp.arange(group_rows, dtype=jnp.int32)
    key_segment = place_tokens(group_index, lengths_row)[0]
    first_start = local_index[0] - token_position[0]
    last_index = local_index[token_rows - 1]
    range_rows = min(512, group_rows)
    span_starts = list(range(0, group_rows, range_rows))
    resid = tokens.astype(jnp.float32)
    normed_one, inverse_one = normalize(resid)
    hidden_one = (normed_one * gain_one.astype(jnp.float32)).astype(jnp.bfloat16)
    query = jnp.dot(hidden_one, w_query, preferred_element_type=jnp.float32)
    key_projection = jnp.dot(hidden_one, w_key, preferred_element_type=jnp.float32)
    value_proj = jnp.dot(hidden_one, w_value, preferred_element_type=jnp.float32)
    query_batch = apply_rotary(query, token_position, QUERY_HEADS, 1.0).astype(jnp.bfloat16)
    key_batch = apply_rotary(key_projection, token_position, KEYVAL_HEADS, 1.0).astype(jnp.bfloat16)
    value_batch = value_proj.astype(jnp.bfloat16)
    kv_width = KEYVAL_HEADS * HEAD_SIZE
    kv_all = lax.all_gather(
        jnp.concatenate([key_batch, value_batch], axis=1), "narrow", axis=0, tiled=True
    )
    key_all, value_all = kv_all[:, :kv_width], kv_all[:, kv_width:]
    query_tensor_split = query_batch.reshape(token_rows, KEYVAL_HEADS, group_width, HEAD_SIZE)

    def span_setup(span_start, key_source, value_source):
        key_tensor_split = lax.slice_in_dim(
            key_source, span_start, span_start + range_rows
        ).reshape(range_rows, KEYVAL_HEADS, HEAD_SIZE)
        value_tensor_split = lax.slice_in_dim(
            value_source, span_start, span_start + range_rows
        ).reshape(range_rows, KEYVAL_HEADS, HEAD_SIZE)
        span_segment = lax.slice_in_dim(key_segment, span_start, span_start + range_rows)
        span_index = lax.slice_in_dim(group_index, span_start, span_start + range_rows)
        allowed = (segment[:, None] == span_segment[None, :]) & (
            span_index[None, :] <= local_index[:, None]
        )
        needed = (span_start <= last_index) & (span_start + range_rows - 1 >= first_start)
        return (key_tensor_split, value_tensor_split, allowed[None, None], needed)

    running_maximum = jnp.full((KEYVAL_HEADS, group_width, token_rows), masked_logits, jnp.float32)
    running_denominator = jnp.zeros((KEYVAL_HEADS, group_width, token_rows), jnp.float32)
    for span_start in span_starts:
        key_tensor_split, value_tensor_split, allowed, needed = span_setup(
            span_start, key_all, value_all
        )

        def extend(carry):
            old_top, old_total = carry
            scores = (
                jnp.einsum(
                    "qgrd,kgd->grqk",
                    query_tensor_split,
                    key_tensor_split,
                    preferred_element_type=jnp.float32,
                )
                * score_scale
            )
            new_top = jnp.maximum(
                old_top, jnp.max(jnp.where(allowed, scores, masked_logits), axis=-1)
            )
            span_sum = jnp.sum(
                jnp.where(allowed, jnp.exp(scores - new_top[..., None]), 0.0), axis=-1
            )
            return (new_top, old_total * jnp.exp(old_top - new_top) + span_sum)

        running_maximum, running_denominator = lax.cond(
            needed, extend, keep_carry, (running_maximum, running_denominator)
        )
    lse = running_maximum + jnp.log(running_denominator)
    running_total = jnp.zeros((token_rows, KEYVAL_HEADS, group_width, HEAD_SIZE), jnp.float32)
    for span_start in span_starts:
        key_tensor_split, value_tensor_split, allowed, needed = span_setup(
            span_start, key_all, value_all
        )

        def weigh_values(carry):
            scores = (
                jnp.einsum(
                    "qgrd,kgd->grqk",
                    query_tensor_split,
                    key_tensor_split,
                    preferred_element_type=jnp.float32,
                )
                * score_scale
            )
            probs_b = jnp.where(allowed, jnp.exp(scores - lse[..., None]), 0.0).astype(jnp.bfloat16)
            return carry + jnp.einsum(
                "grqk,kgd->qgrd", probs_b, value_tensor_split, preferred_element_type=jnp.float32
            )

        running_total = lax.cond(needed, weigh_values, keep_carry, running_total)
    attention_output = running_total.reshape(token_rows, QUERY_HEADS * HEAD_SIZE).astype(
        jnp.bfloat16
    )
    mixed = resid + jnp.dot(attention_output, w_out, preferred_element_type=jnp.float32)
    normed_two, inverse_two = normalize(mixed)
    hidden_two = (normed_two * gain_two.astype(jnp.float32)).astype(jnp.bfloat16)
    gate = jnp.dot(hidden_two, w_gate, preferred_element_type=jnp.float32)
    upward = jnp.dot(hidden_two, w_up, preferred_element_type=jnp.float32)
    sigma = jax.nn.sigmoid(gate)
    activated = (gate * sigma * upward).astype(jnp.bfloat16)
    output = (mixed + jnp.dot(activated, w_down, preferred_element_type=jnp.float32)).astype(
        jnp.bfloat16
    )
    d_act = jnp.dot(cotangent, w_down.T, preferred_element_type=jnp.float32)
    g_down = jnp.dot(activated.T, cotangent, preferred_element_type=jnp.float32)
    d_gate = (d_act * upward * sigma * (1.0 + gate * (1.0 - sigma))).astype(jnp.bfloat16)
    d_up = (d_act * gate * sigma).astype(jnp.bfloat16)
    g_gate = jnp.dot(hidden_two.T, d_gate, preferred_element_type=jnp.float32)
    g_up = jnp.dot(hidden_two.T, d_up, preferred_element_type=jnp.float32)
    d_hidden_two = jnp.dot(d_gate, w_gate.T, preferred_element_type=jnp.float32) + jnp.dot(
        d_up, w_up.T, preferred_element_type=jnp.float32
    )
    g_gain_two = jnp.sum(d_hidden_two * normed_two, axis=0)
    dn_two = d_hidden_two * gain_two.astype(jnp.float32)
    d_mixed = cotangent.astype(jnp.float32) + inverse_two * (
        dn_two - normed_two * jnp.mean(dn_two * normed_two, axis=-1, keepdims=True)
    )
    d_mixed_b = d_mixed.astype(jnp.bfloat16)
    g_out = jnp.dot(attention_output.T, d_mixed_b, preferred_element_type=jnp.float32)
    attention_output_gradient = jnp.dot(
        d_mixed_b, w_out.T, preferred_element_type=jnp.float32
    ).astype(jnp.bfloat16)
    split_gradient = attention_output_gradient.reshape(
        token_rows, KEYVAL_HEADS, group_width, HEAD_SIZE
    )
    attention_output_split = attention_output.reshape(
        token_rows, KEYVAL_HEADS, group_width, HEAD_SIZE
    )
    softmax_correction = jnp.sum(
        split_gradient.astype(jnp.float32) * attention_output_split.astype(jnp.float32), axis=-1
    ).transpose(1, 2, 0)
    key_back, value_back = (key_all, value_all)
    query_gradient_running = jnp.zeros(
        (token_rows, KEYVAL_HEADS, group_width, HEAD_SIZE), jnp.float32
    )
    key_contributions = []
    value_contributions = []
    for span_start in span_starts:
        key_tensor_split, value_tensor_split, allowed, needed = span_setup(
            span_start, key_back, value_back
        )

        def back_span(carry):
            scores = (
                jnp.einsum(
                    "qgrd,kgd->grqk",
                    query_tensor_split,
                    key_tensor_split,
                    preferred_element_type=jnp.float32,
                )
                * score_scale
            )
            probs = jnp.where(allowed, jnp.exp(scores - lse[..., None]), 0.0)
            probs_b = probs.astype(jnp.bfloat16)
            value_gradient_range = jnp.einsum(
                "pozf,zpom->fpm", probs_b, split_gradient, preferred_element_type=jnp.float32
            )
            d_probs = jnp.einsum(
                "qgrd,kgd->grqk",
                split_gradient,
                value_tensor_split,
                preferred_element_type=jnp.float32,
            )
            score_gradient = (
                probs * (d_probs - softmax_correction[..., None]) * score_scale
            ).astype(jnp.bfloat16)
            new_acc = carry + jnp.einsum(
                "grqk,kgd->qgrd",
                score_gradient,
                key_tensor_split,
                preferred_element_type=jnp.float32,
            )
            key_gradient_range = jnp.einsum(
                "pozf,zpom->fpm",
                score_gradient,
                query_tensor_split,
                preferred_element_type=jnp.float32,
            )
            return (new_acc, key_gradient_range, value_gradient_range)

        def skip_span(carry):
            blank_range = jnp.zeros((range_rows, KEYVAL_HEADS, HEAD_SIZE), jnp.float32)
            return (carry, blank_range, blank_range)

        query_gradient_running, key_gradient_range, value_gradient_range = lax.cond(
            needed, back_span, skip_span, query_gradient_running
        )
        key_contributions.append(key_gradient_range.reshape(range_rows, KEYVAL_HEADS * HEAD_SIZE))
        value_contributions.append(
            value_gradient_range.reshape(range_rows, KEYVAL_HEADS * HEAD_SIZE)
        )
    key_sum_in = jnp.concatenate(key_contributions, axis=0)
    value_sum_in = jnp.concatenate(value_contributions, axis=0)
    kv_sum_in = jnp.concatenate([key_sum_in, value_sum_in], axis=1).reshape(
        narrow_size, token_rows, 2 * kv_width
    )
    kv_grad = kv_sum_in[narrow_rank]
    for shift in range(1, narrow_size):
        sender_block = kv_sum_in[lax.rem(narrow_rank + narrow_size - shift, narrow_size)]
        kv_grad = kv_grad + lax.ppermute(
            sender_block,
            "narrow",
            [(source, source - shift) for source in range(shift, narrow_size)],
        )
    key_gradient, value_gradient = kv_grad[:, :kv_width], kv_grad[:, kv_width:]
    d_query = query_gradient_running.reshape(token_rows, QUERY_HEADS * HEAD_SIZE)
    d_query_b = apply_rotary(d_query, token_position, QUERY_HEADS, -1.0).astype(jnp.bfloat16)
    key_gradient_batch = apply_rotary(key_gradient, token_position, KEYVAL_HEADS, -1.0).astype(
        jnp.bfloat16
    )
    value_gradient_batch = value_gradient.astype(jnp.bfloat16)
    g_query = jnp.dot(hidden_one.T, d_query_b, preferred_element_type=jnp.float32)
    g_key = jnp.dot(hidden_one.T, key_gradient_batch, preferred_element_type=jnp.float32)
    g_value = jnp.dot(hidden_one.T, value_gradient_batch, preferred_element_type=jnp.float32)
    d_hidden_one = (
        jnp.dot(d_query_b, w_query.T, preferred_element_type=jnp.float32)
        + jnp.dot(key_gradient_batch, w_key.T, preferred_element_type=jnp.float32)
        + jnp.dot(value_gradient_batch, w_value.T, preferred_element_type=jnp.float32)
    )
    g_gain_one = jnp.sum(d_hidden_one * normed_one, axis=0)
    dn_one = d_hidden_one * gain_one.astype(jnp.float32)
    d_tokens = (
        d_mixed
        + inverse_one
        * (dn_one - normed_one * jnp.mean(dn_one * normed_one, axis=-1, keepdims=True))
    ).astype(jnp.bfloat16)
    local_grads = jnp.concatenate(
        [
            g_query.reshape(-1),
            g_key.reshape(-1),
            g_value.reshape(-1),
            g_out.reshape(-1),
            g_gate.reshape(-1),
            g_up.reshape(-1),
            g_down.reshape(-1),
            g_gain_one,
            g_gain_two,
        ]
    )
    whole_sum = lax.psum(local_grads, ("wide", "narrow"))
    summed = lax.dynamic_slice_in_dim(whole_sum, narrow_rank * shard_len, shard_len)
    token_total = token_rows * narrow_size * lax.axis_size("wide")
    gradient = summed * (1.0 / math.sqrt(token_total))
    new_first = beta_one * first_moment + (1.0 - beta_one) * gradient
    new_second = beta_two * second_moment + (1.0 - beta_two) * gradient * gradient
    first_hat = new_first / (1.0 - beta_one**STEP)
    second_hat = new_second / (1.0 - beta_two**STEP)
    entry_index = narrow_rank * shard_len + jnp.arange(shard_len, dtype=jnp.int32)
    decay = jnp.where(entry_index < NPARAM - 2 * MODEL_WIDTH, decay_rate, 0.0)
    new_master = master - learn_rate * (
        first_hat / (jnp.sqrt(second_hat) + adam_eps) + decay * master
    )
    return (output, d_tokens, gradient, new_master, new_first, new_second)


def solution(mesh):
    in_specs = (
        P(("wide", "narrow"), None),
        P(("wide", "narrow"), None),
        P("wide", None),
        P("narrow"),
        P("narrow"),
        P("narrow"),
    )
    out_specs = (
        P(("wide", "narrow"), None),
        P(("wide", "narrow"), None),
        P("narrow"),
        P("narrow"),
        P("narrow"),
        P("narrow"),
    )
    return jax.shard_map(body, mesh=mesh, in_specs=in_specs, out_specs=out_specs, check_vma=False)
```

```python
import math

import jax
import jax.numpy as jnp
from jax import lax
from jax.experimental import pallas as pl
from jax.experimental.pallas import tpu as pltpu
from jax.sharding import PartitionSpec as P

MODEL_WIDTH = 512
QUERY_HEADS = 15
KEYVAL_HEADS = 5
HEAD_SIZE = 64
FEEDFWD_UNITS = 1280
STEP = 4
NPARAM = 3277824


eps_norm = 1e-05
rope_base = 100000.0
beta_one = 0.9
beta_two = 0.95
learn_rate = 0.03
decay_rate = 0.1
adam_eps = 1e-08
masked_logits = -1e30


def unpack(flat):
    arrangement_list = [
        (MODEL_WIDTH, QUERY_HEADS * HEAD_SIZE),
        (MODEL_WIDTH, KEYVAL_HEADS * HEAD_SIZE),
        (MODEL_WIDTH, KEYVAL_HEADS * HEAD_SIZE),
        (QUERY_HEADS * HEAD_SIZE, MODEL_WIDTH),
        (MODEL_WIDTH, FEEDFWD_UNITS),
        (MODEL_WIDTH, FEEDFWD_UNITS),
        (FEEDFWD_UNITS, MODEL_WIDTH),
        (MODEL_WIDTH,),
        (MODEL_WIDTH,),
    ]
    pieces = []
    offset = 0
    for layout in arrangement_list:
        length = math.prod(layout)
        pieces.append(flat[offset : offset + length].reshape(layout))
        offset = offset + length
    return pieces


def place_tokens(indices, lengths_row):
    seq_ends = jnp.cumsum(lengths_row)
    seq_starts = seq_ends - lengths_row
    member = (indices[:, None] >= seq_starts[None, :]) & (indices[:, None] < seq_ends[None, :])
    numbers = jnp.arange(lengths_row.shape[0], dtype=jnp.int32)
    segment = jnp.sum(jnp.where(member, numbers[None, :], 0), axis=1)
    token_position = indices - jnp.sum(jnp.where(member, seq_starts[None, :], 0), axis=1)
    return (segment, token_position)


def normalize(values):
    inverse_rms = lax.rsqrt(jnp.mean(values * values, axis=-1, keepdims=True) + eps_norm)
    return (values * inverse_rms, inverse_rms)


def apply_rotary(values, token_position, head_count, turn_sign):
    half_dim = HEAD_SIZE // 2
    inverse = rope_base ** (-2.0 * jnp.arange(half_dim, dtype=jnp.float32) / HEAD_SIZE)
    angles = token_position.astype(jnp.float32)[:, None] * inverse[None, :]
    cosine = jnp.cos(angles)[:, None, :]
    sine = turn_sign * jnp.sin(angles)[:, None, :]
    shaped = values.reshape(values.shape[0], head_count, HEAD_SIZE)
    first_half = shaped[:, :, :half_dim]
    second_half = shaped[:, :, half_dim:]
    turned = jnp.concatenate(
        [first_half * cosine - second_half * sine, second_half * cosine + first_half * sine],
        axis=-1,
    )
    return turned.reshape(values.shape)


def gather_kernel(src_ref, out_ref, send_sems, recv_sems):
    narrow = lax.axis_index("narrow")
    wide = lax.axis_index("wide")
    z_lo = narrow // 2
    core = narrow % 2
    z_hi = (wide // 4) % 2
    flipped = wide + 4 - 8 * z_hi
    split = (src_ref.shape[0] // 32) * 16
    halves = [pl.ds(0, split), pl.ds(split, src_ref.shape[0] - split)]
    sibling = (wide, z_lo * 2 + 1 - core)
    across = [(wide, (1 - z_lo) * 2 + c) for c in (0, 1)]
    around = [(flipped, (1 - z_lo) * 2 + c) for c in (0, 1)]
    barrier = pltpu.get_barrier_semaphore()
    for peer in [sibling] + across + around:
        pl.semaphore_signal(barrier, 1, device_id=peer, device_id_type=pl.DeviceIdType.MESH)
    pl.semaphore_wait(barrier, 5)
    sends = [(sibling, 0), (sibling, 1)] + [(p, 0) for p in across] + [(p, 1) for p in around]
    copies = []
    for number, (peer, part) in enumerate(sends):
        rows = halves[part]
        copy = pltpu.make_async_remote_copy(
            src_ref=src_ref.at[rows],
            dst_ref=out_ref.at[narrow, rows],
            send_sem=send_sems.at[number],
            recv_sem=recv_sems.at[narrow, part],
            device_id=peer,
            device_id_type=pl.DeviceIdType.MESH,
        )
        copy.start()
        copies.append(copy)
    out_ref[narrow] = src_ref[...]
    for copy in copies:
        copy.wait_send()
    for step in range(1, 4):
        owner = lax.rem(narrow + step, 4)
        for part in (0, 1):
            rows = halves[part]
            pltpu.make_async_remote_copy(
                src_ref=src_ref.at[rows],
                dst_ref=out_ref.at[owner, rows],
                send_sem=send_sems.at[0],
                recv_sem=recv_sems.at[owner, part],
                device_id=sibling,
                device_id_type=pl.DeviceIdType.MESH,
            ).wait_recv()


def gather_replica(shard_rows):
    count, width = shard_rows.shape
    return pl.pallas_call(
        gather_kernel,
        out_shape=jax.ShapeDtypeStruct((4, count, width), shard_rows.dtype),
        in_specs=[pl.BlockSpec(memory_space=pltpu.VMEM)],
        out_specs=pl.BlockSpec(memory_space=pltpu.VMEM),
        scratch_shapes=[pltpu.SemaphoreType.DMA((6,)), pltpu.SemaphoreType.DMA((4, 2))],
        compiler_params=pltpu.CompilerParams(collective_id=0, has_side_effects=True),
    )(shard_rows)


def keep_carry(carry):
    return carry


def body(tokens, cotangent, lengths, master, first_moment, second_moment):
    token_rows = tokens.shape[0]
    narrow_size = lax.axis_size("narrow")
    group_rows = token_rows * narrow_size
    narrow_rank = lax.axis_index("narrow")
    group_width = QUERY_HEADS // KEYVAL_HEADS
    score_scale = HEAD_SIZE ** (-0.5)
    shard_len = master.shape[0]
    replica = gather_replica(master.astype(jnp.bfloat16).reshape(shard_len // 128, 128)).reshape(-1)
    w_query, w_key, w_value, w_out, w_gate, w_up, w_down, gain_one, gain_two = unpack(replica)
    lengths_row = lengths[0]
    local_index = narrow_rank * token_rows + jnp.arange(token_rows, dtype=jnp.int32)
    segment, token_position = place_tokens(local_index, lengths_row)
    group_index = jnp.arange(group_rows, dtype=jnp.int32)
    key_segment = place_tokens(group_index, lengths_row)[0]
    first_start = local_index[0] - token_position[0]
    last_index = local_index[token_rows - 1]
    range_rows = token_rows
    span_starts = list(range(0, group_rows, range_rows))
    resid = tokens.astype(jnp.float32)
    normed_one, inverse_one = normalize(resid)
    hidden_one = (normed_one * gain_one.astype(jnp.float32)).astype(jnp.bfloat16)
    query = jnp.dot(hidden_one, w_query, preferred_element_type=jnp.float32)
    key_projection = jnp.dot(hidden_one, w_key, preferred_element_type=jnp.float32)
    value_proj = jnp.dot(hidden_one, w_value, preferred_element_type=jnp.float32)
    query_batch = apply_rotary(query, token_position, QUERY_HEADS, 1.0).astype(jnp.bfloat16)
    key_batch = apply_rotary(key_projection, token_position, KEYVAL_HEADS, 1.0).astype(jnp.bfloat16)
    value_batch = value_proj.astype(jnp.bfloat16)
    kv_width = KEYVAL_HEADS * HEAD_SIZE
    kv_all = lax.all_gather(
        jnp.concatenate([key_batch, value_batch], axis=1), "narrow", axis=0, tiled=True
    )
    key_all, value_all = kv_all[:, :kv_width], kv_all[:, kv_width:]
    query_tensor_split = query_batch.reshape(token_rows, KEYVAL_HEADS, group_width, HEAD_SIZE)

    def span_setup(span_start, key_source, value_source):
        key_tensor_split = lax.slice_in_dim(
            key_source, span_start, span_start + range_rows
        ).reshape(range_rows, KEYVAL_HEADS, HEAD_SIZE)
        value_tensor_split = lax.slice_in_dim(
            value_source, span_start, span_start + range_rows
        ).reshape(range_rows, KEYVAL_HEADS, HEAD_SIZE)
        span_segment = lax.slice_in_dim(key_segment, span_start, span_start + range_rows)
        span_index = lax.slice_in_dim(group_index, span_start, span_start + range_rows)
        allowed = (segment[:, None] == span_segment[None, :]) & (
            span_index[None, :] <= local_index[:, None]
        )
        needed = (span_start <= last_index) & (span_start + range_rows - 1 >= first_start)
        return (key_tensor_split, value_tensor_split, allowed[None, None], needed)

    running_maximum = jnp.full((KEYVAL_HEADS, group_width, token_rows), masked_logits, jnp.float32)
    running_denominator = jnp.zeros((KEYVAL_HEADS, group_width, token_rows), jnp.float32)
    for span_start in span_starts:
        key_tensor_split, value_tensor_split, allowed, needed = span_setup(
            span_start, key_all, value_all
        )

        def extend(carry):
            old_top, old_total = carry
            scores = (
                jnp.einsum(
                    "qgrd,kgd->grqk",
                    query_tensor_split,
                    key_tensor_split,
                    preferred_element_type=jnp.float32,
                )
                * score_scale
            )
            new_top = jnp.maximum(
                old_top, jnp.max(jnp.where(allowed, scores, masked_logits), axis=-1)
            )
            span_sum = jnp.sum(
                jnp.where(allowed, jnp.exp(scores - new_top[..., None]), 0.0), axis=-1
            )
            return (new_top, old_total * jnp.exp(old_top - new_top) + span_sum)

        running_maximum, running_denominator = lax.cond(
            needed, extend, keep_carry, (running_maximum, running_denominator)
        )
    lse = running_maximum + jnp.log(running_denominator)
    running_total = jnp.zeros((token_rows, KEYVAL_HEADS, group_width, HEAD_SIZE), jnp.float32)
    for span_start in span_starts:
        key_tensor_split, value_tensor_split, allowed, needed = span_setup(
            span_start, key_all, value_all
        )

        def weigh_values(carry):
            scores = (
                jnp.einsum(
                    "qgrd,kgd->grqk",
                    query_tensor_split,
                    key_tensor_split,
                    preferred_element_type=jnp.float32,
                )
                * score_scale
            )
            probs_b = jnp.where(allowed, jnp.exp(scores - lse[..., None]), 0.0).astype(jnp.bfloat16)
            return carry + jnp.einsum(
                "grqk,kgd->qgrd", probs_b, value_tensor_split, preferred_element_type=jnp.float32
            )

        running_total = lax.cond(needed, weigh_values, keep_carry, running_total)
    attention_output = running_total.reshape(token_rows, QUERY_HEADS * HEAD_SIZE).astype(
        jnp.bfloat16
    )
    mixed = resid + jnp.dot(attention_output, w_out, preferred_element_type=jnp.float32)
    normed_two, inverse_two = normalize(mixed)
    hidden_two = (normed_two * gain_two.astype(jnp.float32)).astype(jnp.bfloat16)
    gate = jnp.dot(hidden_two, w_gate, preferred_element_type=jnp.float32)
    upward = jnp.dot(hidden_two, w_up, preferred_element_type=jnp.float32)
    sigma = jax.nn.sigmoid(gate)
    activated = (gate * sigma * upward).astype(jnp.bfloat16)
    output = (mixed + jnp.dot(activated, w_down, preferred_element_type=jnp.float32)).astype(
        jnp.bfloat16
    )
    d_act = jnp.dot(cotangent, w_down.T, preferred_element_type=jnp.float32)
    g_down = jnp.dot(activated.T, cotangent, preferred_element_type=jnp.float32)
    d_gate = (d_act * upward * sigma * (1.0 + gate * (1.0 - sigma))).astype(jnp.bfloat16)
    d_up = (d_act * gate * sigma).astype(jnp.bfloat16)
    g_gate = jnp.dot(hidden_two.T, d_gate, preferred_element_type=jnp.float32)
    g_up = jnp.dot(hidden_two.T, d_up, preferred_element_type=jnp.float32)
    d_hidden_two = jnp.dot(d_gate, w_gate.T, preferred_element_type=jnp.float32) + jnp.dot(
        d_up, w_up.T, preferred_element_type=jnp.float32
    )
    g_gain_two = jnp.sum(d_hidden_two * normed_two, axis=0)
    dn_two = d_hidden_two * gain_two.astype(jnp.float32)
    d_mixed = cotangent.astype(jnp.float32) + inverse_two * (
        dn_two - normed_two * jnp.mean(dn_two * normed_two, axis=-1, keepdims=True)
    )
    d_mixed_b = d_mixed.astype(jnp.bfloat16)
    g_out = jnp.dot(attention_output.T, d_mixed_b, preferred_element_type=jnp.float32)
    attention_output_gradient = jnp.dot(
        d_mixed_b, w_out.T, preferred_element_type=jnp.float32
    ).astype(jnp.bfloat16)
    split_gradient = attention_output_gradient.reshape(
        token_rows, KEYVAL_HEADS, group_width, HEAD_SIZE
    )
    attention_output_split = attention_output.reshape(
        token_rows, KEYVAL_HEADS, group_width, HEAD_SIZE
    )
    softmax_correction = jnp.sum(
        split_gradient.astype(jnp.float32) * attention_output_split.astype(jnp.float32), axis=-1
    ).transpose(1, 2, 0)
    key_back, value_back = (key_all, value_all)
    query_gradient_running = jnp.zeros(
        (token_rows, KEYVAL_HEADS, group_width, HEAD_SIZE), jnp.float32
    )
    key_contributions = []
    value_contributions = []
    for span_start in span_starts:
        key_tensor_split, value_tensor_split, allowed, needed = span_setup(
            span_start, key_back, value_back
        )

        def back_span(carry):
            scores = (
                jnp.einsum(
                    "qgrd,kgd->grqk",
                    query_tensor_split,
                    key_tensor_split,
                    preferred_element_type=jnp.float32,
                )
                * score_scale
            )
            probs = jnp.where(allowed, jnp.exp(scores - lse[..., None]), 0.0)
            probs_b = probs.astype(jnp.bfloat16)
            value_gradient_range = jnp.einsum(
                "pozf,zpom->fpm", probs_b, split_gradient, preferred_element_type=jnp.float32
            )
            d_probs = jnp.einsum(
                "qgrd,kgd->grqk",
                split_gradient,
                value_tensor_split,
                preferred_element_type=jnp.float32,
            )
            score_gradient = (
                probs * (d_probs - softmax_correction[..., None]) * score_scale
            ).astype(jnp.bfloat16)
            new_acc = carry + jnp.einsum(
                "grqk,kgd->qgrd",
                score_gradient,
                key_tensor_split,
                preferred_element_type=jnp.float32,
            )
            key_gradient_range = jnp.einsum(
                "pozf,zpom->fpm",
                score_gradient,
                query_tensor_split,
                preferred_element_type=jnp.float32,
            )
            return (new_acc, key_gradient_range, value_gradient_range)

        def skip_span(carry):
            blank_range = jnp.zeros((range_rows, KEYVAL_HEADS, HEAD_SIZE), jnp.float32)
            return (carry, blank_range, blank_range)

        query_gradient_running, key_gradient_range, value_gradient_range = lax.cond(
            needed, back_span, skip_span, query_gradient_running
        )
        key_contributions.append(key_gradient_range.reshape(range_rows, KEYVAL_HEADS * HEAD_SIZE))
        value_contributions.append(
            value_gradient_range.reshape(range_rows, KEYVAL_HEADS * HEAD_SIZE)
        )
    kv_sum_in = jnp.stack(
        [jnp.concatenate(pair, axis=1) for pair in zip(key_contributions, value_contributions)]
    )
    kv_grad = kv_sum_in[narrow_rank]
    for shift in range(1, narrow_size):
        sender_block = kv_sum_in[lax.rem(narrow_rank + narrow_size - shift, narrow_size)]
        kv_grad = kv_grad + lax.ppermute(
            sender_block,
            "narrow",
            [(source, source - shift) for source in range(shift, narrow_size)],
        )
    key_gradient, value_gradient = kv_grad[:, :kv_width], kv_grad[:, kv_width:]
    d_query = query_gradient_running.reshape(token_rows, QUERY_HEADS * HEAD_SIZE)
    d_query_b = apply_rotary(d_query, token_position, QUERY_HEADS, -1.0).astype(jnp.bfloat16)
    key_gradient_batch = apply_rotary(key_gradient, token_position, KEYVAL_HEADS, -1.0).astype(
        jnp.bfloat16
    )
    value_gradient_batch = value_gradient.astype(jnp.bfloat16)
    g_query = jnp.dot(hidden_one.T, d_query_b, preferred_element_type=jnp.float32)
    g_key = jnp.dot(hidden_one.T, key_gradient_batch, preferred_element_type=jnp.float32)
    g_value = jnp.dot(hidden_one.T, value_gradient_batch, preferred_element_type=jnp.float32)
    d_hidden_one = (
        jnp.dot(d_query_b, w_query.T, preferred_element_type=jnp.float32)
        + jnp.dot(key_gradient_batch, w_key.T, preferred_element_type=jnp.float32)
        + jnp.dot(value_gradient_batch, w_value.T, preferred_element_type=jnp.float32)
    )
    g_gain_one = jnp.sum(d_hidden_one * normed_one, axis=0)
    dn_one = d_hidden_one * gain_one.astype(jnp.float32)
    d_tokens = (
        d_mixed
        + inverse_one
        * (dn_one - normed_one * jnp.mean(dn_one * normed_one, axis=-1, keepdims=True))
    ).astype(jnp.bfloat16)
    local_grads = jnp.concatenate(
        [
            g_query.reshape(-1),
            g_key.reshape(-1),
            g_value.reshape(-1),
            g_out.reshape(-1),
            g_gate.reshape(-1),
            g_up.reshape(-1),
            g_down.reshape(-1),
            g_gain_one,
            g_gain_two,
        ]
    )
    whole_sum = lax.psum(local_grads, ("wide", "narrow"))
    summed = lax.dynamic_slice_in_dim(whole_sum, narrow_rank * shard_len, shard_len)
    token_total = token_rows * narrow_size * lax.axis_size("wide")
    gradient = summed * (1.0 / math.sqrt(token_total))
    new_first = beta_one * first_moment + (1.0 - beta_one) * gradient
    new_second = beta_two * second_moment + (1.0 - beta_two) * gradient * gradient
    first_hat = new_first / (1.0 - beta_one**STEP)
    second_hat = new_second / (1.0 - beta_two**STEP)
    entry_index = narrow_rank * shard_len + jnp.arange(shard_len, dtype=jnp.int32)
    decay = jnp.where(entry_index < NPARAM - 2 * MODEL_WIDTH, decay_rate, 0.0)
    new_master = master - learn_rate * (
        first_hat / (jnp.sqrt(second_hat) + adam_eps) + decay * master
    )
    return (output, d_tokens, gradient, new_master, new_first, new_second)


def solution(mesh):
    in_specs = (
        P(("wide", "narrow"), None),
        P(("wide", "narrow"), None),
        P("wide", None),
        P("narrow"),
        P("narrow"),
        P("narrow"),
    )
    out_specs = (
        P(("wide", "narrow"), None),
        P(("wide", "narrow"), None),
        P("narrow"),
        P("narrow"),
        P("narrow"),
        P("narrow"),
    )
    return jax.shard_map(body, mesh=mesh, in_specs=in_specs, out_specs=out_specs, check_vma=False)
```

```python
import math

import jax
import jax.numpy as jnp
from jax import lax
from jax.experimental import pallas as pl
from jax.experimental.pallas import tpu as pltpu
from jax.sharding import PartitionSpec as P

MODEL_WIDTH = 512
QUERY_HEADS = 15
KEYVAL_HEADS = 5
HEAD_SIZE = 64
FEEDFWD_UNITS = 1280
STEP = 4
NPARAM = 3277824


eps_norm = 1e-05
rope_base = 100000.0
beta_one = 0.9
beta_two = 0.95
learn_rate = 0.03
decay_rate = 0.1
adam_eps = 1e-08
masked_logits = -1e30


def unpack(flat):
    arrangement_list = [
        (MODEL_WIDTH, QUERY_HEADS * HEAD_SIZE),
        (MODEL_WIDTH, KEYVAL_HEADS * HEAD_SIZE),
        (MODEL_WIDTH, KEYVAL_HEADS * HEAD_SIZE),
        (QUERY_HEADS * HEAD_SIZE, MODEL_WIDTH),
        (MODEL_WIDTH, FEEDFWD_UNITS),
        (MODEL_WIDTH, FEEDFWD_UNITS),
        (FEEDFWD_UNITS, MODEL_WIDTH),
        (MODEL_WIDTH,),
        (MODEL_WIDTH,),
    ]
    pieces = []
    offset = 0
    for layout in arrangement_list:
        length = math.prod(layout)
        pieces.append(flat[offset : offset + length].reshape(layout))
        offset = offset + length
    return pieces


def place_tokens(indices, lengths_row):
    seq_ends = jnp.cumsum(lengths_row)
    seq_starts = seq_ends - lengths_row
    member = (indices[:, None] >= seq_starts[None, :]) & (indices[:, None] < seq_ends[None, :])
    numbers = jnp.arange(lengths_row.shape[0], dtype=jnp.int32)
    segment = jnp.sum(jnp.where(member, numbers[None, :], 0), axis=1)
    token_position = indices - jnp.sum(jnp.where(member, seq_starts[None, :], 0), axis=1)
    return (segment, token_position)


def normalize(values):
    inverse_rms = lax.rsqrt(jnp.mean(values * values, axis=-1, keepdims=True) + eps_norm)
    return (values * inverse_rms, inverse_rms)


def apply_rotary(values, token_position, head_count, turn_sign):
    half_dim = HEAD_SIZE // 2
    inverse = rope_base ** (-2.0 * jnp.arange(half_dim, dtype=jnp.float32) / HEAD_SIZE)
    angles = token_position.astype(jnp.float32)[:, None] * inverse[None, :]
    cosine = jnp.cos(angles)[:, None, :]
    sine = turn_sign * jnp.sin(angles)[:, None, :]
    shaped = values.reshape(values.shape[0], head_count, HEAD_SIZE)
    first_half = shaped[:, :, :half_dim]
    second_half = shaped[:, :, half_dim:]
    turned = jnp.concatenate(
        [first_half * cosine - second_half * sine, second_half * cosine + first_half * sine],
        axis=-1,
    )
    return turned.reshape(values.shape)


def gather_kernel(src_ref, out_ref, send_sems, recv_sems):
    narrow = lax.axis_index("narrow")
    wide = lax.axis_index("wide")
    z_lo = narrow // 2
    core = narrow % 2
    z_hi = (wide // 4) % 2
    flipped = wide + 4 - 8 * z_hi
    split = (src_ref.shape[0] // 32) * 16
    halves = [pl.ds(0, split), pl.ds(split, src_ref.shape[0] - split)]
    sibling = (wide, z_lo * 2 + 1 - core)
    across = [(wide, (1 - z_lo) * 2 + c) for c in (0, 1)]
    around = [(flipped, (1 - z_lo) * 2 + c) for c in (0, 1)]
    barrier = pltpu.get_barrier_semaphore()
    for peer in [sibling] + across + around:
        pl.semaphore_signal(barrier, 1, device_id=peer, device_id_type=pl.DeviceIdType.MESH)
    pl.semaphore_wait(barrier, 5)
    sends = [(sibling, 0), (sibling, 1)] + [(p, 0) for p in across] + [(p, 1) for p in around]
    copies = []
    for number, (peer, part) in enumerate(sends):
        rows = halves[part]
        copy = pltpu.make_async_remote_copy(
            src_ref=src_ref.at[rows],
            dst_ref=out_ref.at[narrow, rows],
            send_sem=send_sems.at[number],
            recv_sem=recv_sems.at[narrow, part],
            device_id=peer,
            device_id_type=pl.DeviceIdType.MESH,
        )
        copy.start()
        copies.append(copy)
    out_ref[narrow] = src_ref[...]
    for copy in copies:
        copy.wait_send()
    for step in range(1, 4):
        owner = lax.rem(narrow + step, 4)
        for part in (0, 1):
            rows = halves[part]
            pltpu.make_async_remote_copy(
                src_ref=src_ref.at[rows],
                dst_ref=out_ref.at[owner, rows],
                send_sem=send_sems.at[0],
                recv_sem=recv_sems.at[owner, part],
                device_id=sibling,
                device_id_type=pl.DeviceIdType.MESH,
            ).wait_recv()


def gather_replica(shard_rows):
    count, width = shard_rows.shape
    return pl.pallas_call(
        gather_kernel,
        out_shape=jax.ShapeDtypeStruct((4, count, width), shard_rows.dtype),
        in_specs=[pl.BlockSpec(memory_space=pltpu.VMEM)],
        out_specs=pl.BlockSpec(memory_space=pltpu.VMEM),
        scratch_shapes=[pltpu.SemaphoreType.DMA((6,)), pltpu.SemaphoreType.DMA((4, 2))],
        compiler_params=pltpu.CompilerParams(collective_id=0, has_side_effects=True),
    )(shard_rows)


def keep_carry(carry):
    return carry


def body(tokens, cotangent, lengths, master, first_moment, second_moment):
    token_rows = tokens.shape[0]
    narrow_size = lax.axis_size("narrow")
    group_rows = token_rows * narrow_size
    narrow_rank = lax.axis_index("narrow")
    group_width = QUERY_HEADS // KEYVAL_HEADS
    score_scale = HEAD_SIZE ** (-0.5)
    shard_len = master.shape[0]
    replica = gather_replica(master.astype(jnp.bfloat16).reshape(shard_len // 128, 128)).reshape(-1)
    w_query, w_key, w_value, w_out, w_gate, w_up, w_down, gain_one, gain_two = unpack(replica)
    lengths_row = lengths[0]
    local_index = narrow_rank * token_rows + jnp.arange(token_rows, dtype=jnp.int32)
    segment, token_position = place_tokens(local_index, lengths_row)
    group_index = jnp.arange(group_rows, dtype=jnp.int32)
    key_segment = place_tokens(group_index, lengths_row)[0]
    first_start = local_index[0] - token_position[0]
    last_index = local_index[token_rows - 1]
    range_rows = token_rows
    span_starts = list(range(0, group_rows, range_rows))
    resid = tokens.astype(jnp.float32)
    normed_one, inverse_one = normalize(resid)
    hidden_one = (normed_one * gain_one.astype(jnp.float32)).astype(jnp.bfloat16)
    query = jnp.dot(hidden_one, w_query, preferred_element_type=jnp.float32)
    key_projection = jnp.dot(hidden_one, w_key, preferred_element_type=jnp.float32)
    value_proj = jnp.dot(hidden_one, w_value, preferred_element_type=jnp.float32)
    query_batch = apply_rotary(query, token_position, QUERY_HEADS, 1.0).astype(jnp.bfloat16)
    key_batch = apply_rotary(key_projection, token_position, KEYVAL_HEADS, 1.0).astype(jnp.bfloat16)
    value_batch = value_proj.astype(jnp.bfloat16)
    kv_width = KEYVAL_HEADS * HEAD_SIZE
    kv_all = lax.all_gather(
        jnp.concatenate([key_batch, value_batch], axis=1), "narrow", axis=0, tiled=True
    )
    key_all, value_all = kv_all[:, :kv_width], kv_all[:, kv_width:]
    query_tensor_split = query_batch.reshape(token_rows, KEYVAL_HEADS, group_width, HEAD_SIZE)

    def span_setup(span_start, key_source, value_source):
        key_tensor_split = lax.slice_in_dim(
            key_source, span_start, span_start + range_rows
        ).reshape(range_rows, KEYVAL_HEADS, HEAD_SIZE)
        value_tensor_split = lax.slice_in_dim(
            value_source, span_start, span_start + range_rows
        ).reshape(range_rows, KEYVAL_HEADS, HEAD_SIZE)
        span_segment = lax.slice_in_dim(key_segment, span_start, span_start + range_rows)
        span_index = lax.slice_in_dim(group_index, span_start, span_start + range_rows)
        allowed = (segment[:, None] == span_segment[None, :]) & (
            span_index[None, :] <= local_index[:, None]
        )
        needed = (span_start <= last_index) & (span_start + range_rows - 1 >= first_start)
        return (key_tensor_split, value_tensor_split, allowed[None, None], needed)

    running_maximum = jnp.full((KEYVAL_HEADS, group_width, token_rows), masked_logits, jnp.float32)
    running_denominator = jnp.zeros((KEYVAL_HEADS, group_width, token_rows), jnp.float32)
    for span_start in span_starts:
        key_tensor_split, value_tensor_split, allowed, needed = span_setup(
            span_start, key_all, value_all
        )

        def extend(carry):
            old_top, old_total = carry
            scores = (
                jnp.einsum(
                    "qgrd,kgd->grqk",
                    query_tensor_split,
                    key_tensor_split,
                    preferred_element_type=jnp.float32,
                )
                * score_scale
            )
            new_top = jnp.maximum(
                old_top, jnp.max(jnp.where(allowed, scores, masked_logits), axis=-1)
            )
            span_sum = jnp.sum(
                jnp.where(allowed, jnp.exp(scores - new_top[..., None]), 0.0), axis=-1
            )
            return (new_top, old_total * jnp.exp(old_top - new_top) + span_sum)

        running_maximum, running_denominator = lax.cond(
            needed, extend, keep_carry, (running_maximum, running_denominator)
        )
    lse = running_maximum + jnp.log(running_denominator)
    running_total = jnp.zeros((token_rows, KEYVAL_HEADS, group_width, HEAD_SIZE), jnp.float32)
    for span_start in span_starts:
        key_tensor_split, value_tensor_split, allowed, needed = span_setup(
            span_start, key_all, value_all
        )

        def weigh_values(carry):
            scores = (
                jnp.einsum(
                    "qgrd,kgd->grqk",
                    query_tensor_split,
                    key_tensor_split,
                    preferred_element_type=jnp.float32,
                )
                * score_scale
            )
            probs_b = jnp.where(allowed, jnp.exp(scores - lse[..., None]), 0.0).astype(jnp.bfloat16)
            return carry + jnp.einsum(
                "grqk,kgd->qgrd", probs_b, value_tensor_split, preferred_element_type=jnp.float32
            )

        running_total = lax.cond(needed, weigh_values, keep_carry, running_total)
    attention_output = running_total.reshape(token_rows, QUERY_HEADS * HEAD_SIZE).astype(
        jnp.bfloat16
    )
    mixed = resid + jnp.dot(attention_output, w_out, preferred_element_type=jnp.float32)
    normed_two, inverse_two = normalize(mixed)
    hidden_two = (normed_two * gain_two.astype(jnp.float32)).astype(jnp.bfloat16)
    gate = jnp.dot(hidden_two, w_gate, preferred_element_type=jnp.float32)
    upward = jnp.dot(hidden_two, w_up, preferred_element_type=jnp.float32)
    sigma = jax.nn.sigmoid(gate)
    activated = (gate * sigma * upward).astype(jnp.bfloat16)
    output = (mixed + jnp.dot(activated, w_down, preferred_element_type=jnp.float32)).astype(
        jnp.bfloat16
    )
    d_act = jnp.dot(cotangent, w_down.T, preferred_element_type=jnp.float32)
    g_down = jnp.dot(activated.T, cotangent, preferred_element_type=jnp.float32)
    d_gate = (d_act * upward * sigma * (1.0 + gate * (1.0 - sigma))).astype(jnp.bfloat16)
    d_up = (d_act * gate * sigma).astype(jnp.bfloat16)
    g_gate = jnp.dot(hidden_two.T, d_gate, preferred_element_type=jnp.float32)
    g_up = jnp.dot(hidden_two.T, d_up, preferred_element_type=jnp.float32)
    d_hidden_two = jnp.dot(d_gate, w_gate.T, preferred_element_type=jnp.float32) + jnp.dot(
        d_up, w_up.T, preferred_element_type=jnp.float32
    )
    g_gain_two = jnp.sum(d_hidden_two * normed_two, axis=0)
    dn_two = d_hidden_two * gain_two.astype(jnp.float32)
    d_mixed = cotangent.astype(jnp.float32) + inverse_two * (
        dn_two - normed_two * jnp.mean(dn_two * normed_two, axis=-1, keepdims=True)
    )
    d_mixed_b = d_mixed.astype(jnp.bfloat16)
    g_out = jnp.dot(attention_output.T, d_mixed_b, preferred_element_type=jnp.float32)
    attention_output_gradient = jnp.dot(
        d_mixed_b, w_out.T, preferred_element_type=jnp.float32
    ).astype(jnp.bfloat16)
    split_gradient = attention_output_gradient.reshape(
        token_rows, KEYVAL_HEADS, group_width, HEAD_SIZE
    )
    attention_output_split = attention_output.reshape(
        token_rows, KEYVAL_HEADS, group_width, HEAD_SIZE
    )
    softmax_correction = jnp.sum(
        split_gradient.astype(jnp.float32) * attention_output_split.astype(jnp.float32), axis=-1
    ).transpose(1, 2, 0)
    key_back, value_back = (key_all, value_all)
    query_gradient_running = jnp.zeros(
        (token_rows, KEYVAL_HEADS, group_width, HEAD_SIZE), jnp.float32
    )
    key_contributions = []
    value_contributions = []
    for span_start in span_starts:
        key_tensor_split, value_tensor_split, allowed, needed = span_setup(
            span_start, key_back, value_back
        )

        def back_span(carry):
            scores = (
                jnp.einsum(
                    "qgrd,kgd->grqk",
                    query_tensor_split,
                    key_tensor_split,
                    preferred_element_type=jnp.float32,
                )
                * score_scale
            )
            probs = jnp.where(allowed, jnp.exp(scores - lse[..., None]), 0.0)
            probs_b = probs.astype(jnp.bfloat16)
            value_gradient_range = jnp.einsum(
                "pozf,zpom->fpm", probs_b, split_gradient, preferred_element_type=jnp.float32
            )
            d_probs = jnp.einsum(
                "qgrd,kgd->grqk",
                split_gradient,
                value_tensor_split,
                preferred_element_type=jnp.float32,
            )
            score_gradient = (
                probs * (d_probs - softmax_correction[..., None]) * score_scale
            ).astype(jnp.bfloat16)
            new_acc = carry + jnp.einsum(
                "grqk,kgd->qgrd",
                score_gradient,
                key_tensor_split,
                preferred_element_type=jnp.float32,
            )
            key_gradient_range = jnp.einsum(
                "pozf,zpom->fpm",
                score_gradient,
                query_tensor_split,
                preferred_element_type=jnp.float32,
            )
            return (new_acc, key_gradient_range, value_gradient_range)

        def skip_span(carry):
            blank_range = jnp.zeros((range_rows, KEYVAL_HEADS, HEAD_SIZE), jnp.float32)
            return (carry, blank_range, blank_range)

        query_gradient_running, key_gradient_range, value_gradient_range = lax.cond(
            needed, back_span, skip_span, query_gradient_running
        )
        key_contributions.append(key_gradient_range.reshape(range_rows, KEYVAL_HEADS * HEAD_SIZE))
        value_contributions.append(
            value_gradient_range.reshape(range_rows, KEYVAL_HEADS * HEAD_SIZE)
        )
    kv_sum_in = jnp.stack(
        [jnp.concatenate(pair, axis=1) for pair in zip(key_contributions, value_contributions)]
    )
    kv_grad = kv_sum_in[narrow_rank]
    for shift in range(1, narrow_size):
        sender_block = kv_sum_in[lax.rem(narrow_rank + narrow_size - shift, narrow_size)]
        kv_grad = kv_grad + lax.ppermute(
            sender_block,
            "narrow",
            [(source, source - shift) for source in range(shift, narrow_size)],
        )
    key_gradient, value_gradient = kv_grad[:, :kv_width], kv_grad[:, kv_width:]
    d_query = query_gradient_running.reshape(token_rows, QUERY_HEADS * HEAD_SIZE)
    d_query_b = apply_rotary(d_query, token_position, QUERY_HEADS, -1.0).astype(jnp.bfloat16)
    key_gradient_batch = apply_rotary(key_gradient, token_position, KEYVAL_HEADS, -1.0).astype(
        jnp.bfloat16
    )
    value_gradient_batch = value_gradient.astype(jnp.bfloat16)
    g_query = jnp.dot(hidden_one.T, d_query_b, preferred_element_type=jnp.float32)
    g_key = jnp.dot(hidden_one.T, key_gradient_batch, preferred_element_type=jnp.float32)
    g_value = jnp.dot(hidden_one.T, value_gradient_batch, preferred_element_type=jnp.float32)
    d_hidden_one = (
        jnp.dot(d_query_b, w_query.T, preferred_element_type=jnp.float32)
        + jnp.dot(key_gradient_batch, w_key.T, preferred_element_type=jnp.float32)
        + jnp.dot(value_gradient_batch, w_value.T, preferred_element_type=jnp.float32)
    )
    g_gain_one = jnp.sum(d_hidden_one * normed_one, axis=0)
    dn_one = d_hidden_one * gain_one.astype(jnp.float32)
    d_tokens = (
        d_mixed
        + inverse_one
        * (dn_one - normed_one * jnp.mean(dn_one * normed_one, axis=-1, keepdims=True))
    ).astype(jnp.bfloat16)
    down_and_gains = jnp.concatenate([g_down, g_gain_one[None], g_gain_two[None]], axis=0)
    grad_pieces = lax.psum(
        (g_query, g_key, g_value, g_out, g_gate, g_up, down_and_gains), ("wide", "narrow")
    )

    def shard_of(rank):
        def build(pieces):
            parts = []
            offset = 0
            low, high = rank * shard_len, (rank + 1) * shard_len
            for piece in pieces:
                size = piece.size
                start, stop = max(low, offset), min(high, offset + size)
                if start < stop:
                    parts.append(piece.reshape(-1)[start - offset : stop - offset])
                offset = offset + size
            return jnp.concatenate(parts)

        return build

    summed = lax.switch(narrow_rank, [shard_of(rank) for rank in range(narrow_size)], grad_pieces)
    token_total = token_rows * narrow_size * lax.axis_size("wide")
    gradient = summed * (1.0 / math.sqrt(token_total))
    new_first = beta_one * first_moment + (1.0 - beta_one) * gradient
    new_second = beta_two * second_moment + (1.0 - beta_two) * gradient * gradient
    first_hat = new_first / (1.0 - beta_one**STEP)
    second_hat = new_second / (1.0 - beta_two**STEP)
    entry_index = narrow_rank * shard_len + jnp.arange(shard_len, dtype=jnp.int32)
    decay = jnp.where(entry_index < NPARAM - 2 * MODEL_WIDTH, decay_rate, 0.0)
    new_master = master - learn_rate * (
        first_hat / (jnp.sqrt(second_hat) + adam_eps) + decay * master
    )
    return (output, d_tokens, gradient, new_master, new_first, new_second)


def solution(mesh):
    in_specs = (
        P(("wide", "narrow"), None),
        P(("wide", "narrow"), None),
        P("wide", None),
        P("narrow"),
        P("narrow"),
        P("narrow"),
    )
    out_specs = (
        P(("wide", "narrow"), None),
        P(("wide", "narrow"), None),
        P("narrow"),
        P("narrow"),
        P("narrow"),
        P("narrow"),
    )
    return jax.shard_map(body, mesh=mesh, in_specs=in_specs, out_specs=out_specs, check_vma=False)
```

```python
import math

import jax
import jax.numpy as jnp
from jax import lax
from jax.experimental import pallas as pl
from jax.experimental.pallas import tpu as pltpu
from jax.sharding import PartitionSpec as P

MODEL_WIDTH = 512
QUERY_HEADS = 15
KEYVAL_HEADS = 5
HEAD_SIZE = 64
FEEDFWD_UNITS = 1280
STEP = 4
NPARAM = 3277824


eps_norm = 1e-05
rope_base = 100000.0
beta_one = 0.9
beta_two = 0.95
learn_rate = 0.03
decay_rate = 0.1
adam_eps = 1e-08
masked_logits = -1e30


def unpack(flat):
    arrangement_list = [
        (MODEL_WIDTH, QUERY_HEADS * HEAD_SIZE),
        (MODEL_WIDTH, KEYVAL_HEADS * HEAD_SIZE),
        (MODEL_WIDTH, KEYVAL_HEADS * HEAD_SIZE),
        (QUERY_HEADS * HEAD_SIZE, MODEL_WIDTH),
        (MODEL_WIDTH, FEEDFWD_UNITS),
        (MODEL_WIDTH, FEEDFWD_UNITS),
        (FEEDFWD_UNITS, MODEL_WIDTH),
        (MODEL_WIDTH,),
        (MODEL_WIDTH,),
    ]
    pieces = []
    offset = 0
    for layout in arrangement_list:
        length = math.prod(layout)
        pieces.append(flat[offset : offset + length].reshape(layout))
        offset = offset + length
    return pieces


def place_tokens(indices, lengths_row):
    seq_ends = jnp.cumsum(lengths_row)
    seq_starts = seq_ends - lengths_row
    member = (indices[:, None] >= seq_starts[None, :]) & (indices[:, None] < seq_ends[None, :])
    numbers = jnp.arange(lengths_row.shape[0], dtype=jnp.int32)
    segment = jnp.sum(jnp.where(member, numbers[None, :], 0), axis=1)
    token_position = indices - jnp.sum(jnp.where(member, seq_starts[None, :], 0), axis=1)
    return (segment, token_position)


def normalize(values):
    inverse_rms = lax.rsqrt(jnp.mean(values * values, axis=-1, keepdims=True) + eps_norm)
    return (values * inverse_rms, inverse_rms)


def apply_rotary(values, token_position, head_count, turn_sign):
    half_dim = HEAD_SIZE // 2
    inverse = rope_base ** (-2.0 * jnp.arange(half_dim, dtype=jnp.float32) / HEAD_SIZE)
    angles = token_position.astype(jnp.float32)[:, None] * inverse[None, :]
    cosine = jnp.cos(angles)[:, None, :]
    sine = turn_sign * jnp.sin(angles)[:, None, :]
    shaped = values.reshape(values.shape[0], head_count, HEAD_SIZE)
    first_half = shaped[:, :, :half_dim]
    second_half = shaped[:, :, half_dim:]
    turned = jnp.concatenate(
        [first_half * cosine - second_half * sine, second_half * cosine + first_half * sine],
        axis=-1,
    )
    return turned.reshape(values.shape)


def gather_kernel(src_ref, out_ref, send_sems, recv_sems):
    narrow = lax.axis_index("narrow")
    wide = lax.axis_index("wide")
    z_lo = narrow // 2
    core = narrow % 2
    z_hi = (wide // 4) % 2
    flipped = wide + 4 - 8 * z_hi
    split = (src_ref.shape[0] // 32) * 16
    halves = [pl.ds(0, split), pl.ds(split, src_ref.shape[0] - split)]
    sibling = (wide, z_lo * 2 + 1 - core)
    across = [(wide, (1 - z_lo) * 2 + c) for c in (0, 1)]
    around = [(flipped, (1 - z_lo) * 2 + c) for c in (0, 1)]
    barrier = pltpu.get_barrier_semaphore()
    for peer in [sibling] + across + around:
        pl.semaphore_signal(barrier, 1, device_id=peer, device_id_type=pl.DeviceIdType.MESH)
    pl.semaphore_wait(barrier, 5)
    sends = [(sibling, 0), (sibling, 1)] + [(p, 0) for p in across] + [(p, 1) for p in around]
    copies = []
    for number, (peer, part) in enumerate(sends):
        rows = halves[part]
        copy = pltpu.make_async_remote_copy(
            src_ref=src_ref.at[rows],
            dst_ref=out_ref.at[narrow, rows],
            send_sem=send_sems.at[number],
            recv_sem=recv_sems.at[narrow, part],
            device_id=peer,
            device_id_type=pl.DeviceIdType.MESH,
        )
        copy.start()
        copies.append(copy)
    out_ref[narrow] = src_ref[...]
    for copy in copies:
        copy.wait_send()
    for step in range(1, 4):
        owner = lax.rem(narrow + step, 4)
        for part in (0, 1):
            rows = halves[part]
            pltpu.make_async_remote_copy(
                src_ref=src_ref.at[rows],
                dst_ref=out_ref.at[owner, rows],
                send_sem=send_sems.at[0],
                recv_sem=recv_sems.at[owner, part],
                device_id=sibling,
                device_id_type=pl.DeviceIdType.MESH,
            ).wait_recv()


def gather_replica(shard_rows):
    count, width = shard_rows.shape
    return pl.pallas_call(
        gather_kernel,
        out_shape=jax.ShapeDtypeStruct((4, count, width), shard_rows.dtype),
        in_specs=[pl.BlockSpec(memory_space=pltpu.VMEM)],
        out_specs=pl.BlockSpec(memory_space=pltpu.VMEM),
        scratch_shapes=[pltpu.SemaphoreType.DMA((6,)), pltpu.SemaphoreType.DMA((4, 2))],
        compiler_params=pltpu.CompilerParams(collective_id=0, has_side_effects=True),
    )(shard_rows)


def keep_carry(carry):
    return carry


def body(tokens, cotangent, lengths, master, first_moment, second_moment):
    token_rows = tokens.shape[0]
    narrow_size = lax.axis_size("narrow")
    group_rows = token_rows * narrow_size
    narrow_rank = lax.axis_index("narrow")
    group_width = QUERY_HEADS // KEYVAL_HEADS
    score_scale = HEAD_SIZE ** (-0.5)
    shard_len = master.shape[0]
    replica = gather_replica(master.astype(jnp.bfloat16).reshape(shard_len // 128, 128)).reshape(-1)
    w_query, w_key, w_value, w_out, w_gate, w_up, w_down, gain_one, gain_two = unpack(replica)
    lengths_row = lengths[0]
    local_index = narrow_rank * token_rows + jnp.arange(token_rows, dtype=jnp.int32)
    segment, token_position = place_tokens(local_index, lengths_row)
    group_index = jnp.arange(group_rows, dtype=jnp.int32)
    key_segment = place_tokens(group_index, lengths_row)[0]
    first_start = local_index[0] - token_position[0]
    last_index = local_index[token_rows - 1]
    range_rows = token_rows
    span_starts = list(range(0, group_rows, range_rows))
    resid = tokens.astype(jnp.float32)
    normed_one, inverse_one = normalize(resid)
    hidden_one = (normed_one * gain_one.astype(jnp.float32)).astype(jnp.bfloat16)
    query = jnp.dot(hidden_one, w_query, preferred_element_type=jnp.float32)
    key_projection = jnp.dot(hidden_one, w_key, preferred_element_type=jnp.float32)
    value_proj = jnp.dot(hidden_one, w_value, preferred_element_type=jnp.float32)
    query_batch = apply_rotary(query, token_position, QUERY_HEADS, 1.0).astype(jnp.bfloat16)
    key_batch = apply_rotary(key_projection, token_position, KEYVAL_HEADS, 1.0).astype(jnp.bfloat16)
    value_batch = value_proj.astype(jnp.bfloat16)
    kv_width = KEYVAL_HEADS * HEAD_SIZE
    kv_all = lax.all_gather(
        jnp.concatenate([key_batch, value_batch], axis=1), "narrow", axis=0, tiled=True
    )
    key_all, value_all = kv_all[:, :kv_width], kv_all[:, kv_width:]
    query_tensor_split = query_batch.reshape(token_rows, KEYVAL_HEADS, group_width, HEAD_SIZE)

    def span_setup(span_start, key_source, value_source):
        key_tensor_split = lax.slice_in_dim(
            key_source, span_start, span_start + range_rows
        ).reshape(range_rows, KEYVAL_HEADS, HEAD_SIZE)
        value_tensor_split = lax.slice_in_dim(
            value_source, span_start, span_start + range_rows
        ).reshape(range_rows, KEYVAL_HEADS, HEAD_SIZE)
        span_segment = lax.slice_in_dim(key_segment, span_start, span_start + range_rows)
        span_index = lax.slice_in_dim(group_index, span_start, span_start + range_rows)
        allowed = (segment[:, None] == span_segment[None, :]) & (
            span_index[None, :] <= local_index[:, None]
        )
        needed = (span_start <= last_index) & (span_start + range_rows - 1 >= first_start)
        return (key_tensor_split, value_tensor_split, allowed[None, None], needed)

    running_maximum = jnp.full((KEYVAL_HEADS, group_width, token_rows), masked_logits, jnp.float32)
    running_denominator = jnp.zeros((KEYVAL_HEADS, group_width, token_rows), jnp.float32)
    for span_start in span_starts:
        key_tensor_split, value_tensor_split, allowed, needed = span_setup(
            span_start, key_all, value_all
        )

        def extend(carry):
            old_top, old_total = carry
            scores = (
                jnp.einsum(
                    "qgrd,kgd->grqk",
                    query_tensor_split,
                    key_tensor_split,
                    preferred_element_type=jnp.float32,
                )
                * score_scale
            )
            new_top = jnp.maximum(
                old_top, jnp.max(jnp.where(allowed, scores, masked_logits), axis=-1)
            )
            span_sum = jnp.sum(
                jnp.where(allowed, jnp.exp(scores - new_top[..., None]), 0.0), axis=-1
            )
            return (new_top, old_total * jnp.exp(old_top - new_top) + span_sum)

        running_maximum, running_denominator = lax.cond(
            needed, extend, keep_carry, (running_maximum, running_denominator)
        )
    lse = running_maximum + jnp.log(running_denominator)
    running_total = jnp.zeros((token_rows, KEYVAL_HEADS, group_width, HEAD_SIZE), jnp.float32)
    for span_start in span_starts:
        key_tensor_split, value_tensor_split, allowed, needed = span_setup(
            span_start, key_all, value_all
        )

        def weigh_values(carry):
            scores = (
                jnp.einsum(
                    "qgrd,kgd->grqk",
                    query_tensor_split,
                    key_tensor_split,
                    preferred_element_type=jnp.float32,
                )
                * score_scale
            )
            probs_b = jnp.where(allowed, jnp.exp(scores - lse[..., None]), 0.0).astype(jnp.bfloat16)
            return carry + jnp.einsum(
                "grqk,kgd->qgrd", probs_b, value_tensor_split, preferred_element_type=jnp.float32
            )

        running_total = lax.cond(needed, weigh_values, keep_carry, running_total)
    attention_output = running_total.reshape(token_rows, QUERY_HEADS * HEAD_SIZE).astype(
        jnp.bfloat16
    )
    mixed = resid + jnp.dot(attention_output, w_out, preferred_element_type=jnp.float32)
    normed_two, inverse_two = normalize(mixed)
    hidden_two = (normed_two * gain_two.astype(jnp.float32)).astype(jnp.bfloat16)
    gate = jnp.dot(hidden_two, w_gate, preferred_element_type=jnp.float32)
    upward = jnp.dot(hidden_two, w_up, preferred_element_type=jnp.float32)
    sigma = jax.nn.sigmoid(gate)
    activated = (gate * sigma * upward).astype(jnp.bfloat16)
    output = (mixed + jnp.dot(activated, w_down, preferred_element_type=jnp.float32)).astype(
        jnp.bfloat16
    )
    d_act = jnp.dot(cotangent, w_down.T, preferred_element_type=jnp.float32)
    g_down = jnp.dot(activated.T, cotangent, preferred_element_type=jnp.float32)
    d_gate = (d_act * upward * sigma * (1.0 + gate * (1.0 - sigma))).astype(jnp.bfloat16)
    d_up = (d_act * gate * sigma).astype(jnp.bfloat16)
    g_gate = jnp.dot(hidden_two.T, d_gate, preferred_element_type=jnp.float32)
    g_up = jnp.dot(hidden_two.T, d_up, preferred_element_type=jnp.float32)
    d_hidden_two = jnp.dot(d_gate, w_gate.T, preferred_element_type=jnp.float32) + jnp.dot(
        d_up, w_up.T, preferred_element_type=jnp.float32
    )
    g_gain_two = jnp.sum(d_hidden_two * normed_two, axis=0)
    dn_two = d_hidden_two * gain_two.astype(jnp.float32)
    d_mixed = cotangent.astype(jnp.float32) + inverse_two * (
        dn_two - normed_two * jnp.mean(dn_two * normed_two, axis=-1, keepdims=True)
    )
    d_mixed_b = d_mixed.astype(jnp.bfloat16)
    g_out = jnp.dot(attention_output.T, d_mixed_b, preferred_element_type=jnp.float32)
    attention_output_gradient = jnp.dot(
        d_mixed_b, w_out.T, preferred_element_type=jnp.float32
    ).astype(jnp.bfloat16)
    split_gradient = attention_output_gradient.reshape(
        token_rows, KEYVAL_HEADS, group_width, HEAD_SIZE
    )
    attention_output_split = attention_output.reshape(
        token_rows, KEYVAL_HEADS, group_width, HEAD_SIZE
    )
    softmax_correction = jnp.sum(
        split_gradient.astype(jnp.float32) * attention_output_split.astype(jnp.float32), axis=-1
    ).transpose(1, 2, 0)
    key_back, value_back = (key_all, value_all)
    query_gradient_running = jnp.zeros(
        (token_rows, KEYVAL_HEADS, group_width, HEAD_SIZE), jnp.float32
    )
    key_contributions = []
    value_contributions = []
    for span_start in span_starts:
        key_tensor_split, value_tensor_split, allowed, needed = span_setup(
            span_start, key_back, value_back
        )

        def back_span(carry):
            scores = (
                jnp.einsum(
                    "qgrd,kgd->grqk",
                    query_tensor_split,
                    key_tensor_split,
                    preferred_element_type=jnp.float32,
                )
                * score_scale
            )
            probs = jnp.where(allowed, jnp.exp(scores - lse[..., None]), 0.0)
            probs_b = probs.astype(jnp.bfloat16)
            value_gradient_range = jnp.einsum(
                "pozf,zpom->fpm", probs_b, split_gradient, preferred_element_type=jnp.float32
            )
            d_probs = jnp.einsum(
                "qgrd,kgd->grqk",
                split_gradient,
                value_tensor_split,
                preferred_element_type=jnp.float32,
            )
            score_gradient = (
                probs * (d_probs - softmax_correction[..., None]) * score_scale
            ).astype(jnp.bfloat16)
            new_acc = carry + jnp.einsum(
                "grqk,kgd->qgrd",
                score_gradient,
                key_tensor_split,
                preferred_element_type=jnp.float32,
            )
            key_gradient_range = jnp.einsum(
                "pozf,zpom->fpm",
                score_gradient,
                query_tensor_split,
                preferred_element_type=jnp.float32,
            )
            return (new_acc, key_gradient_range, value_gradient_range)

        def skip_span(carry):
            blank_range = jnp.zeros((range_rows, KEYVAL_HEADS, HEAD_SIZE), jnp.float32)
            return (carry, blank_range, blank_range)

        query_gradient_running, key_gradient_range, value_gradient_range = lax.cond(
            needed, back_span, skip_span, query_gradient_running
        )
        key_contributions.append(key_gradient_range.reshape(range_rows, KEYVAL_HEADS * HEAD_SIZE))
        value_contributions.append(
            value_gradient_range.reshape(range_rows, KEYVAL_HEADS * HEAD_SIZE)
        )
    kv_sum_in = jnp.stack(
        [jnp.concatenate(pair, axis=1) for pair in zip(key_contributions, value_contributions)]
    )
    kv_grad = kv_sum_in[narrow_rank]
    for shift in range(1, narrow_size):
        sender_block = kv_sum_in[lax.rem(narrow_rank + narrow_size - shift, narrow_size)]
        kv_grad = kv_grad + lax.ppermute(
            sender_block,
            "narrow",
            [(source, source - shift) for source in range(shift, narrow_size)],
        )
    key_gradient, value_gradient = kv_grad[:, :kv_width], kv_grad[:, kv_width:]
    d_query = query_gradient_running.reshape(token_rows, QUERY_HEADS * HEAD_SIZE)
    d_query_b = apply_rotary(d_query, token_position, QUERY_HEADS, -1.0).astype(jnp.bfloat16)
    key_gradient_batch = apply_rotary(key_gradient, token_position, KEYVAL_HEADS, -1.0).astype(
        jnp.bfloat16
    )
    value_gradient_batch = value_gradient.astype(jnp.bfloat16)
    g_query = jnp.dot(hidden_one.T, d_query_b, preferred_element_type=jnp.float32)
    g_key_value = jnp.dot(
        hidden_one.T,
        jnp.concatenate([key_gradient_batch, value_gradient_batch], axis=1),
        preferred_element_type=jnp.float32,
    )
    d_hidden_one = (
        jnp.dot(d_query_b, w_query.T, preferred_element_type=jnp.float32)
        + jnp.dot(key_gradient_batch, w_key.T, preferred_element_type=jnp.float32)
        + jnp.dot(value_gradient_batch, w_value.T, preferred_element_type=jnp.float32)
    )
    g_gain_one = jnp.sum(d_hidden_one * normed_one, axis=0)
    dn_one = d_hidden_one * gain_one.astype(jnp.float32)
    d_tokens = (
        d_mixed
        + inverse_one
        * (dn_one - normed_one * jnp.mean(dn_one * normed_one, axis=-1, keepdims=True))
    ).astype(jnp.bfloat16)
    out_and_gains = jnp.concatenate([g_out, g_gain_one[None], g_gain_two[None]], axis=0)
    grad_pieces = lax.psum(
        (g_query, g_key_value, out_and_gains, g_gate, g_up, g_down), ("wide", "narrow")
    )
    out_rows = QUERY_HEADS * HEAD_SIZE
    kv_width_total = KEYVAL_HEADS * HEAD_SIZE
    flat_pieces = [
        (0, 0, None),
        (1, 0, kv_width_total),
        (1, kv_width_total, kv_width_total),
        (2, 0, out_rows),
        (3, 0, None),
        (4, 0, None),
        (5, 0, None),
        (2, out_rows, 2),
    ]

    def shard_of(rank):
        def build(pieces):
            parts = []
            offset = 0
            low, high = rank * shard_len, (rank + 1) * shard_len
            for index, column, width in flat_pieces:
                piece = pieces[index]
                if index == 2:
                    piece = piece[column : column + width]
                elif width is not None:
                    piece = piece[:, column : column + width]
                rows, cols = piece.shape
                size = rows * cols
                start, stop = max(low, offset), min(high, offset + size)
                if start < stop:
                    first_row = (start - offset) // cols
                    last_row = -(-(stop - offset) // cols)
                    block = piece[first_row:last_row].reshape(-1)
                    base = offset + first_row * cols
                    parts.append(block[start - base : stop - base])
                offset = offset + size
            return jnp.concatenate(parts)

        return build

    summed = lax.switch(narrow_rank, [shard_of(rank) for rank in range(narrow_size)], grad_pieces)
    token_total = token_rows * narrow_size * lax.axis_size("wide")
    gradient = summed * (1.0 / math.sqrt(token_total))
    new_first = beta_one * first_moment + (1.0 - beta_one) * gradient
    new_second = beta_two * second_moment + (1.0 - beta_two) * gradient * gradient
    first_hat = new_first / (1.0 - beta_one**STEP)
    second_hat = new_second / (1.0 - beta_two**STEP)
    entry_index = narrow_rank * shard_len + jnp.arange(shard_len, dtype=jnp.int32)
    decay = jnp.where(entry_index < NPARAM - 2 * MODEL_WIDTH, decay_rate, 0.0)
    new_master = master - learn_rate * (
        first_hat / (jnp.sqrt(second_hat) + adam_eps) + decay * master
    )
    return (output, d_tokens, gradient, new_master, new_first, new_second)


def solution(mesh):
    in_specs = (
        P(("wide", "narrow"), None),
        P(("wide", "narrow"), None),
        P("wide", None),
        P("narrow"),
        P("narrow"),
        P("narrow"),
    )
    out_specs = (
        P(("wide", "narrow"), None),
        P(("wide", "narrow"), None),
        P("narrow"),
        P("narrow"),
        P("narrow"),
        P("narrow"),
    )
    return jax.shard_map(body, mesh=mesh, in_specs=in_specs, out_specs=out_specs, check_vma=False)
```

```python
import math

import jax
import jax.numpy as jnp
from jax import lax
from jax.experimental import pallas as pl
from jax.experimental.pallas import tpu as pltpu
from jax.sharding import PartitionSpec as P

MODEL_WIDTH = 512
QUERY_HEADS = 15
KEYVAL_HEADS = 5
HEAD_SIZE = 64
FEEDFWD_UNITS = 1280
STEP = 4
NPARAM = 3277824


eps_norm = 1e-05
rope_base = 100000.0
beta_one = 0.9
beta_two = 0.95
learn_rate = 0.03
decay_rate = 0.1
adam_eps = 1e-08
masked_logits = -1e30


def unpack(flat):
    arrangement_list = [
        (MODEL_WIDTH, QUERY_HEADS * HEAD_SIZE),
        (MODEL_WIDTH, KEYVAL_HEADS * HEAD_SIZE),
        (MODEL_WIDTH, KEYVAL_HEADS * HEAD_SIZE),
        (QUERY_HEADS * HEAD_SIZE, MODEL_WIDTH),
        (MODEL_WIDTH, FEEDFWD_UNITS),
        (MODEL_WIDTH, FEEDFWD_UNITS),
        (FEEDFWD_UNITS, MODEL_WIDTH),
        (MODEL_WIDTH,),
        (MODEL_WIDTH,),
    ]
    pieces = []
    offset = 0
    for layout in arrangement_list:
        length = math.prod(layout)
        pieces.append(flat[offset : offset + length].reshape(layout))
        offset = offset + length
    return pieces


def place_tokens(indices, lengths_row):
    seq_ends = jnp.cumsum(lengths_row)
    seq_starts = seq_ends - lengths_row
    member = (indices[:, None] >= seq_starts[None, :]) & (indices[:, None] < seq_ends[None, :])
    numbers = jnp.arange(lengths_row.shape[0], dtype=jnp.int32)
    segment = jnp.sum(jnp.where(member, numbers[None, :], 0), axis=1)
    token_position = indices - jnp.sum(jnp.where(member, seq_starts[None, :], 0), axis=1)
    return (segment, token_position)


def normalize(values):
    inverse_rms = lax.rsqrt(jnp.mean(values * values, axis=-1, keepdims=True) + eps_norm)
    return (values * inverse_rms, inverse_rms)


def apply_rotary(values, token_position, head_count, turn_sign):
    half_dim = HEAD_SIZE // 2
    inverse = rope_base ** (-2.0 * jnp.arange(half_dim, dtype=jnp.float32) / HEAD_SIZE)
    angles = token_position.astype(jnp.float32)[:, None] * inverse[None, :]
    cosine = jnp.cos(angles)[:, None, :]
    sine = turn_sign * jnp.sin(angles)[:, None, :]
    shaped = values.reshape(values.shape[0], head_count, HEAD_SIZE)
    first_half = shaped[:, :, :half_dim]
    second_half = shaped[:, :, half_dim:]
    turned = jnp.concatenate(
        [first_half * cosine - second_half * sine, second_half * cosine + first_half * sine],
        axis=-1,
    )
    return turned.reshape(values.shape)


def gather_kernel(src_ref, out_ref, send_sems, recv_sems):
    narrow = lax.axis_index("narrow")
    wide = lax.axis_index("wide")
    z_lo = narrow // 2
    core = narrow % 2
    z_hi = (wide // 4) % 2
    flipped = wide + 4 - 8 * z_hi
    split = (src_ref.shape[0] // 32) * 16
    halves = [pl.ds(0, split), pl.ds(split, src_ref.shape[0] - split)]
    sibling = (wide, z_lo * 2 + 1 - core)
    across = [(wide, (1 - z_lo) * 2 + c) for c in (0, 1)]
    around = [(flipped, (1 - z_lo) * 2 + c) for c in (0, 1)]
    barrier = pltpu.get_barrier_semaphore()
    for peer in [sibling] + across + around:
        pl.semaphore_signal(barrier, 1, device_id=peer, device_id_type=pl.DeviceIdType.MESH)
    pl.semaphore_wait(barrier, 5)
    sends = [(sibling, 0), (sibling, 1)] + [(p, 0) for p in across] + [(p, 1) for p in around]
    copies = []
    for number, (peer, part) in enumerate(sends):
        rows = halves[part]
        copy = pltpu.make_async_remote_copy(
            src_ref=src_ref.at[rows],
            dst_ref=out_ref.at[narrow, rows],
            send_sem=send_sems.at[number],
            recv_sem=recv_sems.at[narrow, part],
            device_id=peer,
            device_id_type=pl.DeviceIdType.MESH,
        )
        copy.start()
        copies.append(copy)
    out_ref[narrow] = src_ref[...]
    for copy in copies:
        copy.wait_send()
    for step in range(1, 4):
        owner = lax.rem(narrow + step, 4)
        for part in (0, 1):
            rows = halves[part]
            pltpu.make_async_remote_copy(
                src_ref=src_ref.at[rows],
                dst_ref=out_ref.at[owner, rows],
                send_sem=send_sems.at[0],
                recv_sem=recv_sems.at[owner, part],
                device_id=sibling,
                device_id_type=pl.DeviceIdType.MESH,
            ).wait_recv()


def gather_replica(shard_rows):
    count, width = shard_rows.shape
    return pl.pallas_call(
        gather_kernel,
        out_shape=jax.ShapeDtypeStruct((4, count, width), shard_rows.dtype),
        in_specs=[pl.BlockSpec(memory_space=pltpu.VMEM)],
        out_specs=pl.BlockSpec(memory_space=pltpu.VMEM),
        scratch_shapes=[pltpu.SemaphoreType.DMA((6,)), pltpu.SemaphoreType.DMA((4, 2))],
        compiler_params=pltpu.CompilerParams(collective_id=0, has_side_effects=True),
    )(shard_rows)


def keep_carry(carry):
    return carry


def body(tokens, cotangent, lengths, master, first_moment, second_moment):
    token_rows = tokens.shape[0]
    narrow_size = lax.axis_size("narrow")
    group_rows = token_rows * narrow_size
    narrow_rank = lax.axis_index("narrow")
    group_width = QUERY_HEADS // KEYVAL_HEADS
    score_scale = HEAD_SIZE ** (-0.5)
    shard_len = master.shape[0]
    replica = gather_replica(master.astype(jnp.bfloat16).reshape(shard_len // 128, 128)).reshape(-1)
    w_query, w_key, w_value, w_out, w_gate, w_up, w_down, gain_one, gain_two = unpack(replica)
    lengths_row = lengths[0]
    local_index = narrow_rank * token_rows + jnp.arange(token_rows, dtype=jnp.int32)
    segment, token_position = place_tokens(local_index, lengths_row)
    group_index = jnp.arange(group_rows, dtype=jnp.int32)
    key_segment = place_tokens(group_index, lengths_row)[0]
    first_start = local_index[0] - token_position[0]
    last_index = local_index[token_rows - 1]
    range_rows = token_rows
    span_starts = list(range(0, group_rows, range_rows))
    resid = tokens.astype(jnp.float32)
    normed_one, inverse_one = normalize(resid)
    hidden_one = (normed_one * gain_one.astype(jnp.float32)).astype(jnp.bfloat16)
    query = jnp.dot(hidden_one, w_query, preferred_element_type=jnp.float32)
    key_projection = jnp.dot(hidden_one, w_key, preferred_element_type=jnp.float32)
    value_proj = jnp.dot(hidden_one, w_value, preferred_element_type=jnp.float32)
    query_batch = apply_rotary(query, token_position, QUERY_HEADS, 1.0).astype(jnp.bfloat16)
    key_batch = apply_rotary(key_projection, token_position, KEYVAL_HEADS, 1.0).astype(jnp.bfloat16)
    value_batch = value_proj.astype(jnp.bfloat16)
    kv_width = KEYVAL_HEADS * HEAD_SIZE
    kv_all = lax.all_gather(
        jnp.concatenate([key_batch, value_batch], axis=1), "narrow", axis=0, tiled=True
    )
    key_all, value_all = kv_all[:, :kv_width], kv_all[:, kv_width:]
    query_tensor_split = query_batch.reshape(token_rows, KEYVAL_HEADS, group_width, HEAD_SIZE)

    def span_setup(span_start, key_source, value_source):
        key_tensor_split = lax.slice_in_dim(
            key_source, span_start, span_start + range_rows
        ).reshape(range_rows, KEYVAL_HEADS, HEAD_SIZE)
        value_tensor_split = lax.slice_in_dim(
            value_source, span_start, span_start + range_rows
        ).reshape(range_rows, KEYVAL_HEADS, HEAD_SIZE)
        span_segment = lax.slice_in_dim(key_segment, span_start, span_start + range_rows)
        span_index = lax.slice_in_dim(group_index, span_start, span_start + range_rows)
        allowed = (segment[:, None] == span_segment[None, :]) & (
            span_index[None, :] <= local_index[:, None]
        )
        needed = (span_start <= last_index) & (span_start + range_rows - 1 >= first_start)
        return (key_tensor_split, value_tensor_split, allowed[None, None], needed)

    running_maximum = jnp.full((KEYVAL_HEADS, group_width, token_rows), masked_logits, jnp.float32)
    running_denominator = jnp.zeros((KEYVAL_HEADS, group_width, token_rows), jnp.float32)
    for span_start in span_starts:
        key_tensor_split, value_tensor_split, allowed, needed = span_setup(
            span_start, key_all, value_all
        )

        def extend(carry):
            old_top, old_total = carry
            scores = (
                jnp.einsum(
                    "qgrd,kgd->grqk",
                    query_tensor_split,
                    key_tensor_split,
                    preferred_element_type=jnp.float32,
                )
                * score_scale
            )
            new_top = jnp.maximum(
                old_top, jnp.max(jnp.where(allowed, scores, masked_logits), axis=-1)
            )
            span_sum = jnp.sum(
                jnp.where(allowed, jnp.exp(scores - new_top[..., None]), 0.0), axis=-1
            )
            return (new_top, old_total * jnp.exp(old_top - new_top) + span_sum)

        running_maximum, running_denominator = lax.cond(
            needed, extend, keep_carry, (running_maximum, running_denominator)
        )
    lse = running_maximum + jnp.log(running_denominator)
    running_total = jnp.zeros((token_rows, KEYVAL_HEADS, group_width, HEAD_SIZE), jnp.float32)
    for span_start in span_starts:
        key_tensor_split, value_tensor_split, allowed, needed = span_setup(
            span_start, key_all, value_all
        )

        def weigh_values(carry):
            scores = (
                jnp.einsum(
                    "qgrd,kgd->grqk",
                    query_tensor_split,
                    key_tensor_split,
                    preferred_element_type=jnp.float32,
                )
                * score_scale
            )
            probs_b = jnp.where(allowed, jnp.exp(scores - lse[..., None]), 0.0).astype(jnp.bfloat16)
            return carry + jnp.einsum(
                "grqk,kgd->qgrd", probs_b, value_tensor_split, preferred_element_type=jnp.float32
            )

        running_total = lax.cond(needed, weigh_values, keep_carry, running_total)
    attention_output = running_total.reshape(token_rows, QUERY_HEADS * HEAD_SIZE).astype(
        jnp.bfloat16
    )
    mixed = resid + jnp.dot(attention_output, w_out, preferred_element_type=jnp.float32)
    normed_two, inverse_two = normalize(mixed)
    hidden_two = (normed_two * gain_two.astype(jnp.float32)).astype(jnp.bfloat16)
    gate = jnp.dot(hidden_two, w_gate, preferred_element_type=jnp.float32)
    upward = jnp.dot(hidden_two, w_up, preferred_element_type=jnp.float32)
    sigma = jax.nn.sigmoid(gate)
    activated = (gate * sigma * upward).astype(jnp.bfloat16)
    output = (mixed + jnp.dot(activated, w_down, preferred_element_type=jnp.float32)).astype(
        jnp.bfloat16
    )
    d_act = jnp.dot(cotangent, w_down.T, preferred_element_type=jnp.float32)
    g_down = jnp.dot(activated.T, cotangent, preferred_element_type=jnp.float32)
    d_gate = (d_act * upward * sigma * (1.0 + gate * (1.0 - sigma))).astype(jnp.bfloat16)
    d_up = (d_act * gate * sigma).astype(jnp.bfloat16)
    g_gate = jnp.dot(hidden_two.T, d_gate, preferred_element_type=jnp.float32)
    g_up = jnp.dot(hidden_two.T, d_up, preferred_element_type=jnp.float32)
    d_hidden_two = jnp.dot(d_gate, w_gate.T, preferred_element_type=jnp.float32) + jnp.dot(
        d_up, w_up.T, preferred_element_type=jnp.float32
    )
    g_gain_two = jnp.sum(d_hidden_two * normed_two, axis=0)
    dn_two = d_hidden_two * gain_two.astype(jnp.float32)
    d_mixed = cotangent.astype(jnp.float32) + inverse_two * (
        dn_two - normed_two * jnp.mean(dn_two * normed_two, axis=-1, keepdims=True)
    )
    d_mixed_b = d_mixed.astype(jnp.bfloat16)
    g_out = jnp.dot(attention_output.T, d_mixed_b, preferred_element_type=jnp.float32)
    attention_output_gradient = jnp.dot(
        d_mixed_b, w_out.T, preferred_element_type=jnp.float32
    ).astype(jnp.bfloat16)
    split_gradient = attention_output_gradient.reshape(
        token_rows, KEYVAL_HEADS, group_width, HEAD_SIZE
    )
    attention_output_split = attention_output.reshape(
        token_rows, KEYVAL_HEADS, group_width, HEAD_SIZE
    )
    softmax_correction = jnp.sum(
        split_gradient.astype(jnp.float32) * attention_output_split.astype(jnp.float32), axis=-1
    ).transpose(1, 2, 0)
    key_back, value_back = (key_all, value_all)
    query_gradient_running = jnp.zeros(
        (token_rows, KEYVAL_HEADS, group_width, HEAD_SIZE), jnp.float32
    )
    key_contributions = []
    value_contributions = []
    for span_start in span_starts:
        key_tensor_split, value_tensor_split, allowed, needed = span_setup(
            span_start, key_back, value_back
        )

        def back_span(carry):
            scores = (
                jnp.einsum(
                    "qgrd,kgd->grqk",
                    query_tensor_split,
                    key_tensor_split,
                    preferred_element_type=jnp.float32,
                )
                * score_scale
            )
            probs = jnp.where(allowed, jnp.exp(scores - lse[..., None]), 0.0)
            probs_b = probs.astype(jnp.bfloat16)
            value_gradient_range = jnp.einsum(
                "pozf,zpom->fpm", probs_b, split_gradient, preferred_element_type=jnp.float32
            )
            d_probs = jnp.einsum(
                "qgrd,kgd->grqk",
                split_gradient,
                value_tensor_split,
                preferred_element_type=jnp.float32,
            )
            score_gradient = (
                probs * (d_probs - softmax_correction[..., None]) * score_scale
            ).astype(jnp.bfloat16)
            new_acc = carry + jnp.einsum(
                "grqk,kgd->qgrd",
                score_gradient,
                key_tensor_split,
                preferred_element_type=jnp.float32,
            )
            key_gradient_range = jnp.einsum(
                "pozf,zpom->fpm",
                score_gradient,
                query_tensor_split,
                preferred_element_type=jnp.float32,
            )
            return (new_acc, key_gradient_range, value_gradient_range)

        def skip_span(carry):
            blank_range = jnp.zeros((range_rows, KEYVAL_HEADS, HEAD_SIZE), jnp.float32)
            return (carry, blank_range, blank_range)

        query_gradient_running, key_gradient_range, value_gradient_range = lax.cond(
            needed, back_span, skip_span, query_gradient_running
        )
        key_contributions.append(key_gradient_range.reshape(range_rows, KEYVAL_HEADS * HEAD_SIZE))
        value_contributions.append(
            value_gradient_range.reshape(range_rows, KEYVAL_HEADS * HEAD_SIZE)
        )
    kv_sum_in = jnp.stack(
        [jnp.concatenate(pair, axis=1) for pair in zip(key_contributions, value_contributions)]
    )
    kv_grad = kv_sum_in[narrow_rank]
    for shift in range(1, narrow_size):
        sender_block = kv_sum_in[lax.rem(narrow_rank + narrow_size - shift, narrow_size)]
        kv_grad = kv_grad + lax.ppermute(
            sender_block,
            "narrow",
            [(source, source - shift) for source in range(shift, narrow_size)],
        )
    key_gradient, value_gradient = kv_grad[:, :kv_width], kv_grad[:, kv_width:]
    d_query = query_gradient_running.reshape(token_rows, QUERY_HEADS * HEAD_SIZE)
    d_query_b = apply_rotary(d_query, token_position, QUERY_HEADS, -1.0).astype(jnp.bfloat16)
    key_gradient_batch = apply_rotary(key_gradient, token_position, KEYVAL_HEADS, -1.0).astype(
        jnp.bfloat16
    )
    value_gradient_batch = value_gradient.astype(jnp.bfloat16)
    g_query = jnp.dot(hidden_one.T, d_query_b, preferred_element_type=jnp.float32)
    g_key_value = jnp.dot(
        hidden_one.T,
        jnp.concatenate([key_gradient_batch, value_gradient_batch], axis=1),
        preferred_element_type=jnp.float32,
    )
    d_hidden_one = (
        jnp.dot(d_query_b, w_query.T, preferred_element_type=jnp.float32)
        + jnp.dot(key_gradient_batch, w_key.T, preferred_element_type=jnp.float32)
        + jnp.dot(value_gradient_batch, w_value.T, preferred_element_type=jnp.float32)
    )
    g_gain_one = jnp.sum(d_hidden_one * normed_one, axis=0)
    dn_one = d_hidden_one * gain_one.astype(jnp.float32)
    d_tokens = (
        d_mixed
        + inverse_one
        * (dn_one - normed_one * jnp.mean(dn_one * normed_one, axis=-1, keepdims=True))
    ).astype(jnp.bfloat16)
    out_and_gains = jnp.concatenate([g_out, g_gain_one[None], g_gain_two[None]], axis=0)
    grad_pieces = lax.psum(
        (g_query, g_key_value, out_and_gains, g_gate, g_up, g_down), ("wide", "narrow")
    )
    out_rows = QUERY_HEADS * HEAD_SIZE
    kv_width_total = KEYVAL_HEADS * HEAD_SIZE
    flat_pieces = [
        (0, 0, None),
        (1, 0, kv_width_total),
        (1, kv_width_total, kv_width_total),
        (2, 0, out_rows),
        (3, 0, None),
        (4, 0, None),
        (5, 0, None),
        (2, out_rows, 2),
    ]

    def shard_of(rank):
        def build(pieces):
            parts = []
            offset = 0
            low, high = rank * shard_len, (rank + 1) * shard_len
            for index, column, width in flat_pieces:
                piece = pieces[index]
                if index == 2:
                    piece = piece[column : column + width]
                elif width is not None:
                    piece = piece[:, column : column + width]
                rows, cols = piece.shape
                size = rows * cols
                start, stop = max(low, offset), min(high, offset + size)
                if start < stop:
                    first_row = (start - offset) // cols
                    last_row = -(-(stop - offset) // cols)
                    block = piece[first_row:last_row].reshape(-1)
                    base = offset + first_row * cols
                    parts.append(block[start - base : stop - base])
                offset = offset + size
            return jnp.concatenate(parts)

        return build

    token_total = token_rows * narrow_size * lax.axis_size("wide")

    def update_of(rank):
        def update(pieces, master, first_moment, second_moment):
            gradient = shard_of(rank)(pieces) * (1.0 / math.sqrt(token_total))
            new_first = beta_one * first_moment + (1.0 - beta_one) * gradient
            new_second = beta_two * second_moment + (1.0 - beta_two) * gradient * gradient
            first_hat = new_first / (1.0 - beta_one**STEP)
            second_hat = new_second / (1.0 - beta_two**STEP)
            entry_index = rank * shard_len + jnp.arange(shard_len, dtype=jnp.int32)
            decay = jnp.where(entry_index < NPARAM - 2 * MODEL_WIDTH, decay_rate, 0.0)
            new_master = master - learn_rate * (
                first_hat / (jnp.sqrt(second_hat) + adam_eps) + decay * master
            )
            return (gradient, new_master, new_first, new_second)

        return update

    gradient, new_master, new_first, new_second = lax.switch(
        narrow_rank,
        [update_of(rank) for rank in range(narrow_size)],
        grad_pieces,
        master,
        first_moment,
        second_moment,
    )
    return (output, d_tokens, gradient, new_master, new_first, new_second)


def solution(mesh):
    in_specs = (
        P(("wide", "narrow"), None),
        P(("wide", "narrow"), None),
        P("wide", None),
        P("narrow"),
        P("narrow"),
        P("narrow"),
    )
    out_specs = (
        P(("wide", "narrow"), None),
        P(("wide", "narrow"), None),
        P("narrow"),
        P("narrow"),
        P("narrow"),
        P("narrow"),
    )
    return jax.shard_map(body, mesh=mesh, in_specs=in_specs, out_specs=out_specs, check_vma=False)
```

```python
import math

import jax
import jax.numpy as jnp
from jax import lax
from jax.experimental import pallas as pl
from jax.experimental.pallas import tpu as pltpu
from jax.sharding import PartitionSpec as P

MODEL_WIDTH = 512
QUERY_HEADS = 15
KEYVAL_HEADS = 5
HEAD_SIZE = 64
FEEDFWD_UNITS = 1280
STEP = 4
NPARAM = 3277824


eps_norm = 1e-05
rope_base = 100000.0
beta_one = 0.9
beta_two = 0.95
learn_rate = 0.03
decay_rate = 0.1
adam_eps = 1e-08
masked_logits = -1e30


def unpack(flat):
    arrangement_list = [
        (MODEL_WIDTH, QUERY_HEADS * HEAD_SIZE),
        (MODEL_WIDTH, KEYVAL_HEADS * HEAD_SIZE),
        (MODEL_WIDTH, KEYVAL_HEADS * HEAD_SIZE),
        (QUERY_HEADS * HEAD_SIZE, MODEL_WIDTH),
        (MODEL_WIDTH, FEEDFWD_UNITS),
        (MODEL_WIDTH, FEEDFWD_UNITS),
        (FEEDFWD_UNITS, MODEL_WIDTH),
        (MODEL_WIDTH,),
        (MODEL_WIDTH,),
    ]
    pieces = []
    offset = 0
    for layout in arrangement_list:
        length = math.prod(layout)
        pieces.append(flat[offset : offset + length].reshape(layout))
        offset = offset + length
    return pieces


def place_tokens(indices, lengths_row):
    seq_ends = jnp.cumsum(lengths_row)
    seq_starts = seq_ends - lengths_row
    member = (indices[:, None] >= seq_starts[None, :]) & (indices[:, None] < seq_ends[None, :])
    numbers = jnp.arange(lengths_row.shape[0], dtype=jnp.int32)
    segment = jnp.sum(jnp.where(member, numbers[None, :], 0), axis=1)
    token_position = indices - jnp.sum(jnp.where(member, seq_starts[None, :], 0), axis=1)
    return (segment, token_position)


def normalize(values):
    inverse_rms = lax.rsqrt(jnp.mean(values * values, axis=-1, keepdims=True) + eps_norm)
    return (values * inverse_rms, inverse_rms)


def apply_rotary(values, token_position, head_count, turn_sign):
    half_dim = HEAD_SIZE // 2
    inverse = rope_base ** (-2.0 * jnp.arange(half_dim, dtype=jnp.float32) / HEAD_SIZE)
    angles = token_position.astype(jnp.float32)[:, None] * inverse[None, :]
    cosine = jnp.cos(angles)[:, None, :]
    sine = turn_sign * jnp.sin(angles)[:, None, :]
    shaped = values.reshape(values.shape[0], head_count, HEAD_SIZE)
    first_half = shaped[:, :, :half_dim]
    second_half = shaped[:, :, half_dim:]
    turned = jnp.concatenate(
        [first_half * cosine - second_half * sine, second_half * cosine + first_half * sine],
        axis=-1,
    )
    return turned.reshape(values.shape)


def gather_kernel(src_ref, out_ref, send_sems, recv_sems):
    narrow = lax.axis_index("narrow")
    wide = lax.axis_index("wide")
    z_lo = narrow // 2
    core = narrow % 2
    z_hi = (wide // 4) % 2
    flipped = wide + 4 - 8 * z_hi
    split = (src_ref.shape[0] // 32) * 16
    halves = [pl.ds(0, split), pl.ds(split, src_ref.shape[0] - split)]
    sibling = (wide, z_lo * 2 + 1 - core)
    across = [(wide, (1 - z_lo) * 2 + c) for c in (0, 1)]
    around = [(flipped, (1 - z_lo) * 2 + c) for c in (0, 1)]
    barrier = pltpu.get_barrier_semaphore()
    for peer in [sibling] + across + around:
        pl.semaphore_signal(barrier, 1, device_id=peer, device_id_type=pl.DeviceIdType.MESH)
    pl.semaphore_wait(barrier, 5)
    sends = [(sibling, 0), (sibling, 1)] + [(p, 0) for p in across] + [(p, 1) for p in around]
    copies = []
    for number, (peer, part) in enumerate(sends):
        rows = halves[part]
        copy = pltpu.make_async_remote_copy(
            src_ref=src_ref.at[rows],
            dst_ref=out_ref.at[narrow, rows],
            send_sem=send_sems.at[number],
            recv_sem=recv_sems.at[narrow, part],
            device_id=peer,
            device_id_type=pl.DeviceIdType.MESH,
        )
        copy.start()
        copies.append(copy)
    out_ref[narrow] = src_ref[...]
    for copy in copies:
        copy.wait_send()
    for step in range(1, 4):
        owner = lax.rem(narrow + step, 4)
        for part in (0, 1):
            rows = halves[part]
            pltpu.make_async_remote_copy(
                src_ref=src_ref.at[rows],
                dst_ref=out_ref.at[owner, rows],
                send_sem=send_sems.at[0],
                recv_sem=recv_sems.at[owner, part],
                device_id=sibling,
                device_id_type=pl.DeviceIdType.MESH,
            ).wait_recv()


def gather_replica(shard_rows):
    count, width = shard_rows.shape
    return pl.pallas_call(
        gather_kernel,
        out_shape=jax.ShapeDtypeStruct((4, count, width), shard_rows.dtype),
        in_specs=[pl.BlockSpec(memory_space=pltpu.VMEM)],
        out_specs=pl.BlockSpec(memory_space=pltpu.VMEM),
        scratch_shapes=[pltpu.SemaphoreType.DMA((6,)), pltpu.SemaphoreType.DMA((4, 2))],
        compiler_params=pltpu.CompilerParams(collective_id=0, has_side_effects=True),
    )(shard_rows)


def keep_carry(carry):
    return carry


def body(tokens, cotangent, lengths, master, first_moment, second_moment):
    token_rows = tokens.shape[0]
    narrow_size = lax.axis_size("narrow")
    group_rows = token_rows * narrow_size
    narrow_rank = lax.axis_index("narrow")
    group_width = QUERY_HEADS // KEYVAL_HEADS
    score_scale = HEAD_SIZE ** (-0.5)
    shard_len = master.shape[0]
    replica = gather_replica(master.astype(jnp.bfloat16).reshape(shard_len // 128, 128)).reshape(-1)
    w_query, w_key, w_value, w_out, w_gate, w_up, w_down, gain_one, gain_two = unpack(replica)
    lengths_row = lengths[0]
    local_index = narrow_rank * token_rows + jnp.arange(token_rows, dtype=jnp.int32)
    segment, token_position = place_tokens(local_index, lengths_row)
    group_index = jnp.arange(group_rows, dtype=jnp.int32)
    key_segment = place_tokens(group_index, lengths_row)[0]
    first_start = local_index[0] - token_position[0]
    last_index = local_index[token_rows - 1]
    range_rows = token_rows
    span_starts = list(range(0, group_rows, range_rows))
    resid = tokens.astype(jnp.float32)
    normed_one, inverse_one = normalize(resid)
    hidden_one = (normed_one * gain_one.astype(jnp.float32)).astype(jnp.bfloat16)
    query = jnp.dot(hidden_one, w_query, preferred_element_type=jnp.float32)
    key_projection = jnp.dot(hidden_one, w_key, preferred_element_type=jnp.float32)
    value_proj = jnp.dot(hidden_one, w_value, preferred_element_type=jnp.float32)
    query_batch = apply_rotary(query, token_position, QUERY_HEADS, 1.0).astype(jnp.bfloat16)
    key_batch = apply_rotary(key_projection, token_position, KEYVAL_HEADS, 1.0).astype(jnp.bfloat16)
    value_batch = value_proj.astype(jnp.bfloat16)
    kv_width = KEYVAL_HEADS * HEAD_SIZE
    kv_all = lax.all_gather(
        jnp.concatenate([key_batch, value_batch], axis=1), "narrow", axis=0, tiled=True
    )
    key_all, value_all = kv_all[:, :kv_width], kv_all[:, kv_width:]
    query_tensor_split = query_batch.reshape(token_rows, KEYVAL_HEADS, group_width, HEAD_SIZE)

    def span_setup(span_start, key_source, value_source):
        key_tensor_split = lax.slice_in_dim(
            key_source, span_start, span_start + range_rows
        ).reshape(range_rows, KEYVAL_HEADS, HEAD_SIZE)
        value_tensor_split = lax.slice_in_dim(
            value_source, span_start, span_start + range_rows
        ).reshape(range_rows, KEYVAL_HEADS, HEAD_SIZE)
        span_segment = lax.slice_in_dim(key_segment, span_start, span_start + range_rows)
        span_index = lax.slice_in_dim(group_index, span_start, span_start + range_rows)
        allowed = (segment[:, None] == span_segment[None, :]) & (
            span_index[None, :] <= local_index[:, None]
        )
        needed = (span_start <= last_index) & (span_start + range_rows - 1 >= first_start)
        return (key_tensor_split, value_tensor_split, allowed[None, None], needed)

    running_maximum = jnp.full((KEYVAL_HEADS, group_width, token_rows), masked_logits, jnp.float32)
    running_denominator = jnp.zeros((KEYVAL_HEADS, group_width, token_rows), jnp.float32)
    for span_start in span_starts:
        key_tensor_split, value_tensor_split, allowed, needed = span_setup(
            span_start, key_all, value_all
        )

        def extend(carry):
            old_top, old_total = carry
            scores = (
                jnp.einsum(
                    "qgrd,kgd->grqk",
                    query_tensor_split,
                    key_tensor_split,
                    preferred_element_type=jnp.float32,
                )
                * score_scale
            )
            new_top = jnp.maximum(
                old_top, jnp.max(jnp.where(allowed, scores, masked_logits), axis=-1)
            )
            span_sum = jnp.sum(
                jnp.where(allowed, jnp.exp(scores - new_top[..., None]), 0.0), axis=-1
            )
            return (new_top, old_total * jnp.exp(old_top - new_top) + span_sum)

        running_maximum, running_denominator = lax.cond(
            needed, extend, keep_carry, (running_maximum, running_denominator)
        )
    lse = running_maximum + jnp.log(running_denominator)
    running_total = jnp.zeros((token_rows, KEYVAL_HEADS, group_width, HEAD_SIZE), jnp.float32)
    for span_start in span_starts:
        key_tensor_split, value_tensor_split, allowed, needed = span_setup(
            span_start, key_all, value_all
        )

        def weigh_values(carry):
            scores = (
                jnp.einsum(
                    "qgrd,kgd->grqk",
                    query_tensor_split,
                    key_tensor_split,
                    preferred_element_type=jnp.float32,
                )
                * score_scale
            )
            probs_b = jnp.where(allowed, jnp.exp(scores - lse[..., None]), 0.0).astype(jnp.bfloat16)
            return carry + jnp.einsum(
                "grqk,kgd->qgrd", probs_b, value_tensor_split, preferred_element_type=jnp.float32
            )

        running_total = lax.cond(needed, weigh_values, keep_carry, running_total)
    attention_output = running_total.reshape(token_rows, QUERY_HEADS * HEAD_SIZE).astype(
        jnp.bfloat16
    )
    mixed = resid + jnp.dot(attention_output, w_out, preferred_element_type=jnp.float32)
    normed_two, inverse_two = normalize(mixed)
    hidden_two = (normed_two * gain_two.astype(jnp.float32)).astype(jnp.bfloat16)
    gate = jnp.dot(hidden_two, w_gate, preferred_element_type=jnp.float32)
    upward = jnp.dot(hidden_two, w_up, preferred_element_type=jnp.float32)
    sigma = jax.nn.sigmoid(gate)
    activated = (gate * sigma * upward).astype(jnp.bfloat16)
    output = (mixed + jnp.dot(activated, w_down, preferred_element_type=jnp.float32)).astype(
        jnp.bfloat16
    )
    d_act = jnp.dot(cotangent, w_down.T, preferred_element_type=jnp.float32)
    g_down = jnp.dot(activated.T, cotangent, preferred_element_type=jnp.float32)
    d_gate = (d_act * upward * sigma * (1.0 + gate * (1.0 - sigma))).astype(jnp.bfloat16)
    d_up = (d_act * gate * sigma).astype(jnp.bfloat16)
    g_gate = jnp.dot(hidden_two.T, d_gate, preferred_element_type=jnp.float32)
    g_up = jnp.dot(hidden_two.T, d_up, preferred_element_type=jnp.float32)
    d_hidden_two = jnp.dot(d_gate, w_gate.T, preferred_element_type=jnp.float32) + jnp.dot(
        d_up, w_up.T, preferred_element_type=jnp.float32
    )
    g_gain_two = jnp.sum(d_hidden_two * normed_two, axis=0)
    dn_two = d_hidden_two * gain_two.astype(jnp.float32)
    d_mixed = cotangent.astype(jnp.float32) + inverse_two * (
        dn_two - normed_two * jnp.mean(dn_two * normed_two, axis=-1, keepdims=True)
    )
    d_mixed_b = d_mixed.astype(jnp.bfloat16)
    g_out = jnp.dot(attention_output.T, d_mixed_b, preferred_element_type=jnp.float32)
    attention_output_gradient = jnp.dot(
        d_mixed_b, w_out.T, preferred_element_type=jnp.float32
    ).astype(jnp.bfloat16)
    split_gradient = attention_output_gradient.reshape(
        token_rows, KEYVAL_HEADS, group_width, HEAD_SIZE
    )
    attention_output_split = attention_output.reshape(
        token_rows, KEYVAL_HEADS, group_width, HEAD_SIZE
    )
    softmax_correction = jnp.sum(
        split_gradient.astype(jnp.float32) * attention_output_split.astype(jnp.float32), axis=-1
    ).transpose(1, 2, 0)
    key_back, value_back = (key_all, value_all)
    query_gradient_running = jnp.zeros(
        (token_rows, KEYVAL_HEADS, group_width, HEAD_SIZE), jnp.float32
    )
    key_contributions = []
    value_contributions = []
    for span_start in span_starts:
        key_tensor_split, value_tensor_split, allowed, needed = span_setup(
            span_start, key_back, value_back
        )

        def back_span(carry):
            scores = (
                jnp.einsum(
                    "qgrd,kgd->grqk",
                    query_tensor_split,
                    key_tensor_split,
                    preferred_element_type=jnp.float32,
                )
                * score_scale
            )
            probs = jnp.where(allowed, jnp.exp(scores - lse[..., None]), 0.0)
            probs_b = probs.astype(jnp.bfloat16)
            value_gradient_range = jnp.einsum(
                "pozf,zpom->fpm", probs_b, split_gradient, preferred_element_type=jnp.float32
            )
            d_probs = jnp.einsum(
                "qgrd,kgd->grqk",
                split_gradient,
                value_tensor_split,
                preferred_element_type=jnp.float32,
            )
            score_gradient = (
                probs * (d_probs - softmax_correction[..., None]) * score_scale
            ).astype(jnp.bfloat16)
            new_acc = carry + jnp.einsum(
                "grqk,kgd->qgrd",
                score_gradient,
                key_tensor_split,
                preferred_element_type=jnp.float32,
            )
            key_gradient_range = jnp.einsum(
                "pozf,zpom->fpm",
                score_gradient,
                query_tensor_split,
                preferred_element_type=jnp.float32,
            )
            return (new_acc, key_gradient_range, value_gradient_range)

        def skip_span(carry):
            blank_range = jnp.zeros((range_rows, KEYVAL_HEADS, HEAD_SIZE), jnp.float32)
            return (carry, blank_range, blank_range)

        query_gradient_running, key_gradient_range, value_gradient_range = lax.cond(
            needed, back_span, skip_span, query_gradient_running
        )
        key_contributions.append(key_gradient_range.reshape(range_rows, KEYVAL_HEADS * HEAD_SIZE))
        value_contributions.append(
            value_gradient_range.reshape(range_rows, KEYVAL_HEADS * HEAD_SIZE)
        )
    kv_sum_in = jnp.stack(
        [jnp.concatenate(pair, axis=1) for pair in zip(key_contributions, value_contributions)]
    )
    kv_grad = kv_sum_in[narrow_rank]
    for shift in range(1, narrow_size):
        sender_block = kv_sum_in[lax.rem(narrow_rank + narrow_size - shift, narrow_size)]
        kv_grad = kv_grad + lax.ppermute(
            sender_block.astype(jnp.bfloat16),
            "narrow",
            [(source, source - shift) for source in range(shift, narrow_size)],
        ).astype(jnp.float32)
    key_gradient, value_gradient = kv_grad[:, :kv_width], kv_grad[:, kv_width:]
    d_query = query_gradient_running.reshape(token_rows, QUERY_HEADS * HEAD_SIZE)
    d_query_b = apply_rotary(d_query, token_position, QUERY_HEADS, -1.0).astype(jnp.bfloat16)
    key_gradient_batch = apply_rotary(key_gradient, token_position, KEYVAL_HEADS, -1.0).astype(
        jnp.bfloat16
    )
    value_gradient_batch = value_gradient.astype(jnp.bfloat16)
    g_query = jnp.dot(hidden_one.T, d_query_b, preferred_element_type=jnp.float32)
    g_key_value = jnp.dot(
        hidden_one.T,
        jnp.concatenate([key_gradient_batch, value_gradient_batch], axis=1),
        preferred_element_type=jnp.float32,
    )
    d_hidden_one = (
        jnp.dot(d_query_b, w_query.T, preferred_element_type=jnp.float32)
        + jnp.dot(key_gradient_batch, w_key.T, preferred_element_type=jnp.float32)
        + jnp.dot(value_gradient_batch, w_value.T, preferred_element_type=jnp.float32)
    )
    g_gain_one = jnp.sum(d_hidden_one * normed_one, axis=0)
    dn_one = d_hidden_one * gain_one.astype(jnp.float32)
    d_tokens = (
        d_mixed
        + inverse_one
        * (dn_one - normed_one * jnp.mean(dn_one * normed_one, axis=-1, keepdims=True))
    ).astype(jnp.bfloat16)
    out_and_gains = jnp.concatenate([g_out, g_gain_one[None], g_gain_two[None]], axis=0)
    grad_pieces = lax.psum(
        (g_query, g_key_value, out_and_gains, g_gate, g_up, g_down), ("wide", "narrow")
    )
    out_rows = QUERY_HEADS * HEAD_SIZE
    kv_width_total = KEYVAL_HEADS * HEAD_SIZE
    flat_pieces = [
        (0, 0, None),
        (1, 0, kv_width_total),
        (1, kv_width_total, kv_width_total),
        (2, 0, out_rows),
        (3, 0, None),
        (4, 0, None),
        (5, 0, None),
        (2, out_rows, 2),
    ]

    def shard_of(rank):
        def build(pieces):
            parts = []
            offset = 0
            low, high = rank * shard_len, (rank + 1) * shard_len
            for index, column, width in flat_pieces:
                piece = pieces[index]
                if index == 2:
                    piece = piece[column : column + width]
                elif width is not None:
                    piece = piece[:, column : column + width]
                rows, cols = piece.shape
                size = rows * cols
                start, stop = max(low, offset), min(high, offset + size)
                if start < stop:
                    first_row = (start - offset) // cols
                    last_row = -(-(stop - offset) // cols)
                    block = piece[first_row:last_row].reshape(-1)
                    base = offset + first_row * cols
                    parts.append(block[start - base : stop - base])
                offset = offset + size
            return jnp.concatenate(parts)

        return build

    summed = lax.switch(narrow_rank, [shard_of(rank) for rank in range(narrow_size)], grad_pieces)
    token_total = token_rows * narrow_size * lax.axis_size("wide")
    gradient = summed * (1.0 / math.sqrt(token_total))
    new_first = beta_one * first_moment + (1.0 - beta_one) * gradient
    new_second = beta_two * second_moment + (1.0 - beta_two) * gradient * gradient
    first_hat = new_first / (1.0 - beta_one**STEP)
    second_hat = new_second / (1.0 - beta_two**STEP)
    entry_index = narrow_rank * shard_len + jnp.arange(shard_len, dtype=jnp.int32)
    decay = jnp.where(entry_index < NPARAM - 2 * MODEL_WIDTH, decay_rate, 0.0)
    new_master = master - learn_rate * (
        first_hat / (jnp.sqrt(second_hat) + adam_eps) + decay * master
    )
    return (output, d_tokens, gradient, new_master, new_first, new_second)


def solution(mesh):
    in_specs = (
        P(("wide", "narrow"), None),
        P(("wide", "narrow"), None),
        P("wide", None),
        P("narrow"),
        P("narrow"),
        P("narrow"),
    )
    out_specs = (
        P(("wide", "narrow"), None),
        P(("wide", "narrow"), None),
        P("narrow"),
        P("narrow"),
        P("narrow"),
        P("narrow"),
    )
    return jax.shard_map(body, mesh=mesh, in_specs=in_specs, out_specs=out_specs, check_vma=False)
```

```python
import math

import jax
import jax.numpy as jnp
from jax import lax
from jax.experimental import pallas as pl
from jax.experimental.pallas import tpu as pltpu
from jax.sharding import PartitionSpec as P

MODEL_WIDTH = 512
QUERY_HEADS = 15
KEYVAL_HEADS = 5
HEAD_SIZE = 64
FEEDFWD_UNITS = 1280
STEP = 4
NPARAM = 3277824


eps_norm = 1e-05
rope_base = 100000.0
beta_one = 0.9
beta_two = 0.95
learn_rate = 0.03
decay_rate = 0.1
adam_eps = 1e-08
masked_logits = -1e30


def unpack(flat):
    arrangement_list = [
        (MODEL_WIDTH, QUERY_HEADS * HEAD_SIZE),
        (MODEL_WIDTH, KEYVAL_HEADS * HEAD_SIZE),
        (MODEL_WIDTH, KEYVAL_HEADS * HEAD_SIZE),
        (QUERY_HEADS * HEAD_SIZE, MODEL_WIDTH),
        (MODEL_WIDTH, FEEDFWD_UNITS),
        (MODEL_WIDTH, FEEDFWD_UNITS),
        (FEEDFWD_UNITS, MODEL_WIDTH),
        (MODEL_WIDTH,),
        (MODEL_WIDTH,),
    ]
    pieces = []
    offset = 0
    for layout in arrangement_list:
        length = math.prod(layout)
        pieces.append(flat[offset : offset + length].reshape(layout))
        offset = offset + length
    return pieces


def place_tokens(indices, lengths_row):
    seq_ends = jnp.cumsum(lengths_row)
    seq_starts = seq_ends - lengths_row
    member = (indices[:, None] >= seq_starts[None, :]) & (indices[:, None] < seq_ends[None, :])
    numbers = jnp.arange(lengths_row.shape[0], dtype=jnp.int32)
    segment = jnp.sum(jnp.where(member, numbers[None, :], 0), axis=1)
    token_position = indices - jnp.sum(jnp.where(member, seq_starts[None, :], 0), axis=1)
    return (segment, token_position)


def normalize(values):
    inverse_rms = lax.rsqrt(jnp.mean(values * values, axis=-1, keepdims=True) + eps_norm)
    return (values * inverse_rms, inverse_rms)


def apply_rotary(values, token_position, head_count, turn_sign):
    half_dim = HEAD_SIZE // 2
    inverse = rope_base ** (-2.0 * jnp.arange(half_dim, dtype=jnp.float32) / HEAD_SIZE)
    angles = token_position.astype(jnp.float32)[:, None] * inverse[None, :]
    cosine = jnp.cos(angles)[:, None, :]
    sine = turn_sign * jnp.sin(angles)[:, None, :]
    shaped = values.reshape(values.shape[0], head_count, HEAD_SIZE)
    first_half = shaped[:, :, :half_dim]
    second_half = shaped[:, :, half_dim:]
    turned = jnp.concatenate(
        [first_half * cosine - second_half * sine, second_half * cosine + first_half * sine],
        axis=-1,
    )
    return turned.reshape(values.shape)


def gather_kernel(src_ref, out_ref, send_sems, recv_sems):
    narrow = lax.axis_index("narrow")
    wide = lax.axis_index("wide")
    z_lo = narrow // 2
    core = narrow % 2
    z_hi = (wide // 4) % 2
    flipped = wide + 4 - 8 * z_hi
    split = (src_ref.shape[0] // 32) * 16
    halves = [pl.ds(0, split), pl.ds(split, src_ref.shape[0] - split)]
    sibling = (wide, z_lo * 2 + 1 - core)
    across = [(wide, (1 - z_lo) * 2 + c) for c in (0, 1)]
    around = [(flipped, (1 - z_lo) * 2 + c) for c in (0, 1)]
    barrier = pltpu.get_barrier_semaphore()
    for peer in [sibling] + across + around:
        pl.semaphore_signal(barrier, 1, device_id=peer, device_id_type=pl.DeviceIdType.MESH)
    pl.semaphore_wait(barrier, 5)
    sends = [(sibling, 0), (sibling, 1)] + [(p, 0) for p in across] + [(p, 1) for p in around]
    copies = []
    for number, (peer, part) in enumerate(sends):
        rows = halves[part]
        copy = pltpu.make_async_remote_copy(
            src_ref=src_ref.at[rows],
            dst_ref=out_ref.at[narrow, rows],
            send_sem=send_sems.at[number],
            recv_sem=recv_sems.at[narrow, part],
            device_id=peer,
            device_id_type=pl.DeviceIdType.MESH,
        )
        copy.start()
        copies.append(copy)
    out_ref[narrow] = src_ref[...]
    for copy in copies:
        copy.wait_send()
    for step in range(1, 4):
        owner = lax.rem(narrow + step, 4)
        for part in (0, 1):
            rows = halves[part]
            pltpu.make_async_remote_copy(
                src_ref=src_ref.at[rows],
                dst_ref=out_ref.at[owner, rows],
                send_sem=send_sems.at[0],
                recv_sem=recv_sems.at[owner, part],
                device_id=sibling,
                device_id_type=pl.DeviceIdType.MESH,
            ).wait_recv()


def gather_replica(shard_rows):
    count, width = shard_rows.shape
    return pl.pallas_call(
        gather_kernel,
        out_shape=jax.ShapeDtypeStruct((4, count, width), shard_rows.dtype),
        in_specs=[pl.BlockSpec(memory_space=pltpu.VMEM)],
        out_specs=pl.BlockSpec(memory_space=pltpu.VMEM),
        scratch_shapes=[pltpu.SemaphoreType.DMA((6,)), pltpu.SemaphoreType.DMA((4, 2))],
        compiler_params=pltpu.CompilerParams(collective_id=0, has_side_effects=True),
    )(shard_rows)


def keep_carry(carry):
    return carry


def body(tokens, cotangent, lengths, master, first_moment, second_moment):
    token_rows = tokens.shape[0]
    narrow_size = lax.axis_size("narrow")
    group_rows = token_rows * narrow_size
    narrow_rank = lax.axis_index("narrow")
    group_width = QUERY_HEADS // KEYVAL_HEADS
    score_scale = HEAD_SIZE ** (-0.5)
    shard_len = master.shape[0]
    replica = gather_replica(master.astype(jnp.bfloat16).reshape(shard_len // 128, 128)).reshape(-1)
    w_query, w_key, w_value, w_out, w_gate, w_up, w_down, gain_one, gain_two = unpack(replica)
    lengths_row = lengths[0]
    local_index = narrow_rank * token_rows + jnp.arange(token_rows, dtype=jnp.int32)
    segment, token_position = place_tokens(local_index, lengths_row)
    group_index = jnp.arange(group_rows, dtype=jnp.int32)
    key_segment = place_tokens(group_index, lengths_row)[0]
    first_start = local_index[0] - token_position[0]
    last_index = local_index[token_rows - 1]
    range_rows = token_rows
    span_starts = list(range(0, group_rows, range_rows))
    resid = tokens.astype(jnp.float32)
    normed_one, inverse_one = normalize(resid)
    hidden_one = (normed_one * gain_one.astype(jnp.float32)).astype(jnp.bfloat16)
    query = jnp.dot(hidden_one, w_query, preferred_element_type=jnp.float32)
    key_projection = jnp.dot(hidden_one, w_key, preferred_element_type=jnp.float32)
    value_proj = jnp.dot(hidden_one, w_value, preferred_element_type=jnp.float32)
    query_batch = apply_rotary(query, token_position, QUERY_HEADS, 1.0).astype(jnp.bfloat16)
    key_batch = apply_rotary(key_projection, token_position, KEYVAL_HEADS, 1.0).astype(jnp.bfloat16)
    value_batch = value_proj.astype(jnp.bfloat16)
    kv_width = KEYVAL_HEADS * HEAD_SIZE
    kv_all = lax.all_gather(
        jnp.concatenate([key_batch, value_batch], axis=1), "narrow", axis=0, tiled=True
    )
    key_all, value_all = kv_all[:, :kv_width], kv_all[:, kv_width:]
    query_tensor_split = query_batch.reshape(token_rows, KEYVAL_HEADS, group_width, HEAD_SIZE)

    def span_setup(span_start, key_source, value_source):
        key_tensor_split = lax.slice_in_dim(
            key_source, span_start, span_start + range_rows
        ).reshape(range_rows, KEYVAL_HEADS, HEAD_SIZE)
        value_tensor_split = lax.slice_in_dim(
            value_source, span_start, span_start + range_rows
        ).reshape(range_rows, KEYVAL_HEADS, HEAD_SIZE)
        span_segment = lax.slice_in_dim(key_segment, span_start, span_start + range_rows)
        span_index = lax.slice_in_dim(group_index, span_start, span_start + range_rows)
        allowed = (segment[:, None] == span_segment[None, :]) & (
            span_index[None, :] <= local_index[:, None]
        )
        needed = (span_start <= last_index) & (span_start + range_rows - 1 >= first_start)
        return (key_tensor_split, value_tensor_split, allowed[None, None], needed)

    running_maximum = jnp.full((KEYVAL_HEADS, group_width, token_rows), masked_logits, jnp.float32)
    running_denominator = jnp.zeros((KEYVAL_HEADS, group_width, token_rows), jnp.float32)
    for span_start in span_starts:
        key_tensor_split, value_tensor_split, allowed, needed = span_setup(
            span_start, key_all, value_all
        )

        def extend(carry):
            old_top, old_total = carry
            scores = (
                jnp.einsum(
                    "qgrd,kgd->grqk",
                    query_tensor_split,
                    key_tensor_split,
                    preferred_element_type=jnp.float32,
                )
                * score_scale
            )
            new_top = jnp.maximum(
                old_top, jnp.max(jnp.where(allowed, scores, masked_logits), axis=-1)
            )
            span_sum = jnp.sum(
                jnp.where(allowed, jnp.exp(scores - new_top[..., None]), 0.0), axis=-1
            )
            return (new_top, old_total * jnp.exp(old_top - new_top) + span_sum)

        running_maximum, running_denominator = lax.cond(
            needed, extend, keep_carry, (running_maximum, running_denominator)
        )
    lse = running_maximum + jnp.log(running_denominator)
    running_total = jnp.zeros((token_rows, KEYVAL_HEADS, group_width, HEAD_SIZE), jnp.float32)
    for span_start in span_starts:
        key_tensor_split, value_tensor_split, allowed, needed = span_setup(
            span_start, key_all, value_all
        )

        def weigh_values(carry):
            scores = (
                jnp.einsum(
                    "qgrd,kgd->grqk",
                    query_tensor_split,
                    key_tensor_split,
                    preferred_element_type=jnp.float32,
                )
                * score_scale
            )
            probs_b = jnp.where(allowed, jnp.exp(scores - lse[..., None]), 0.0).astype(jnp.bfloat16)
            return carry + jnp.einsum(
                "grqk,kgd->qgrd", probs_b, value_tensor_split, preferred_element_type=jnp.float32
            )

        running_total = lax.cond(needed, weigh_values, keep_carry, running_total)
    attention_output = running_total.reshape(token_rows, QUERY_HEADS * HEAD_SIZE).astype(
        jnp.bfloat16
    )
    mixed = resid + jnp.dot(attention_output, w_out, preferred_element_type=jnp.float32)
    normed_two, inverse_two = normalize(mixed)
    hidden_two = (normed_two * gain_two.astype(jnp.float32)).astype(jnp.bfloat16)
    gate = jnp.dot(hidden_two, w_gate, preferred_element_type=jnp.float32)
    upward = jnp.dot(hidden_two, w_up, preferred_element_type=jnp.float32)
    sigma = jax.nn.sigmoid(gate)
    activated = (gate * sigma * upward).astype(jnp.bfloat16)
    output = (mixed + jnp.dot(activated, w_down, preferred_element_type=jnp.float32)).astype(
        jnp.bfloat16
    )
    d_act = jnp.dot(cotangent, w_down.T, preferred_element_type=jnp.float32)
    g_down = jnp.dot(activated.T, cotangent, preferred_element_type=jnp.float32)
    d_gate = (d_act * upward * sigma * (1.0 + gate * (1.0 - sigma))).astype(jnp.bfloat16)
    d_up = (d_act * gate * sigma).astype(jnp.bfloat16)
    g_gate = jnp.dot(hidden_two.T, d_gate, preferred_element_type=jnp.float32)
    g_up = jnp.dot(hidden_two.T, d_up, preferred_element_type=jnp.float32)
    d_hidden_two = jnp.dot(d_gate, w_gate.T, preferred_element_type=jnp.float32) + jnp.dot(
        d_up, w_up.T, preferred_element_type=jnp.float32
    )
    g_gain_two = jnp.sum(d_hidden_two * normed_two, axis=0)
    dn_two = d_hidden_two * gain_two.astype(jnp.float32)
    d_mixed = cotangent.astype(jnp.float32) + inverse_two * (
        dn_two - normed_two * jnp.mean(dn_two * normed_two, axis=-1, keepdims=True)
    )
    d_mixed_b = d_mixed.astype(jnp.bfloat16)
    g_out_rows = jnp.dot(
        jnp.pad(attention_output, ((0, 0), (0, 2))).T, d_mixed_b, preferred_element_type=jnp.float32
    )
    attention_output_gradient = jnp.dot(
        d_mixed_b, w_out.T, preferred_element_type=jnp.float32
    ).astype(jnp.bfloat16)
    split_gradient = attention_output_gradient.reshape(
        token_rows, KEYVAL_HEADS, group_width, HEAD_SIZE
    )
    attention_output_split = attention_output.reshape(
        token_rows, KEYVAL_HEADS, group_width, HEAD_SIZE
    )
    softmax_correction = jnp.sum(
        split_gradient.astype(jnp.float32) * attention_output_split.astype(jnp.float32), axis=-1
    ).transpose(1, 2, 0)
    key_back, value_back = (key_all, value_all)
    query_gradient_running = jnp.zeros(
        (token_rows, KEYVAL_HEADS, group_width, HEAD_SIZE), jnp.float32
    )
    key_contributions = []
    value_contributions = []
    for span_start in span_starts:
        key_tensor_split, value_tensor_split, allowed, needed = span_setup(
            span_start, key_back, value_back
        )

        def back_span(carry):
            scores = (
                jnp.einsum(
                    "qgrd,kgd->grqk",
                    query_tensor_split,
                    key_tensor_split,
                    preferred_element_type=jnp.float32,
                )
                * score_scale
            )
            probs = jnp.where(allowed, jnp.exp(scores - lse[..., None]), 0.0)
            probs_b = probs.astype(jnp.bfloat16)
            value_gradient_range = jnp.einsum(
                "pozf,zpom->fpm", probs_b, split_gradient, preferred_element_type=jnp.float32
            )
            d_probs = jnp.einsum(
                "qgrd,kgd->grqk",
                split_gradient,
                value_tensor_split,
                preferred_element_type=jnp.float32,
            )
            score_gradient = (
                probs * (d_probs - softmax_correction[..., None]) * score_scale
            ).astype(jnp.bfloat16)
            new_acc = carry + jnp.einsum(
                "grqk,kgd->qgrd",
                score_gradient,
                key_tensor_split,
                preferred_element_type=jnp.float32,
            )
            key_gradient_range = jnp.einsum(
                "pozf,zpom->fpm",
                score_gradient,
                query_tensor_split,
                preferred_element_type=jnp.float32,
            )
            return (new_acc, key_gradient_range, value_gradient_range)

        def skip_span(carry):
            blank_range = jnp.zeros((range_rows, KEYVAL_HEADS, HEAD_SIZE), jnp.float32)
            return (carry, blank_range, blank_range)

        query_gradient_running, key_gradient_range, value_gradient_range = lax.cond(
            needed, back_span, skip_span, query_gradient_running
        )
        key_contributions.append(key_gradient_range.reshape(range_rows, KEYVAL_HEADS * HEAD_SIZE))
        value_contributions.append(
            value_gradient_range.reshape(range_rows, KEYVAL_HEADS * HEAD_SIZE)
        )
    kv_sum_in = jnp.stack(
        [jnp.concatenate(pair, axis=1) for pair in zip(key_contributions, value_contributions)]
    )
    kv_grad = kv_sum_in[narrow_rank]
    for shift in range(1, narrow_size):
        sender_block = kv_sum_in[lax.rem(narrow_rank + narrow_size - shift, narrow_size)]
        kv_grad = kv_grad + lax.ppermute(
            sender_block.astype(jnp.bfloat16),
            "narrow",
            [(source, source - shift) for source in range(shift, narrow_size)],
        ).astype(jnp.float32)
    key_gradient, value_gradient = kv_grad[:, :kv_width], kv_grad[:, kv_width:]
    d_query = query_gradient_running.reshape(token_rows, QUERY_HEADS * HEAD_SIZE)
    d_query_b = apply_rotary(d_query, token_position, QUERY_HEADS, -1.0).astype(jnp.bfloat16)
    key_gradient_batch = apply_rotary(key_gradient, token_position, KEYVAL_HEADS, -1.0).astype(
        jnp.bfloat16
    )
    value_gradient_batch = value_gradient.astype(jnp.bfloat16)
    g_query = jnp.dot(hidden_one.T, d_query_b, preferred_element_type=jnp.float32)
    g_key_value = jnp.dot(
        hidden_one.T,
        jnp.concatenate([key_gradient_batch, value_gradient_batch], axis=1),
        preferred_element_type=jnp.float32,
    )
    d_hidden_one = (
        jnp.dot(d_query_b, w_query.T, preferred_element_type=jnp.float32)
        + jnp.dot(key_gradient_batch, w_key.T, preferred_element_type=jnp.float32)
        + jnp.dot(value_gradient_batch, w_value.T, preferred_element_type=jnp.float32)
    )
    g_gain_one = jnp.sum(d_hidden_one * normed_one, axis=0)
    dn_one = d_hidden_one * gain_one.astype(jnp.float32)
    d_tokens = (
        d_mixed
        + inverse_one
        * (dn_one - normed_one * jnp.mean(dn_one * normed_one, axis=-1, keepdims=True))
    ).astype(jnp.bfloat16)
    out_and_gains = lax.dynamic_update_slice(
        g_out_rows, jnp.stack([g_gain_one, g_gain_two]), (QUERY_HEADS * HEAD_SIZE, 0)
    )
    grad_pieces = lax.psum(
        (g_query, g_key_value, out_and_gains, g_gate, g_up, g_down), ("wide", "narrow")
    )
    out_rows = QUERY_HEADS * HEAD_SIZE
    kv_width_total = KEYVAL_HEADS * HEAD_SIZE
    flat_pieces = [
        (0, 0, None),
        (1, 0, kv_width_total),
        (1, kv_width_total, kv_width_total),
        (2, 0, out_rows),
        (3, 0, None),
        (4, 0, None),
        (5, 0, None),
        (2, out_rows, 2),
    ]

    def shard_of(rank):
        def build(pieces):
            parts = []
            offset = 0
            low, high = rank * shard_len, (rank + 1) * shard_len
            for index, column, width in flat_pieces:
                piece = pieces[index]
                if index == 2:
                    piece = piece[column : column + width]
                elif width is not None:
                    piece = piece[:, column : column + width]
                rows, cols = piece.shape
                size = rows * cols
                start, stop = max(low, offset), min(high, offset + size)
                if start < stop:
                    first_row = (start - offset) // cols
                    last_row = -(-(stop - offset) // cols)
                    block = piece[first_row:last_row].reshape(-1)
                    base = offset + first_row * cols
                    parts.append(block[start - base : stop - base])
                offset = offset + size
            return jnp.concatenate(parts)

        return build

    summed = lax.switch(narrow_rank, [shard_of(rank) for rank in range(narrow_size)], grad_pieces)
    token_total = token_rows * narrow_size * lax.axis_size("wide")
    gradient = summed * (1.0 / math.sqrt(token_total))
    new_first = beta_one * first_moment + (1.0 - beta_one) * gradient
    new_second = beta_two * second_moment + (1.0 - beta_two) * gradient * gradient
    first_hat = new_first / (1.0 - beta_one**STEP)
    second_hat = new_second / (1.0 - beta_two**STEP)
    entry_index = narrow_rank * shard_len + jnp.arange(shard_len, dtype=jnp.int32)
    decay = jnp.where(entry_index < NPARAM - 2 * MODEL_WIDTH, decay_rate, 0.0)
    new_master = master - learn_rate * (
        first_hat / (jnp.sqrt(second_hat) + adam_eps) + decay * master
    )
    return (output, d_tokens, gradient, new_master, new_first, new_second)


def solution(mesh):
    in_specs = (
        P(("wide", "narrow"), None),
        P(("wide", "narrow"), None),
        P("wide", None),
        P("narrow"),
        P("narrow"),
        P("narrow"),
    )
    out_specs = (
        P(("wide", "narrow"), None),
        P(("wide", "narrow"), None),
        P("narrow"),
        P("narrow"),
        P("narrow"),
        P("narrow"),
    )
    return jax.shard_map(body, mesh=mesh, in_specs=in_specs, out_specs=out_specs, check_vma=False)
```

```python
import math

import jax
import jax.numpy as jnp
from jax import lax
from jax.experimental import pallas as pl
from jax.experimental.pallas import tpu as pltpu
from jax.sharding import PartitionSpec as P

MODEL_WIDTH = 512
QUERY_HEADS = 15
KEYVAL_HEADS = 5
HEAD_SIZE = 64
FEEDFWD_UNITS = 1280
STEP = 4
NPARAM = 3277824


eps_norm = 1e-05
rope_base = 100000.0
beta_one = 0.9
beta_two = 0.95
learn_rate = 0.03
decay_rate = 0.1
adam_eps = 1e-08
masked_logits = -1e30


def unpack(flat):
    arrangement_list = [
        (MODEL_WIDTH, QUERY_HEADS * HEAD_SIZE),
        (MODEL_WIDTH, KEYVAL_HEADS * HEAD_SIZE),
        (MODEL_WIDTH, KEYVAL_HEADS * HEAD_SIZE),
        (QUERY_HEADS * HEAD_SIZE, MODEL_WIDTH),
        (MODEL_WIDTH, FEEDFWD_UNITS),
        (MODEL_WIDTH, FEEDFWD_UNITS),
        (FEEDFWD_UNITS, MODEL_WIDTH),
        (MODEL_WIDTH,),
        (MODEL_WIDTH,),
    ]
    pieces = []
    offset = 0
    for layout in arrangement_list:
        length = math.prod(layout)
        pieces.append(flat[offset : offset + length].reshape(layout))
        offset = offset + length
    return pieces


def place_tokens(indices, lengths_row):
    seq_ends = jnp.cumsum(lengths_row)
    seq_starts = seq_ends - lengths_row
    member = (indices[:, None] >= seq_starts[None, :]) & (indices[:, None] < seq_ends[None, :])
    numbers = jnp.arange(lengths_row.shape[0], dtype=jnp.int32)
    segment = jnp.sum(jnp.where(member, numbers[None, :], 0), axis=1)
    token_position = indices - jnp.sum(jnp.where(member, seq_starts[None, :], 0), axis=1)
    return (segment, token_position)


def normalize(values):
    inverse_rms = lax.rsqrt(jnp.mean(values * values, axis=-1, keepdims=True) + eps_norm)
    return (values * inverse_rms, inverse_rms)


def apply_rotary(values, token_position, head_count, turn_sign):
    half_dim = HEAD_SIZE // 2
    inverse = rope_base ** (-2.0 * jnp.arange(half_dim, dtype=jnp.float32) / HEAD_SIZE)
    angles = token_position.astype(jnp.float32)[:, None] * inverse[None, :]
    cosine = jnp.cos(angles)[:, None, :]
    sine = turn_sign * jnp.sin(angles)[:, None, :]
    shaped = values.reshape(values.shape[0], head_count, HEAD_SIZE)
    first_half = shaped[:, :, :half_dim]
    second_half = shaped[:, :, half_dim:]
    turned = jnp.concatenate(
        [first_half * cosine - second_half * sine, second_half * cosine + first_half * sine],
        axis=-1,
    )
    return turned.reshape(values.shape)


def gather_kernel(src_ref, out_ref, send_sems, recv_sems):
    narrow = lax.axis_index("narrow")
    wide = lax.axis_index("wide")
    z_lo = narrow // 2
    core = narrow % 2
    z_hi = (wide // 4) % 2
    flipped = wide + 4 - 8 * z_hi
    split = (src_ref.shape[0] // 32) * 16
    halves = [pl.ds(0, split), pl.ds(split, src_ref.shape[0] - split)]
    sibling = (wide, z_lo * 2 + 1 - core)
    across = [(wide, (1 - z_lo) * 2 + c) for c in (0, 1)]
    around = [(flipped, (1 - z_lo) * 2 + c) for c in (0, 1)]
    barrier = pltpu.get_barrier_semaphore()
    for peer in [sibling] + across + around:
        pl.semaphore_signal(barrier, 1, device_id=peer, device_id_type=pl.DeviceIdType.MESH)
    pl.semaphore_wait(barrier, 5)
    sends = [(sibling, 0), (sibling, 1)] + [(p, 0) for p in across] + [(p, 1) for p in around]
    copies = []
    for number, (peer, part) in enumerate(sends):
        rows = halves[part]
        copy = pltpu.make_async_remote_copy(
            src_ref=src_ref.at[rows],
            dst_ref=out_ref.at[narrow, rows],
            send_sem=send_sems.at[number],
            recv_sem=recv_sems.at[narrow, part],
            device_id=peer,
            device_id_type=pl.DeviceIdType.MESH,
        )
        copy.start()
        copies.append(copy)
    out_ref[narrow] = src_ref[...]
    for copy in copies:
        copy.wait_send()
    for step in range(1, 4):
        owner = lax.rem(narrow + step, 4)
        for part in (0, 1):
            rows = halves[part]
            pltpu.make_async_remote_copy(
                src_ref=src_ref.at[rows],
                dst_ref=out_ref.at[owner, rows],
                send_sem=send_sems.at[0],
                recv_sem=recv_sems.at[owner, part],
                device_id=sibling,
                device_id_type=pl.DeviceIdType.MESH,
            ).wait_recv()


def gather_replica(shard_rows):
    count, width = shard_rows.shape
    return pl.pallas_call(
        gather_kernel,
        out_shape=jax.ShapeDtypeStruct((4, count, width), shard_rows.dtype),
        in_specs=[pl.BlockSpec(memory_space=pltpu.VMEM)],
        out_specs=pl.BlockSpec(memory_space=pltpu.VMEM),
        scratch_shapes=[pltpu.SemaphoreType.DMA((6,)), pltpu.SemaphoreType.DMA((4, 2))],
        compiler_params=pltpu.CompilerParams(collective_id=0, has_side_effects=True),
    )(shard_rows)


def keep_carry(carry):
    return carry


def body(tokens, cotangent, lengths, master, first_moment, second_moment):
    token_rows = tokens.shape[0]
    narrow_size = lax.axis_size("narrow")
    group_rows = token_rows * narrow_size
    narrow_rank = lax.axis_index("narrow")
    group_width = QUERY_HEADS // KEYVAL_HEADS
    score_scale = HEAD_SIZE ** (-0.5)
    shard_len = master.shape[0]
    replica = gather_replica(master.astype(jnp.bfloat16).reshape(shard_len // 128, 128)).reshape(-1)
    w_query, w_key, w_value, w_out, w_gate, w_up, w_down, gain_one, gain_two = unpack(replica)
    lengths_row = lengths[0]
    local_index = narrow_rank * token_rows + jnp.arange(token_rows, dtype=jnp.int32)
    segment, token_position = place_tokens(local_index, lengths_row)
    group_index = jnp.arange(group_rows, dtype=jnp.int32)
    key_segment = place_tokens(group_index, lengths_row)[0]
    first_start = local_index[0] - token_position[0]
    last_index = local_index[token_rows - 1]
    range_rows = token_rows
    span_starts = list(range(0, group_rows, range_rows))
    resid = tokens.astype(jnp.float32)
    normed_one, inverse_one = normalize(resid)
    hidden_one = (normed_one * gain_one.astype(jnp.float32)).astype(jnp.bfloat16)
    query = jnp.dot(hidden_one, w_query, preferred_element_type=jnp.float32)
    key_projection = jnp.dot(hidden_one, w_key, preferred_element_type=jnp.float32)
    value_proj = jnp.dot(hidden_one, w_value, preferred_element_type=jnp.float32)
    query_batch = apply_rotary(query, token_position, QUERY_HEADS, 1.0).astype(jnp.bfloat16)
    key_batch = apply_rotary(key_projection, token_position, KEYVAL_HEADS, 1.0).astype(jnp.bfloat16)
    value_batch = value_proj.astype(jnp.bfloat16)
    kv_width = KEYVAL_HEADS * HEAD_SIZE
    kv_all = lax.all_gather(
        jnp.concatenate([key_batch, value_batch], axis=1), "narrow", axis=0, tiled=True
    )
    key_all, value_all = kv_all[:, :kv_width], kv_all[:, kv_width:]
    query_tensor_split = query_batch.reshape(token_rows, KEYVAL_HEADS, group_width, HEAD_SIZE)

    def span_setup(span_start, key_source, value_source):
        key_tensor_split = lax.slice_in_dim(
            key_source, span_start, span_start + range_rows
        ).reshape(range_rows, KEYVAL_HEADS, HEAD_SIZE)
        value_tensor_split = lax.slice_in_dim(
            value_source, span_start, span_start + range_rows
        ).reshape(range_rows, KEYVAL_HEADS, HEAD_SIZE)
        span_segment = lax.slice_in_dim(key_segment, span_start, span_start + range_rows)
        span_index = lax.slice_in_dim(group_index, span_start, span_start + range_rows)
        allowed = (segment[:, None] == span_segment[None, :]) & (
            span_index[None, :] <= local_index[:, None]
        )
        needed = (span_start <= last_index) & (span_start + range_rows - 1 >= first_start)
        return (key_tensor_split, value_tensor_split, allowed[None, None], needed)

    running_maximum = jnp.full((KEYVAL_HEADS, group_width, token_rows), masked_logits, jnp.float32)
    running_denominator = jnp.zeros((KEYVAL_HEADS, group_width, token_rows), jnp.float32)
    for span_start in span_starts:
        key_tensor_split, value_tensor_split, allowed, needed = span_setup(
            span_start, key_all, value_all
        )

        def extend(carry):
            old_top, old_total = carry
            scores = (
                jnp.einsum(
                    "qgrd,kgd->grqk",
                    query_tensor_split,
                    key_tensor_split,
                    preferred_element_type=jnp.float32,
                )
                * score_scale
            )
            new_top = jnp.maximum(
                old_top, jnp.max(jnp.where(allowed, scores, masked_logits), axis=-1)
            )
            span_sum = jnp.sum(
                jnp.where(allowed, jnp.exp(scores - new_top[..., None]), 0.0), axis=-1
            )
            return (new_top, old_total * jnp.exp(old_top - new_top) + span_sum)

        running_maximum, running_denominator = lax.cond(
            needed, extend, keep_carry, (running_maximum, running_denominator)
        )
    lse = running_maximum + jnp.log(running_denominator)
    running_total = jnp.zeros((token_rows, KEYVAL_HEADS, group_width, HEAD_SIZE), jnp.float32)
    for span_start in span_starts:
        key_tensor_split, value_tensor_split, allowed, needed = span_setup(
            span_start, key_all, value_all
        )

        def weigh_values(carry):
            scores = (
                jnp.einsum(
                    "qgrd,kgd->grqk",
                    query_tensor_split,
                    key_tensor_split,
                    preferred_element_type=jnp.float32,
                )
                * score_scale
            )
            probs_b = jnp.where(allowed, jnp.exp(scores - lse[..., None]), 0.0).astype(jnp.bfloat16)
            return carry + jnp.einsum(
                "grqk,kgd->qgrd", probs_b, value_tensor_split, preferred_element_type=jnp.float32
            )

        running_total = lax.cond(needed, weigh_values, keep_carry, running_total)
    attention_output = running_total.reshape(token_rows, QUERY_HEADS * HEAD_SIZE).astype(
        jnp.bfloat16
    )
    mixed = resid + jnp.dot(attention_output, w_out, preferred_element_type=jnp.float32)
    normed_two, inverse_two = normalize(mixed)
    hidden_two = (normed_two * gain_two.astype(jnp.float32)).astype(jnp.bfloat16)
    gate = jnp.dot(hidden_two, w_gate, preferred_element_type=jnp.float32)
    upward = jnp.dot(hidden_two, w_up, preferred_element_type=jnp.float32)
    sigma = jax.nn.sigmoid(gate)
    activated = (gate * sigma * upward).astype(jnp.bfloat16)
    output = (mixed + jnp.dot(activated, w_down, preferred_element_type=jnp.float32)).astype(
        jnp.bfloat16
    )
    d_act = jnp.dot(cotangent, w_down.T, preferred_element_type=jnp.float32)
    g_down = jnp.dot(activated.T, cotangent, preferred_element_type=jnp.float32)
    d_gate = (d_act * upward * sigma * (1.0 + gate * (1.0 - sigma))).astype(jnp.bfloat16)
    d_up = (d_act * gate * sigma).astype(jnp.bfloat16)
    g_gate = jnp.dot(hidden_two.T, d_gate, preferred_element_type=jnp.float32)
    g_up = jnp.dot(hidden_two.T, d_up, preferred_element_type=jnp.float32)
    d_hidden_two = jnp.dot(d_gate, w_gate.T, preferred_element_type=jnp.float32) + jnp.dot(
        d_up, w_up.T, preferred_element_type=jnp.float32
    )
    g_gain_two = jnp.sum(d_hidden_two * normed_two, axis=0)
    dn_two = d_hidden_two * gain_two.astype(jnp.float32)
    d_mixed = cotangent.astype(jnp.float32) + inverse_two * (
        dn_two - normed_two * jnp.mean(dn_two * normed_two, axis=-1, keepdims=True)
    )
    d_mixed_b = d_mixed.astype(jnp.bfloat16)
    g_out = jnp.dot(attention_output.T, d_mixed_b, preferred_element_type=jnp.float32)
    attention_output_gradient = jnp.dot(
        d_mixed_b, w_out.T, preferred_element_type=jnp.float32
    ).astype(jnp.bfloat16)
    split_gradient = attention_output_gradient.reshape(
        token_rows, KEYVAL_HEADS, group_width, HEAD_SIZE
    )
    attention_output_split = attention_output.reshape(
        token_rows, KEYVAL_HEADS, group_width, HEAD_SIZE
    )
    softmax_correction = jnp.sum(
        split_gradient.astype(jnp.float32) * attention_output_split.astype(jnp.float32), axis=-1
    ).transpose(1, 2, 0)
    key_back, value_back = (key_all, value_all)
    query_gradient_running = jnp.zeros(
        (token_rows, KEYVAL_HEADS, group_width, HEAD_SIZE), jnp.float32
    )
    received = []
    own_block = None
    for shift in reversed(range(narrow_size)):
        span_start = (narrow_rank - shift) * range_rows
        safe_start = jnp.maximum(span_start, 0)
        key_tensor_split = lax.dynamic_slice_in_dim(key_back, safe_start, range_rows).reshape(
            range_rows, KEYVAL_HEADS, HEAD_SIZE
        )
        value_tensor_split = lax.dynamic_slice_in_dim(value_back, safe_start, range_rows).reshape(
            range_rows, KEYVAL_HEADS, HEAD_SIZE
        )
        span_segment = lax.dynamic_slice_in_dim(key_segment, safe_start, range_rows)
        span_index = safe_start + jnp.arange(range_rows, dtype=jnp.int32)
        allowed = (
            (segment[:, None] == span_segment[None, :]) & (span_index[None, :] <= local_index[:, None])
        )[None, None]
        needed = (
            (span_start >= 0)
            & (span_start <= last_index)
            & (span_start + range_rows - 1 >= first_start)
        )

        def back_span(carry):
            scores = (
                jnp.einsum(
                    "qgrd,kgd->grqk",
                    query_tensor_split,
                    key_tensor_split,
                    preferred_element_type=jnp.float32,
                )
                * score_scale
            )
            probs = jnp.where(allowed, jnp.exp(scores - lse[..., None]), 0.0)
            probs_b = probs.astype(jnp.bfloat16)
            value_gradient_range = jnp.einsum(
                "pozf,zpom->fpm", probs_b, split_gradient, preferred_element_type=jnp.float32
            )
            d_probs = jnp.einsum(
                "qgrd,kgd->grqk",
                split_gradient,
                value_tensor_split,
                preferred_element_type=jnp.float32,
            )
            score_gradient = (
                probs * (d_probs - softmax_correction[..., None]) * score_scale
            ).astype(jnp.bfloat16)
            new_acc = carry + jnp.einsum(
                "grqk,kgd->qgrd",
                score_gradient,
                key_tensor_split,
                preferred_element_type=jnp.float32,
            )
            key_gradient_range = jnp.einsum(
                "pozf,zpom->fpm",
                score_gradient,
                query_tensor_split,
                preferred_element_type=jnp.float32,
            )
            return (new_acc, key_gradient_range, value_gradient_range)

        def skip_span(carry):
            blank_range = jnp.zeros((range_rows, KEYVAL_HEADS, HEAD_SIZE), jnp.float32)
            return (carry, blank_range, blank_range)

        query_gradient_running, key_gradient_range, value_gradient_range = lax.cond(
            needed, back_span, skip_span, query_gradient_running
        )
        kv_block = jnp.concatenate(
            [
                key_gradient_range.reshape(range_rows, kv_width),
                value_gradient_range.reshape(range_rows, kv_width),
            ],
            axis=1,
        )
        if shift == 0:
            own_block = kv_block
        else:
            received.append(
                lax.ppermute(
                    kv_block.astype(jnp.bfloat16),
                    "narrow",
                    [(source, source - shift) for source in range(shift, narrow_size)],
                )
            )
    kv_grad = own_block
    for block in received:
        kv_grad = kv_grad + block.astype(jnp.float32)
    key_gradient, value_gradient = kv_grad[:, :kv_width], kv_grad[:, kv_width:]
    d_query = query_gradient_running.reshape(token_rows, QUERY_HEADS * HEAD_SIZE)
    d_query_b = apply_rotary(d_query, token_position, QUERY_HEADS, -1.0).astype(jnp.bfloat16)
    key_gradient_batch = apply_rotary(key_gradient, token_position, KEYVAL_HEADS, -1.0).astype(
        jnp.bfloat16
    )
    value_gradient_batch = value_gradient.astype(jnp.bfloat16)
    g_query = jnp.dot(hidden_one.T, d_query_b, preferred_element_type=jnp.float32)
    g_key_value = jnp.dot(
        hidden_one.T,
        jnp.concatenate([key_gradient_batch, value_gradient_batch], axis=1),
        preferred_element_type=jnp.float32,
    )
    d_hidden_one = (
        jnp.dot(d_query_b, w_query.T, preferred_element_type=jnp.float32)
        + jnp.dot(key_gradient_batch, w_key.T, preferred_element_type=jnp.float32)
        + jnp.dot(value_gradient_batch, w_value.T, preferred_element_type=jnp.float32)
    )
    g_gain_one = jnp.sum(d_hidden_one * normed_one, axis=0)
    dn_one = d_hidden_one * gain_one.astype(jnp.float32)
    d_tokens = (
        d_mixed
        + inverse_one
        * (dn_one - normed_one * jnp.mean(dn_one * normed_one, axis=-1, keepdims=True))
    ).astype(jnp.bfloat16)
    out_and_gains = jnp.concatenate([g_out, g_gain_one[None], g_gain_two[None]], axis=0)
    grad_pieces = lax.psum(
        (g_query, g_key_value, out_and_gains, g_gate, g_up, g_down), ("wide", "narrow")
    )
    out_rows = QUERY_HEADS * HEAD_SIZE
    kv_width_total = KEYVAL_HEADS * HEAD_SIZE
    flat_pieces = [
        (0, 0, None),
        (1, 0, kv_width_total),
        (1, kv_width_total, kv_width_total),
        (2, 0, out_rows),
        (3, 0, None),
        (4, 0, None),
        (5, 0, None),
        (2, out_rows, 2),
    ]

    def shard_of(rank):
        def build(pieces):
            parts = []
            offset = 0
            low, high = rank * shard_len, (rank + 1) * shard_len
            for index, column, width in flat_pieces:
                piece = pieces[index]
                if index == 2:
                    piece = piece[column : column + width]
                elif width is not None:
                    piece = piece[:, column : column + width]
                rows, cols = piece.shape
                size = rows * cols
                start, stop = max(low, offset), min(high, offset + size)
                if start < stop:
                    first_row = (start - offset) // cols
                    last_row = -(-(stop - offset) // cols)
                    block = piece[first_row:last_row].reshape(-1)
                    base = offset + first_row * cols
                    parts.append(block[start - base : stop - base])
                offset = offset + size
            return jnp.concatenate(parts)

        return build

    summed = lax.switch(narrow_rank, [shard_of(rank) for rank in range(narrow_size)], grad_pieces)
    token_total = token_rows * narrow_size * lax.axis_size("wide")
    gradient = summed * (1.0 / math.sqrt(token_total))
    new_first = beta_one * first_moment + (1.0 - beta_one) * gradient
    new_second = beta_two * second_moment + (1.0 - beta_two) * gradient * gradient
    first_hat = new_first / (1.0 - beta_one**STEP)
    second_hat = new_second / (1.0 - beta_two**STEP)
    entry_index = narrow_rank * shard_len + jnp.arange(shard_len, dtype=jnp.int32)
    decay = jnp.where(entry_index < NPARAM - 2 * MODEL_WIDTH, decay_rate, 0.0)
    new_master = master - learn_rate * (
        first_hat / (jnp.sqrt(second_hat) + adam_eps) + decay * master
    )
    return (output, d_tokens, gradient, new_master, new_first, new_second)


def solution(mesh):
    in_specs = (
        P(("wide", "narrow"), None),
        P(("wide", "narrow"), None),
        P("wide", None),
        P("narrow"),
        P("narrow"),
        P("narrow"),
    )
    out_specs = (
        P(("wide", "narrow"), None),
        P(("wide", "narrow"), None),
        P("narrow"),
        P("narrow"),
        P("narrow"),
        P("narrow"),
    )
    return jax.shard_map(body, mesh=mesh, in_specs=in_specs, out_specs=out_specs, check_vma=False)
```

```python
import math

import jax
import jax.numpy as jnp
from jax import lax
from jax.experimental import pallas as pl
from jax.experimental.pallas import tpu as pltpu
from jax.sharding import PartitionSpec as P

MODEL_WIDTH = 512
QUERY_HEADS = 15
KEYVAL_HEADS = 5
HEAD_SIZE = 64
FEEDFWD_UNITS = 1280
STEP = 4
NPARAM = 3277824


eps_norm = 1e-05
rope_base = 100000.0
beta_one = 0.9
beta_two = 0.95
learn_rate = 0.03
decay_rate = 0.1
adam_eps = 1e-08
masked_logits = -1e30


def unpack(flat):
    arrangement_list = [
        (MODEL_WIDTH, QUERY_HEADS * HEAD_SIZE),
        (MODEL_WIDTH, KEYVAL_HEADS * HEAD_SIZE),
        (MODEL_WIDTH, KEYVAL_HEADS * HEAD_SIZE),
        (QUERY_HEADS * HEAD_SIZE, MODEL_WIDTH),
        (MODEL_WIDTH, FEEDFWD_UNITS),
        (MODEL_WIDTH, FEEDFWD_UNITS),
        (FEEDFWD_UNITS, MODEL_WIDTH),
        (MODEL_WIDTH,),
        (MODEL_WIDTH,),
    ]
    pieces = []
    offset = 0
    for layout in arrangement_list:
        length = math.prod(layout)
        pieces.append(flat[offset : offset + length].reshape(layout))
        offset = offset + length
    return pieces


def place_tokens(indices, lengths_row):
    seq_ends = jnp.cumsum(lengths_row)
    seq_starts = seq_ends - lengths_row
    member = (indices[:, None] >= seq_starts[None, :]) & (indices[:, None] < seq_ends[None, :])
    numbers = jnp.arange(lengths_row.shape[0], dtype=jnp.int32)
    segment = jnp.sum(jnp.where(member, numbers[None, :], 0), axis=1)
    token_position = indices - jnp.sum(jnp.where(member, seq_starts[None, :], 0), axis=1)
    return (segment, token_position)


def normalize(values):
    inverse_rms = lax.rsqrt(jnp.mean(values * values, axis=-1, keepdims=True) + eps_norm)
    return (values * inverse_rms, inverse_rms)


def apply_rotary(values, token_position, head_count, turn_sign):
    half_dim = HEAD_SIZE // 2
    inverse = rope_base ** (-2.0 * jnp.arange(half_dim, dtype=jnp.float32) / HEAD_SIZE)
    angles = token_position.astype(jnp.float32)[:, None] * inverse[None, :]
    cosine = jnp.cos(angles)[:, None, :]
    sine = turn_sign * jnp.sin(angles)[:, None, :]
    shaped = values.reshape(values.shape[0], head_count, HEAD_SIZE)
    first_half = shaped[:, :, :half_dim]
    second_half = shaped[:, :, half_dim:]
    turned = jnp.concatenate(
        [first_half * cosine - second_half * sine, second_half * cosine + first_half * sine],
        axis=-1,
    )
    return turned.reshape(values.shape)


def gather_kernel(src_ref, out_ref, send_sems, recv_sems):
    narrow = lax.axis_index("narrow")
    wide = lax.axis_index("wide")
    z_lo = narrow // 2
    core = narrow % 2
    z_hi = (wide // 4) % 2
    flipped = wide + 4 - 8 * z_hi
    split = (src_ref.shape[0] // 32) * 16
    halves = [pl.ds(0, split), pl.ds(split, src_ref.shape[0] - split)]
    sibling = (wide, z_lo * 2 + 1 - core)
    across = [(wide, (1 - z_lo) * 2 + c) for c in (0, 1)]
    around = [(flipped, (1 - z_lo) * 2 + c) for c in (0, 1)]
    barrier = pltpu.get_barrier_semaphore()
    for peer in [sibling] + across + around:
        pl.semaphore_signal(barrier, 1, device_id=peer, device_id_type=pl.DeviceIdType.MESH)
    pl.semaphore_wait(barrier, 5)
    sends = [(sibling, 0), (sibling, 1)] + [(p, 0) for p in across] + [(p, 1) for p in around]
    copies = []
    for number, (peer, part) in enumerate(sends):
        rows = halves[part]
        copy = pltpu.make_async_remote_copy(
            src_ref=src_ref.at[rows],
            dst_ref=out_ref.at[narrow, rows],
            send_sem=send_sems.at[number],
            recv_sem=recv_sems.at[narrow, part],
            device_id=peer,
            device_id_type=pl.DeviceIdType.MESH,
        )
        copy.start()
        copies.append(copy)
    out_ref[narrow] = src_ref[...]
    for copy in copies:
        copy.wait_send()
    for step in range(1, 4):
        owner = lax.rem(narrow + step, 4)
        for part in (0, 1):
            rows = halves[part]
            pltpu.make_async_remote_copy(
                src_ref=src_ref.at[rows],
                dst_ref=out_ref.at[owner, rows],
                send_sem=send_sems.at[0],
                recv_sem=recv_sems.at[owner, part],
                device_id=sibling,
                device_id_type=pl.DeviceIdType.MESH,
            ).wait_recv()


def gather_replica(shard_rows):
    count, width = shard_rows.shape
    return pl.pallas_call(
        gather_kernel,
        out_shape=jax.ShapeDtypeStruct((4, count, width), shard_rows.dtype),
        in_specs=[pl.BlockSpec(memory_space=pltpu.VMEM)],
        out_specs=pl.BlockSpec(memory_space=pltpu.VMEM),
        scratch_shapes=[pltpu.SemaphoreType.DMA((6,)), pltpu.SemaphoreType.DMA((4, 2))],
        compiler_params=pltpu.CompilerParams(collective_id=0, has_side_effects=True),
    )(shard_rows)


def keep_carry(carry):
    return carry


def body(tokens, cotangent, lengths, master, first_moment, second_moment):
    token_rows = tokens.shape[0]
    narrow_size = lax.axis_size("narrow")
    group_rows = token_rows * narrow_size
    narrow_rank = lax.axis_index("narrow")
    group_width = QUERY_HEADS // KEYVAL_HEADS
    score_scale = HEAD_SIZE ** (-0.5)
    shard_len = master.shape[0]
    replica = gather_replica(master.astype(jnp.bfloat16).reshape(shard_len // 128, 128)).reshape(-1)
    w_query, w_key, w_value, w_out, w_gate, w_up, w_down, gain_one, gain_two = unpack(replica)
    lengths_row = lengths[0]
    local_index = narrow_rank * token_rows + jnp.arange(token_rows, dtype=jnp.int32)
    segment, token_position = place_tokens(local_index, lengths_row)
    group_index = jnp.arange(group_rows, dtype=jnp.int32)
    key_segment = place_tokens(group_index, lengths_row)[0]
    first_start = local_index[0] - token_position[0]
    last_index = local_index[token_rows - 1]
    range_rows = token_rows
    span_starts = list(range(0, group_rows, range_rows))
    forward_rows = min(512, group_rows)
    forward_starts = list(range(0, group_rows, forward_rows))
    resid = tokens.astype(jnp.float32)
    normed_one, inverse_one = normalize(resid)
    hidden_one = (normed_one * gain_one.astype(jnp.float32)).astype(jnp.bfloat16)
    query = jnp.dot(hidden_one, w_query, preferred_element_type=jnp.float32)
    key_projection = jnp.dot(hidden_one, w_key, preferred_element_type=jnp.float32)
    value_proj = jnp.dot(hidden_one, w_value, preferred_element_type=jnp.float32)
    query_batch = apply_rotary(query, token_position, QUERY_HEADS, 1.0).astype(jnp.bfloat16)
    key_batch = apply_rotary(key_projection, token_position, KEYVAL_HEADS, 1.0).astype(jnp.bfloat16)
    value_batch = value_proj.astype(jnp.bfloat16)
    kv_width = KEYVAL_HEADS * HEAD_SIZE
    kv_all = lax.all_gather(
        jnp.concatenate([key_batch, value_batch], axis=1), "narrow", axis=0, tiled=True
    )
    key_all, value_all = kv_all[:, :kv_width], kv_all[:, kv_width:]
    query_tensor_split = query_batch.reshape(token_rows, KEYVAL_HEADS, group_width, HEAD_SIZE)

    def span_setup(span_start, key_source, value_source, range_rows=range_rows):
        key_tensor_split = lax.slice_in_dim(
            key_source, span_start, span_start + range_rows
        ).reshape(range_rows, KEYVAL_HEADS, HEAD_SIZE)
        value_tensor_split = lax.slice_in_dim(
            value_source, span_start, span_start + range_rows
        ).reshape(range_rows, KEYVAL_HEADS, HEAD_SIZE)
        span_segment = lax.slice_in_dim(key_segment, span_start, span_start + range_rows)
        span_index = lax.slice_in_dim(group_index, span_start, span_start + range_rows)
        allowed = (segment[:, None] == span_segment[None, :]) & (
            span_index[None, :] <= local_index[:, None]
        )
        needed = (span_start <= last_index) & (span_start + range_rows - 1 >= first_start)
        return (key_tensor_split, value_tensor_split, allowed[None, None], needed)

    running_maximum = jnp.full((KEYVAL_HEADS, group_width, token_rows), masked_logits, jnp.float32)
    running_denominator = jnp.zeros((KEYVAL_HEADS, group_width, token_rows), jnp.float32)
    for span_start in forward_starts:
        key_tensor_split, value_tensor_split, allowed, needed = span_setup(
            span_start, key_all, value_all, forward_rows
        )

        def extend(carry):
            old_top, old_total = carry
            scores = (
                jnp.einsum(
                    "qgrd,kgd->grqk",
                    query_tensor_split,
                    key_tensor_split,
                    preferred_element_type=jnp.float32,
                )
                * score_scale
            )
            new_top = jnp.maximum(
                old_top, jnp.max(jnp.where(allowed, scores, masked_logits), axis=-1)
            )
            span_sum = jnp.sum(
                jnp.where(allowed, jnp.exp(scores - new_top[..., None]), 0.0), axis=-1
            )
            return (new_top, old_total * jnp.exp(old_top - new_top) + span_sum)

        running_maximum, running_denominator = lax.cond(
            needed, extend, keep_carry, (running_maximum, running_denominator)
        )
    lse = running_maximum + jnp.log(running_denominator)
    running_total = jnp.zeros((token_rows, KEYVAL_HEADS, group_width, HEAD_SIZE), jnp.float32)
    for span_start in forward_starts:
        key_tensor_split, value_tensor_split, allowed, needed = span_setup(
            span_start, key_all, value_all, forward_rows
        )

        def weigh_values(carry):
            scores = (
                jnp.einsum(
                    "qgrd,kgd->grqk",
                    query_tensor_split,
                    key_tensor_split,
                    preferred_element_type=jnp.float32,
                )
                * score_scale
            )
            probs_b = jnp.where(allowed, jnp.exp(scores - lse[..., None]), 0.0).astype(jnp.bfloat16)
            return carry + jnp.einsum(
                "grqk,kgd->qgrd", probs_b, value_tensor_split, preferred_element_type=jnp.float32
            )

        running_total = lax.cond(needed, weigh_values, keep_carry, running_total)
    attention_output = running_total.reshape(token_rows, QUERY_HEADS * HEAD_SIZE).astype(
        jnp.bfloat16
    )
    mixed = resid + jnp.dot(attention_output, w_out, preferred_element_type=jnp.float32)
    normed_two, inverse_two = normalize(mixed)
    hidden_two = (normed_two * gain_two.astype(jnp.float32)).astype(jnp.bfloat16)
    gate = jnp.dot(hidden_two, w_gate, preferred_element_type=jnp.float32)
    upward = jnp.dot(hidden_two, w_up, preferred_element_type=jnp.float32)
    sigma = jax.nn.sigmoid(gate)
    activated = (gate * sigma * upward).astype(jnp.bfloat16)
    output = (mixed + jnp.dot(activated, w_down, preferred_element_type=jnp.float32)).astype(
        jnp.bfloat16
    )
    d_act = jnp.dot(cotangent, w_down.T, preferred_element_type=jnp.float32)
    g_down = jnp.dot(activated.T, cotangent, preferred_element_type=jnp.float32)
    d_gate = (d_act * upward * sigma * (1.0 + gate * (1.0 - sigma))).astype(jnp.bfloat16)
    d_up = (d_act * gate * sigma).astype(jnp.bfloat16)
    g_gate = jnp.dot(hidden_two.T, d_gate, preferred_element_type=jnp.float32)
    g_up = jnp.dot(hidden_two.T, d_up, preferred_element_type=jnp.float32)
    d_hidden_two = jnp.dot(d_gate, w_gate.T, preferred_element_type=jnp.float32) + jnp.dot(
        d_up, w_up.T, preferred_element_type=jnp.float32
    )
    g_gain_two = jnp.sum(d_hidden_two * normed_two, axis=0)
    dn_two = d_hidden_two * gain_two.astype(jnp.float32)
    d_mixed = cotangent.astype(jnp.float32) + inverse_two * (
        dn_two - normed_two * jnp.mean(dn_two * normed_two, axis=-1, keepdims=True)
    )
    d_mixed_b = d_mixed.astype(jnp.bfloat16)
    g_out = jnp.dot(attention_output.T, d_mixed_b, preferred_element_type=jnp.float32)
    attention_output_gradient = jnp.dot(
        d_mixed_b, w_out.T, preferred_element_type=jnp.float32
    ).astype(jnp.bfloat16)
    split_gradient = attention_output_gradient.reshape(
        token_rows, KEYVAL_HEADS, group_width, HEAD_SIZE
    )
    attention_output_split = attention_output.reshape(
        token_rows, KEYVAL_HEADS, group_width, HEAD_SIZE
    )
    softmax_correction = jnp.sum(
        split_gradient.astype(jnp.float32) * attention_output_split.astype(jnp.float32), axis=-1
    ).transpose(1, 2, 0)
    key_back, value_back = (key_all, value_all)
    query_gradient_running = jnp.zeros(
        (token_rows, KEYVAL_HEADS, group_width, HEAD_SIZE), jnp.float32
    )
    key_contributions = []
    value_contributions = []
    for span_start in span_starts:
        key_tensor_split, value_tensor_split, allowed, needed = span_setup(
            span_start, key_back, value_back
        )

        def back_span(carry):
            scores = (
                jnp.einsum(
                    "qgrd,kgd->grqk",
                    query_tensor_split,
                    key_tensor_split,
                    preferred_element_type=jnp.float32,
                )
                * score_scale
            )
            probs = jnp.where(allowed, jnp.exp(scores - lse[..., None]), 0.0)
            probs_b = probs.astype(jnp.bfloat16)
            value_gradient_range = jnp.einsum(
                "pozf,zpom->fpm", probs_b, split_gradient, preferred_element_type=jnp.float32
            )
            d_probs = jnp.einsum(
                "qgrd,kgd->grqk",
                split_gradient,
                value_tensor_split,
                preferred_element_type=jnp.float32,
            )
            score_gradient = (
                probs * (d_probs - softmax_correction[..., None]) * score_scale
            ).astype(jnp.bfloat16)
            new_acc = carry + jnp.einsum(
                "grqk,kgd->qgrd",
                score_gradient,
                key_tensor_split,
                preferred_element_type=jnp.float32,
            )
            key_gradient_range = jnp.einsum(
                "pozf,zpom->fpm",
                score_gradient,
                query_tensor_split,
                preferred_element_type=jnp.float32,
            )
            return (new_acc, key_gradient_range, value_gradient_range)

        def skip_span(carry):
            blank_range = jnp.zeros((range_rows, KEYVAL_HEADS, HEAD_SIZE), jnp.float32)
            return (carry, blank_range, blank_range)

        query_gradient_running, key_gradient_range, value_gradient_range = lax.cond(
            needed, back_span, skip_span, query_gradient_running
        )
        key_contributions.append(key_gradient_range.reshape(range_rows, KEYVAL_HEADS * HEAD_SIZE))
        value_contributions.append(
            value_gradient_range.reshape(range_rows, KEYVAL_HEADS * HEAD_SIZE)
        )
    kv_sum_in = jnp.stack(
        [jnp.concatenate(pair, axis=1) for pair in zip(key_contributions, value_contributions)]
    )
    kv_grad = kv_sum_in[narrow_rank]
    for shift in range(1, narrow_size):
        sender_block = kv_sum_in[lax.rem(narrow_rank + narrow_size - shift, narrow_size)]
        kv_grad = kv_grad + lax.ppermute(
            sender_block.astype(jnp.bfloat16),
            "narrow",
            [(source, source - shift) for source in range(shift, narrow_size)],
        ).astype(jnp.float32)
    key_gradient, value_gradient = kv_grad[:, :kv_width], kv_grad[:, kv_width:]
    d_query = query_gradient_running.reshape(token_rows, QUERY_HEADS * HEAD_SIZE)
    d_query_b = apply_rotary(d_query, token_position, QUERY_HEADS, -1.0).astype(jnp.bfloat16)
    key_gradient_batch = apply_rotary(key_gradient, token_position, KEYVAL_HEADS, -1.0).astype(
        jnp.bfloat16
    )
    value_gradient_batch = value_gradient.astype(jnp.bfloat16)
    g_query = jnp.dot(hidden_one.T, d_query_b, preferred_element_type=jnp.float32)
    g_key_value = jnp.dot(
        hidden_one.T,
        jnp.concatenate([key_gradient_batch, value_gradient_batch], axis=1),
        preferred_element_type=jnp.float32,
    )
    d_hidden_one = (
        jnp.dot(d_query_b, w_query.T, preferred_element_type=jnp.float32)
        + jnp.dot(key_gradient_batch, w_key.T, preferred_element_type=jnp.float32)
        + jnp.dot(value_gradient_batch, w_value.T, preferred_element_type=jnp.float32)
    )
    g_gain_one = jnp.sum(d_hidden_one * normed_one, axis=0)
    dn_one = d_hidden_one * gain_one.astype(jnp.float32)
    d_tokens = (
        d_mixed
        + inverse_one
        * (dn_one - normed_one * jnp.mean(dn_one * normed_one, axis=-1, keepdims=True))
    ).astype(jnp.bfloat16)
    out_and_gains = jnp.concatenate([g_out, g_gain_one[None], g_gain_two[None]], axis=0)
    grad_pieces = lax.psum(
        (g_query, g_key_value, out_and_gains, g_gate, g_up, g_down), ("wide", "narrow")
    )
    out_rows = QUERY_HEADS * HEAD_SIZE
    kv_width_total = KEYVAL_HEADS * HEAD_SIZE
    flat_pieces = [
        (0, 0, None),
        (1, 0, kv_width_total),
        (1, kv_width_total, kv_width_total),
        (2, 0, out_rows),
        (3, 0, None),
        (4, 0, None),
        (5, 0, None),
        (2, out_rows, 2),
    ]

    def shard_of(rank):
        def build(pieces):
            parts = []
            offset = 0
            low, high = rank * shard_len, (rank + 1) * shard_len
            for index, column, width in flat_pieces:
                piece = pieces[index]
                if index == 2:
                    piece = piece[column : column + width]
                elif width is not None:
                    piece = piece[:, column : column + width]
                rows, cols = piece.shape
                size = rows * cols
                start, stop = max(low, offset), min(high, offset + size)
                if start < stop:
                    first_row = (start - offset) // cols
                    last_row = -(-(stop - offset) // cols)
                    block = piece[first_row:last_row].reshape(-1)
                    base = offset + first_row * cols
                    parts.append(block[start - base : stop - base])
                offset = offset + size
            return jnp.concatenate(parts)

        return build

    summed = lax.switch(narrow_rank, [shard_of(rank) for rank in range(narrow_size)], grad_pieces)
    token_total = token_rows * narrow_size * lax.axis_size("wide")
    gradient = summed * (1.0 / math.sqrt(token_total))
    new_first = beta_one * first_moment + (1.0 - beta_one) * gradient
    new_second = beta_two * second_moment + (1.0 - beta_two) * gradient * gradient
    first_hat = new_first / (1.0 - beta_one**STEP)
    second_hat = new_second / (1.0 - beta_two**STEP)
    entry_index = narrow_rank * shard_len + jnp.arange(shard_len, dtype=jnp.int32)
    decay = jnp.where(entry_index < NPARAM - 2 * MODEL_WIDTH, decay_rate, 0.0)
    new_master = master - learn_rate * (
        first_hat / (jnp.sqrt(second_hat) + adam_eps) + decay * master
    )
    return (output, d_tokens, gradient, new_master, new_first, new_second)


def solution(mesh):
    in_specs = (
        P(("wide", "narrow"), None),
        P(("wide", "narrow"), None),
        P("wide", None),
        P("narrow"),
        P("narrow"),
        P("narrow"),
    )
    out_specs = (
        P(("wide", "narrow"), None),
        P(("wide", "narrow"), None),
        P("narrow"),
        P("narrow"),
        P("narrow"),
        P("narrow"),
    )
    return jax.shard_map(body, mesh=mesh, in_specs=in_specs, out_specs=out_specs, check_vma=False)
```
